32 devices in a mesh: dp: 8 (over z, x), seq: 4 (over y, core).
Axes of the slice: x: 2, y: 2, z: 4, core: 2. Of those that a mesh axis runs over, the one named last changes fastest.
Arguments:
- hidden: bfloat16 [8, 512, 768], P('dp', 'seq'), may hold values from -6 to 6
- char_ids: int32 [8, 512, 16], P('dp', 'seq'), may hold values from 0 to 127, as said below
- groups: int32 [8], P('dp'), may hold values from 0 to 7
- lengths: int32 [8], P('dp'), may hold values from 128 to 512, as said below
- cotangent: bfloat16 [8, 512, 768], P('dp', 'seq'), may hold values from -6 to 6
- qkv_weight: bfloat16 [768, 2304], P(('dp', 'seq')), may hold values from -0.21875 to 0.21875
- out_weight: bfloat16 [768, 768], P(('dp', 'seq')), may hold values from -0.875 to 0.875
- up_weight: bfloat16 [768, 3072], P(('dp', 'seq')), may hold values from -0.21875 to 0.21875
- down_weight: bfloat16 [3072, 768], P(('dp', 'seq')), may hold values from -0.109375 to 0.109375
- norm_gain: bfloat16 [3, 768], P(None, ('dp', 'seq')), may hold values from 0.5 to 1.5
- norm_bias: bfloat16 [3, 768], P(None, ('dp', 'seq')), may hold values from -1.5 to 1.5
- char_table: bfloat16 [1024, 256], P(('dp', 'seq')), may hold values from -6 to 6
- gru_input: bfloat16 [512, 1152], P(('dp', 'seq')), may hold values from -0.375 to 0.375
- gru_recur: bfloat16 [768, 1152], P(('dp', 'seq')), may hold values from -0.3125 to 0.3125
- merge_weight: bfloat16 [1536, 768], P(('dp', 'seq')), may hold values from -0.21875 to 0.21875
- conv_weight: bfloat16 [4608, 768], P(('dp', 'seq')), may hold values from -0.09375 to 0.09375
Outputs:
- result: bfloat16 [8, 512, 768], P('dp', 'seq')
- hidden_grad: bfloat16 [8, 512, 768], P('dp', 'seq')
- qkv_grad: float32 [768, 2304], P(('dp', 'seq'))
- out_grad: float32 [768, 768], P(('dp', 'seq'))
- up_grad: float32 [768, 3072], P(('dp', 'seq'))
- down_grad: float32 [3072, 768], P(('dp', 'seq'))
- gain_grad: float32 [3, 768], P(None, ('dp', 'seq'))
- bias_grad: float32 [3, 768], P(None, ('dp', 'seq'))
- table_grad: float32 [1024, 256], P(('dp', 'seq'))
- gru_input_grad: float32 [512, 1152], P(('dp', 'seq'))
- gru_recur_grad: float32 [768, 1152], P(('dp', 'seq'))
- merge_grad: float32 [1536, 768], P(('dp', 'seq'))
- conv_grad: float32 [4608, 768], P(('dp', 'seq'))
The draws below stay inside these ranges and needn't reach their ends.
Inputs may be any that keep to these rules, and one draw needn't show every extreme that they name: `char_ids`: in each token the nonzero ids come first and the rest of its 16 slots are 0; the first slot is never 0. `lengths`: positions at or past a sequence's length are padding that attention does not read as keys.
All inputs are finite; a program needn't handle non-finite values.
Results may differ from the reference program's by a relative error of at most 0.017.
Values may be sent and summed in bfloat16 or wider, within the bound.
A program may use at most 256 MiB of HBM per device.

```python
import math
import jax
import jax.numpy as jnp
from jax import lax

D = 768
HD = 64
FF = 3072
H = 384
CE = 256
SUBV = 128
NGROUP = 8
NCH = 16
LEN = 512
SEQS = 8


def draw_char_ids(key, part):
    key_count = jax.random.fold_in(key, 11)
    key_ids = jax.random.fold_in(key, 12)
    counts = jax.random.randint(key_count, (SEQS, LEN, 1), 1, NCH + 1)
    ids = jax.random.randint(key_ids, (SEQS, LEN, NCH), 1, SUBV)
    slots = jnp.arange(NCH)[None, None, :]
    return jnp.where(slots < counts, ids, 0).astype(jnp.int32)


def draw_lengths(key, part):
    drawn = jax.random.randint(jax.random.fold_in(key, 21), (SEQS,), LEN // 4, LEN + 1)
    return jnp.where(jnp.arange(SEQS) == 0, LEN, drawn).astype(jnp.int32)


def set_ends(values, stream_key, low, top_value):
    longest = values.shape.index(max(values.shape))
    spots = []
    for shift in (0, 1):
        where = [jax.random.randint(jax.random.fold_in(stream_key, axis), (), 0, length) for axis, length in enumerate(values.shape)]
        where[longest] = (where[longest] + shift) % values.shape[longest]
        spots.append(tuple(where))
    return values.at[spots[0]].set(low).at[spots[1]].set(top_value)


def shard_levels(own_key, extent, shards, smallest, high):
    def one(dim, blocks):
        steps = jax.random.uniform(jax.random.fold_in(jax.random.fold_in(own_key, 6), dim), (blocks,), jnp.float32, smallest / len(shards), high / len(shards))
        return jnp.repeat(jnp.exp(steps), extent[dim] // blocks).reshape((-1,) + (1,) * (len(extent) - dim - 1))

    gain = one(*shards[0])
    for cut in shards[1:]:
        gain = gain * one(*cut)
    return gain


def gaussian(stream_key, extent, scale, bound, pieces=(), kind=jnp.bfloat16):
    gain = shard_levels(stream_key, extent, pieces, -0.22, 0.18) if pieces else 1.0
    values = jax.random.normal(stream_key, extent, jnp.float32) * scale * gain
    return jnp.minimum(jnp.maximum(values, -bound), bound).astype(kind)


def setup_inputs(seed: int = 0) -> dict:
    keys = jax.random.split(jax.random.key(seed), 17)
    return {
        "hidden": gaussian(keys[0], (SEQS, LEN, D), 1.0, 6.0, ((0, 8), (1, 4))),
        "char_ids": draw_char_ids(jax.random.fold_in(keys[16], 71), 0),
        "groups": set_ends(jax.random.randint(keys[2], (SEQS,), 0, NGROUP), jax.random.fold_in(keys[2], 1), 0, NGROUP - 1).astype(jnp.int32),
        "lengths": draw_lengths(jax.random.fold_in(keys[16], 71), 0),
        "cotangent": gaussian(keys[4], (SEQS, LEN, D), 1.0, 6.0, ((0, 8), (1, 4))),
        "qkv_weight": gaussian(keys[5], (D, 3 * D), D ** -0.5, 0.21875, ((0, 32),)),
        "out_weight": gaussian(keys[6], (D, D), (D // 16) ** -0.5, 0.875, ((0, 32),)),
        "up_weight": gaussian(keys[7], (D, FF), D ** -0.5, 0.21875, ((0, 32),)),
        "down_weight": gaussian(keys[8], (FF, D), FF ** -0.5, 0.109375, ((0, 32),)),
        "norm_gain": jnp.clip(1.0 + 0.1 * jax.random.normal(keys[9], (3, D), jnp.float32), 0.5, 1.5).astype(jnp.bfloat16),
        "norm_bias": gaussian(keys[10], (3, D), 0.3, 1.5, ((1, 32),)),
        "char_table": gaussian(keys[11], (NGROUP * SUBV, CE), 1.0, 6.0, ((0, 32),)),
        "gru_input": gaussian(keys[12], (2 * CE, 3 * H), CE ** -0.5, 0.375, ((0, 32),)),
        "gru_recur": gaussian(keys[13], (2 * H, 3 * H), H ** -0.5, 0.3125, ((0, 32),)),
        "merge_weight": gaussian(keys[14], (2 * D, D), D ** -0.5, 0.21875, ((0, 32),)),
        "conv_weight": gaussian(keys[15], (6 * D, D), (6 * D) ** -0.5, 0.09375, ((0, 32),)),
    }


@jax.custom_vjp
def low(v):
    return lax.optimization_barrier(v.astype(jnp.bfloat16)).astype(jnp.float32)

@jax.custom_vjp
def low_back(v):
    return v

def low_keep(v):
    return (low(v), None)

def low_pass(kept, grad):
    return (grad,)

def back_keep(v):
    return (v, None)

def back_low(kept, grad):
    return (low(grad),)
low.defvjp(low_keep, low_pass)
low_back.defvjp(back_keep, back_low)
eps = 1e-05
HIGHEST = lax.Precision.HIGHEST

def matmul_high(left, right):
    return jnp.matmul(left, right, precision=HIGHEST)

def norm_rows(residual, row_gain, row_bias):
    centered = residual - lax.optimization_barrier(jnp.mean(residual, axis=-1, keepdims=True))
    spread = lax.optimization_barrier(jnp.mean(centered * centered, axis=-1, keepdims=True))
    return centered * lax.rsqrt(spread + eps) * row_gain + row_bias

def cell(gate_input, gate_recur, carry_state, is_live):
    units = carry_state.shape[-1]
    reset = jax.nn.sigmoid(gate_input[..., :units] + gate_recur[..., :units])
    update = jax.nn.sigmoid(gate_input[..., units:2 * units] + gate_recur[..., units:2 * units])
    candidate = jnp.tanh(gate_input[..., 2 * units:] + reset * gate_recur[..., 2 * units:])
    fresh = (1.0 - update) * candidate + update * carry_state
    return jnp.where(is_live, fresh, carry_state)

def forward(params, hidden, char_ids, groups, lengths):
    qkv_w, out_w, up_w, down_w, gains, biases, table, gru_in, gru_rec, merge_w, conv_w = params
    seq_count, seq_len, features = hidden.shape
    head_count = features // HD
    score_scale = 1.0 / math.sqrt(HD)
    qkv = low(low_back(matmul_high(hidden, qkv_w)))
    queries = qkv[..., :features].reshape(seq_count, seq_len, head_count, HD)
    all_keys = qkv[..., features:2 * features].reshape(seq_count, seq_len, head_count, HD)
    values = qkv[..., 2 * features:].reshape(seq_count, seq_len, head_count, HD)
    scores = jnp.einsum('bqhd,bkhd->bhqk', queries, all_keys, precision=HIGHEST) * score_scale
    key_valid = jnp.arange(seq_len)[None, None, None, :] < lengths[:, None, None, None]
    scores = low_back(jnp.where(key_valid, scores, -1000000000.0))
    attn_probs = low(jax.nn.softmax(scores, axis=-1))
    attended = jnp.einsum('bhqk,bkhd->bqhd', attn_probs, values, precision=HIGHEST)
    attended = low(low_back(attended)).reshape(seq_count, seq_len, features)
    attn_out = low_back(matmul_high(attended, out_w))
    norm_one = low(norm_rows(hidden + attn_out, gains[0], biases[0]))
    up_proj = low_back(matmul_high(norm_one, up_w))
    active = low(jax.nn.gelu(up_proj, approximate=False))
    ffn_out = low_back(matmul_high(active, down_w))
    norm_two = low(norm_rows(norm_one + ffn_out, gains[1], biases[1]))
    tokens = seq_count * seq_len
    char_rows = groups[:, None, None] * SUBV + char_ids
    char_emb = low_back(table[char_rows]).reshape(tokens, NCH, table.shape[1])
    char_live = (char_ids > 0).reshape(tokens, NCH)
    steps_in = jnp.stack([char_emb, char_emb[:, ::-1]], 0)
    steps_live = jnp.moveaxis(jnp.stack([char_live, char_live[:, ::-1]], 0), 2, 0)
    inward = gru_in.reshape(2, -1, gru_in.shape[1])
    recurrent = gru_rec.reshape(2, -1, gru_rec.shape[1])
    gates_in = low_back(jnp.einsum('dtcz,dzg->cdtg', steps_in, inward, precision=HIGHEST))
    hidden_units = recurrent.shape[1]

    def gru_step(carry_state, step_input):
        gate_input, is_live = step_input
        gate_recur = low_back(jnp.einsum('dth,dhg->dtg', low(carry_state), recurrent, precision=HIGHEST))
        return (cell(gate_input, gate_recur, carry_state, is_live[..., None]), None)
    start_state = jnp.zeros((2, tokens, hidden_units), jnp.float32)
    last_state, _ = lax.scan(jax.checkpoint(gru_step), start_state, (gates_in, steps_live))
    char_vec = low(jnp.concatenate([last_state[0], last_state[1]], -1)).reshape(seq_count, seq_len, features)
    merge_mats = merge_w.reshape(2, features, features)
    merged_rows = jnp.concatenate([matmul_high(norm_two, merge_mats[0]), matmul_high(char_vec, merge_mats[1])], -1)
    merged_rows = low(low_back(merged_rows))
    padded = jnp.pad(merged_rows, ((0, 0), (1, 1), (0, 0)))
    kernel = conv_w.reshape(3, 2 * features, features)
    conv_out = matmul_high(padded[:, :seq_len], kernel[0]) + matmul_high(padded[:, 1:seq_len + 1], kernel[1])
    conv_out = conv_out + matmul_high(padded[:, 2:], kernel[2])
    conv_out = low_back(conv_out)
    return norm_rows(norm_two + conv_out, gains[2], biases[2])

def reference(hidden, char_ids, groups, lengths, cotangent, qkv_weight, out_weight, up_weight, down_weight, norm_gain, norm_bias, char_table, gru_input, gru_recur, merge_weight, conv_weight):
    params = tuple((item.astype(jnp.float32) for item in (qkv_weight, out_weight, up_weight, down_weight, norm_gain, norm_bias, char_table, gru_input, gru_recur, merge_weight, conv_weight)))
    per_group = math.gcd(SEQS, max(1, 4096 // LEN))
    group_count = SEQS // per_group

    def split_groups(array):
        return array.reshape((group_count, per_group) + array.shape[1:])

    def one_group(totals, group_input):
        hidden_part, char_part, group_part, length_part, seed_part = group_input

        def local_forward(weights, stream):
            return forward(weights, stream, char_part, group_part, length_part)
        output, pullback = jax.vjp(local_forward, params, hidden_part.astype(jnp.float32))
        weight_grads, stream_grad = pullback(seed_part.astype(jnp.float32))
        totals = jax.tree.map(lambda total, extra: total + extra, totals, weight_grads)
        return (totals, (output.astype(jnp.bfloat16), stream_grad.astype(jnp.bfloat16)))
    zero_grads = jax.tree.map(jnp.zeros_like, params)
    inputs = (split_groups(hidden), split_groups(char_ids), split_groups(groups), split_groups(lengths), split_groups(cotangent))
    totals, (outputs, stream_grads) = lax.scan(one_group, zero_grads, inputs)
    result = outputs.reshape(SEQS, LEN, -1)
    hidden_grad = stream_grads.reshape(SEQS, LEN, -1)
    return (result, hidden_grad, totals[0], totals[1], totals[2], totals[3], totals[4], totals[5], totals[6], totals[7], totals[8], totals[9], totals[10])
```

```python
import functools
import math

import jax
import jax.numpy as jnp
from jax import lax
from jax.experimental import pallas as pl
from jax.experimental.pallas import tpu as pltpu
from jax.sharding import PartitionSpec as P

MESH = pl.DeviceIdType.MESH

HD = 64
SUBV = 128

eps = 1e-05

class Place:
    def __init__(self, dp_size):
        dp, seq = lax.axis_index("dp"), lax.axis_index("seq")
        self.lines = dp_size // 2
        self.a, self.b = dp // 2, lax.rem(dp, 2)
        self.y, self.c = seq // 2, lax.rem(seq, 2)
        flip_b = (self.a * 2 + 1 - self.b, seq)
        flip_y = (dp, (1 - self.y) * 2 + self.c)
        pick = lambda u, v: tuple(i + self.c * (j - i) for i, j in zip(u, v))
        self.first, self.second = pick(flip_b, flip_y), pick(flip_y, flip_b)
        self.sibling = (dp, self.y * 2 + 1 - self.c)
        self.up, self.down = (dp + 2, seq), (dp - 2, seq)
        self.f = self.b + self.c * (self.y - self.b)
        self.s = self.y + self.c * (self.b - self.y)
        self.has_up, self.has_down = self.a < self.lines - 1, self.a > 0

    def unit(self, a, f, s, c=None):
        c = self.c if c is None else c
        return a * 8 + f * (4 - 2 * c) + s * (2 + 2 * c) + c

    def barrier(self):
        sem = pltpu.get_barrier_semaphore()
        for who in (self.first, self.second, self.sibling):
            pl.semaphore_signal(sem, inc=1, device_id=who, device_id_type=MESH)

        @pl.when(self.has_up)
        def _():
            pl.semaphore_signal(sem, inc=1, device_id=self.up, device_id_type=MESH)

        @pl.when(self.has_down)
        def _():
            pl.semaphore_signal(sem, inc=1, device_id=self.down, device_id_type=MESH)

        pl.semaphore_wait(sem, 3 + self.has_up.astype(jnp.int32) + self.has_down.astype(jnp.int32))


def push(src, dst, send, recv, who):
    return pltpu.make_async_remote_copy(
        src_ref=src, dst_ref=dst, send_sem=send, recv_sem=recv, device_id=who, device_id_type=MESH
    )


class Gather:
    def __init__(self, at, shard, full, sems):
        self.at, self.shard, self.full = at, shard, full
        self.up_s, self.down_s, self.sum_s, self.line_r, self.second_r, self.one = sems

    def to_lines(self, src, slot, index, up, down):
        at = self.at
        if up is not False:
            @pl.when(at.has_up if up is True else jnp.logical_and(up, at.has_up))
            def _():
                push(src, self.full.at[index], self.up_s.at[slot], self.line_r.at[slot], at.up).start()
        if down is not False:
            @pl.when(at.has_down if down is True else jnp.logical_and(down, at.has_down))
            def _():
                push(src, self.full.at[index], self.down_s.at[slot], self.line_r.at[slot], at.down).start()

    def across(self, src, slot, index):
        push(src, self.full.at[index], self.sum_s.at[0], self.second_r.at[slot], self.at.second).start()
        self.aside(src, index)

    def aside(self, src, index):
        push(src, self.full.at[index], self.sum_s.at[1], self.one.at[1], self.at.sibling).start()

    def begin(self):
        at = self.at
        me = at.unit(at.a, at.f, at.s)
        pltpu.make_async_copy(self.shard, self.full.at[me], self.one.at[3]).start()
        push(self.shard, self.full.at[me], self.one.at[2], self.one.at[0], at.first).start()
        slot = at.a * 2 + at.f
        self.to_lines(self.shard, slot, me, True, True)
        self.across(self.shard, slot, me)

    def after_first(self):
        at = self.at
        index = at.unit(at.a, 1 - at.f, at.s)
        ref = self.full.at[index]
        push(ref, ref, self.one.at[2], self.one.at[0], at.first).wait_recv()
        slot = at.a * 2 + 1 - at.f
        self.to_lines(ref, slot, index, True, True)
        self.across(ref, slot, index)

    def after_line(self, k, g):
        at = self.at
        for sign in (-1, 1):
            a = at.a + sign * k
            f = at.f if g == 0 else 1 - at.f

            @pl.when(a >= 0 if sign < 0 else a < at.lines)
            def _():
                index, slot = at.unit(a, f, at.s), a * 2 + f
                ref = self.full.at[index]
                push(ref, ref, self.up_s.at[slot], self.line_r.at[slot], at.up).wait_recv()
                self.to_lines(ref, slot, index, sign < 0, sign > 0)
                self.across(ref, slot, index)

    def after_second(self, k, g):
        at = self.at
        for sign in (-1, 1) if k else (1,):
            a = at.a + sign * k
            f = at.f if g == 0 else 1 - at.f

            @pl.when(a >= 0 if sign < 0 else a < at.lines)
            def _():
                index, slot = at.unit(a, f, 1 - at.s), a * 2 + f
                ref = self.full.at[index]
                push(ref, ref, self.sum_s.at[0], self.second_r.at[slot], at.second).wait_recv()
                self.aside(ref, index)

    def finish(self):
        at, n = self.at, self.at.lines
        me = at.unit(at.a, at.f, at.s)
        half = self.full.at[pl.ds(0, 4 * n)]
        push(half, half, self.sum_s.at[1], self.one.at[1], at.sibling).wait_recv()
        pltpu.make_async_copy(self.shard, self.full.at[me], self.one.at[3]).wait()
        push(self.shard, self.full.at[me], self.one.at[2], self.one.at[0], at.first).wait_send()
        push(half, half, self.sum_s.at[1], self.one.at[1], at.sibling).wait_send()
        part = self.full.at[pl.ds(0, 2 * n)]
        push(part, part, self.sum_s.at[0], self.one.at[0], at.second).wait_send()
        for a in range(n):
            for f in range(2):
                slot = a * 2 + f
                ref = self.full.at[0]

                @pl.when(jnp.logical_and(at.has_up, a <= at.a))
                def _():
                    push(ref, ref, self.up_s.at[slot], self.line_r.at[slot], at.up).wait_send()

                @pl.when(jnp.logical_and(at.has_down, a >= at.a))
                def _():
                    push(ref, ref, self.down_s.at[slot], self.line_r.at[slot], at.down).wait_send()


def gather_sems(n):
    dma = pltpu.SemaphoreType.DMA
    return [dma((2 * n,)), dma((2 * n,)), dma((2,)), dma((2 * n,)), dma((2 * n,)), dma((4,))]


def gather_kernel(dp_size, count, *refs):
    shards, fulls, sems = refs[:count], refs[count : 2 * count], refs[2 * count :]
    at = Place(dp_size)
    at.barrier()
    jobs = [Gather(at, shards[i], fulls[i], sems[6 * i : 6 * i + 6]) for i in range(count)]
    for job in jobs:
        job.begin()
    for job in jobs:
        job.after_first()
    for k in range(1, at.lines):
        for g in range(2):
            for job in jobs:
                job.after_line(k, g)
            for job in jobs:
                job.after_second(k - 1, g)
    for g in range(2):
        for job in jobs:
            job.after_second(at.lines - 1, g)
    for job in jobs:
        job.finish()


def gather_all(dp_size, devices, shards, cid=1):
    count = len(shards)
    return pl.pallas_call(
        functools.partial(gather_kernel, dp_size, count),
        out_shape=[jax.ShapeDtypeStruct((devices,) + x.shape, x.dtype) for x in shards],
        in_specs=[pl.BlockSpec(memory_space=pl.ANY)] * count,
        out_specs=[pl.BlockSpec(memory_space=pl.ANY)] * count,
        scratch_shapes=gather_sems(dp_size // 2) * count,
        compiler_params=pltpu.CompilerParams(collective_id=cid, has_side_effects=True),
    )(*shards)


def wide(x):
    return x.astype(jnp.float32)


def add_into(dst, src):
    dst[...] = (wide(dst[...]) + wide(src[...])).astype(dst.dtype)


class Scatter:
    def __init__(self, at, part, out, bufs, sems):
        self.at, self.part, self.out = at, part, out
        self.own, self.sib, self.sec, self.line, self.fst = bufs
        self.one, self.line_s, self.line_r = sems

    def begin(self):
        at = self.at

        def body(j, carry):
            a, f, s = j // 4, lax.rem(j // 2, 2), lax.rem(j, 2)
            push(self.part.at[at.unit(a, f, s, 1 - at.c)], self.sib.at[j], self.one.at[0], self.one.at[1], at.sibling).start()
            return carry

        lax.fori_loop(0, 4 * at.lines, body, 0)

        def load(j, carry):
            a, f, s = j // 4, lax.rem(j // 2, 2), lax.rem(j, 2)
            pltpu.make_async_copy(self.part.at[at.unit(a, f, s)], self.own.at[j], self.one.at[2]).start()
            return carry

        lax.fori_loop(0, 4 * at.lines, load, 0)

    def after_sibling(self):
        at = self.at
        n = 2 * at.lines
        pltpu.make_async_copy(self.part.at[pl.ds(0, 2 * n)], self.own, self.one.at[2]).wait()
        push(self.sib, self.sib, self.one.at[0], self.one.at[1], at.sibling).wait_recv()

        def far(q, carry):
            j = q * 2 + 1 - at.s
            add_into(self.own.at[j], self.sib.at[j])
            return carry

        def send(q, carry):
            push(self.own.at[q * 2 + 1 - at.s], self.sec.at[q], self.one.at[3], self.one.at[4], at.second).start()
            return carry

        def near(q, carry):
            j = q * 2 + at.s
            add_into(self.own.at[j], self.sib.at[j])
            return carry

        lax.fori_loop(0, n, far, 0)
        lax.fori_loop(0, n, send, 0)
        lax.fori_loop(0, n, near, 0)

    def after_second(self):
        at = self.at
        push(self.sec, self.sec, self.one.at[3], self.one.at[4], at.second).wait_recv()

        def body(q, carry):
            add_into(self.own.at[q * 2 + at.s], self.sec.at[q])
            return carry

        lax.fori_loop(0, 2 * at.lines, body, 0)

    def hop(self, low, high, inward, dst, extra):
        at = self.at
        has, who = (at.has_up, at.down) if dst < 0 else (at.has_down, at.up)

        def take(q, carry):
            push(self.line.at[q], self.line.at[q], self.line_s.at[q], self.line_r.at[q], who).wait_recv()
            add_into(self.own.at[q * 2 + at.s], self.line.at[q])
            return carry

        @pl.when(has)
        def _():
            lax.fori_loop(low, high, take, 0)

        def send(q, carry):
            slot = q if dst < 0 else jnp.where(q // 2 == at.a + 1, 2 * at.lines + lax.rem(q, 2), q)
            push(self.own.at[q * 2 + at.s], self.line.at[slot], self.line_s.at[q], self.line_r.at[slot], who).start()
            return carry

        lax.fori_loop(low, high, send, 0)

    def along(self, h):
        at = self.at
        n = at.lines
        hops = n - 1 if n <= 4 else 1

        @pl.when(jnp.logical_and(at.has_down, at.lines - 1 - at.a == h) if hops > 1 else at.has_down)
        def _():
            self.hop(0, 2 * at.a, at.up, -1, None)

        @pl.when(jnp.logical_and(at.has_up, at.a == h) if hops > 1 else at.has_up)
        def _():
            self.hop(2 * at.a + 2, 2 * n, at.down, 1, None)

    def ends(self, f, into):
        at = self.at
        for has, slot in ((at.has_up, 2 * at.a + f), (at.has_down, 2 * at.lines + f)):
            @pl.when(has)
            def _():
                ref = self.line.at[slot]
                push(ref, ref, self.line_s.at[0], self.line_r.at[slot], at.first).wait_recv()
                into[...] = (wide(into[...]) + wide(ref[...])).astype(into.dtype)

    def last_send(self):
        at = self.at
        mine = self.own.at[(2 * at.a + 1 - at.f) * 2 + at.s]
        self.ends(1 - at.f, mine)
        push(mine, self.fst, self.one.at[5], self.one.at[6], at.first).start()
        self.out[...] = wide(self.own[(2 * at.a + at.f) * 2 + at.s])
        self.ends(at.f, self.out)

    def finish(self):
        at = self.at
        push(self.fst, self.fst, self.one.at[5], self.one.at[6], at.first).wait_recv()
        self.out[...] = self.out[...] + wide(self.fst[...])

    def drain(self):
        at = self.at
        n = at.lines
        push(self.sib, self.sib, self.one.at[0], self.one.at[1], at.sibling).wait_send()
        push(self.sec, self.sec, self.one.at[3], self.one.at[4], at.second).wait_send()
        push(self.fst, self.fst, self.one.at[5], self.one.at[6], at.first).wait_send()

        def body(q, carry):
            @pl.when(q // 2 != at.a)
            def _():
                push(self.own.at[q], self.own.at[q], self.line_s.at[q], self.line_r.at[q], at.first).wait_send()
            return carry

        lax.fori_loop(0, 2 * n, body, 0)


def scatter_buffers(n, shape, dtype):
    v = lambda k: pltpu.VMEM((k,) + shape, dtype)
    return [v(4 * n), v(4 * n), v(2 * n), v(2 * n + 2), pltpu.VMEM(shape, dtype)]


def scatter_sems(n):
    dma = pltpu.SemaphoreType.DMA
    return [dma((7,)), dma((2 * n,)), dma((2 * n + 2,))]


def scatter_stages(lines):
    hops = lines - 1 if lines <= 4 else 1
    stages = [Scatter.after_sibling, Scatter.after_second]
    for h in range(hops):
        stages.append(functools.partial(Scatter.along, h=h))
    return stages + [Scatter.last_send, Scatter.finish]


def scatter_kernel(dp_size, count, *refs):
    parts, outs, rest = refs[:count], refs[count : 2 * count], refs[2 * count :]
    at = Place(dp_size)
    at.barrier()
    jobs = [Scatter(at, parts[i], outs[i], rest[8 * i : 8 * i + 5], rest[8 * i + 5 : 8 * i + 8]) for i in range(count)]
    for job in jobs:
        job.begin()
    stages = scatter_stages(at.lines)
    for t in range(count + len(stages) - 1):
        for k, stage in enumerate(stages):
            if 0 <= t - k < count:
                stage(jobs[t - k])
    for job in jobs:
        job.drain()


def scatter_all(dp_size, parts, cid=2):
    count = len(parts)
    n = dp_size // 2
    scratch = []
    for x in parts:
        scratch += scatter_buffers(n, x.shape[1:], x.dtype) + scatter_sems(n)
    return pl.pallas_call(
        functools.partial(scatter_kernel, dp_size, count),
        out_shape=[jax.ShapeDtypeStruct(x.shape[1:], jnp.float32) for x in parts],
        in_specs=[pl.BlockSpec(memory_space=pl.ANY)] * count,
        out_specs=[pl.BlockSpec(memory_space=pltpu.VMEM)] * count,
        scratch_shapes=scratch,
        compiler_params=pltpu.CompilerParams(collective_id=cid, has_side_effects=True, vmem_limit_bytes=64000000),
    )(*parts)


def with_halo(x, sides, width):
    for axis, dim in sides:
        devices, length = (lax.axis_size(axis), x.shape[dim])
        up = [(i, (i + 1) % devices) for i in range(devices - 1)]
        down = [(j, i) for i, j in up]
        last = lax.slice_in_dim(x, length - width, length, axis=dim)
        first = lax.slice_in_dim(x, 0, width, axis=dim)
        before = lax.ppermute(last, axis, up)
        after = lax.ppermute(first, axis, down)
        x = jnp.concatenate([before, x, after], axis=dim)
    return x


def norm_rows(residual, row_gain, row_bias):
    centered = residual - jnp.mean(residual, axis=-1, keepdims=True)
    spread = jnp.mean(centered * centered, axis=-1, keepdims=True)
    return centered * lax.rsqrt(spread + eps) * row_gain + row_bias


def cell(gate_input, gate_recur, carry_state, is_live):
    units = carry_state.shape[-1]
    reset = jax.nn.sigmoid(gate_input[..., :units] + gate_recur[..., :units])
    update = jax.nn.sigmoid(gate_input[..., units : 2 * units] + gate_recur[..., units : 2 * units])
    candidate = jnp.tanh(gate_input[..., 2 * units :] + reset * gate_recur[..., 2 * units :])
    fresh = (1.0 - update) * candidate + update * carry_state
    return jnp.where(is_live, fresh, carry_state)


def gelu_exact(pre_act):
    return jax.nn.gelu(pre_act, approximate=False)


def plain_dot(left, right):
    return jnp.dot(left, right, preferred_element_type=jnp.float32)


def grad_dot(left, right):
    return lax.dot_general(
        left, right, (((0,), (0,)), ((), ())), preferred_element_type=jnp.float32
    )


def back_dot(left, right):
    return lax.dot_general(
        left, right, (((1,), (1,)), ((), ())), preferred_element_type=jnp.float32
    )


def pack_norms(gain, bias, devices=1):
    both = jnp.stack([gain, bias], 0)
    both = both.reshape(2, 3, devices, -1).transpose(2, 0, 1, 3).reshape(devices, -1)
    both = jnp.pad(both, ((0, 0), (0, 1024 - both.shape[1]))).reshape(devices, 8, 128)
    return both[0] if devices == 1 else both


def unpack_norms(tiles, shape):
    devices = tiles.shape[0]
    flat = tiles.reshape(devices, -1)[:, : 2 * shape[0] * shape[1]].reshape(devices, 2, *shape)
    both = flat.transpose(1, 2, 0, 3).reshape(2, shape[0], -1)
    return both[0], both[1]


def local(
    hidden,
    char_ids,
    groups,
    lengths,
    cotangent,
    qkv_weight,
    out_weight,
    up_weight,
    down_weight,
    norm_gain,
    norm_bias,
    char_table,
    gru_input,
    gru_recur,
    merge_weight,
    conv_weight,
):
    dp_size, devices = lax.axis_size("dp"), lax.axis_size("dp") * lax.axis_size("seq")
    norms = pack_norms(norm_gain, norm_bias)
    order = (char_table, gru_input, gru_recur, norms, qkv_weight, out_weight, up_weight, down_weight, merge_weight, conv_weight)
    gathered = gather_all(dp_size, devices, order)
    full_norms = gathered[3]
    (full_table, full_input, full_recur, _, full_qkv, full_out, full_up, full_down, full_merge, full_conv) = [
        x.reshape(-1, x.shape[2]) for x in gathered
    ]
    full_gain, full_bias = unpack_norms(full_norms, norm_gain.shape)
    seq_count, local_len, features = hidden.shape
    nchar = char_ids.shape[2]
    tokens = seq_count * local_len
    head_count = features // HD
    key_span = local_len * lax.axis_size("seq")
    score_scale = 1.0 / math.sqrt(HD)
    gains = full_gain.astype(jnp.float32)
    biases = full_bias.astype(jnp.float32)
    flat_in = hidden.reshape(tokens, features)
    qkv = plain_dot(flat_in, full_qkv).astype(jnp.bfloat16)
    queries = qkv[:, :features].reshape(seq_count, local_len, head_count, HD)
    own_keys = qkv[:, features : 2 * features].reshape(seq_count, local_len, features)
    own_values = qkv[:, 2 * features :].reshape(seq_count, local_len, features)
    all_keys, all_values = (
        lax.all_gather(own_keys, "seq", axis=1, tiled=True),
        lax.all_gather(own_values, "seq", axis=1, tiled=True),
    )
    all_keys = all_keys.reshape(seq_count, key_span, head_count, HD)
    all_values = all_values.reshape(seq_count, key_span, head_count, HD)
    key_valid = jnp.arange(key_span)[None, None, None, :] < lengths[:, None, None, None]

    def score_block():
        raw_scores = (
            jnp.einsum("sqhd,skhd->shqk", queries, all_keys, preferred_element_type=jnp.float32)
            * score_scale
        )
        return jnp.where(key_valid, raw_scores, -1000000000.0)

    scores = score_block()
    log_total = jax.nn.logsumexp(scores, axis=-1, keepdims=True)
    attn_probs = jnp.exp(scores - log_total).astype(jnp.bfloat16)
    attended = jnp.einsum(
        "shqk,skhd->sqhd", attn_probs, all_values, preferred_element_type=jnp.float32
    )
    attended = attended.astype(jnp.bfloat16).reshape(tokens, features)
    resid_one = flat_in.astype(jnp.float32) + plain_dot(attended, full_out)
    norm_one = norm_rows(resid_one, gains[0], biases[0]).astype(jnp.bfloat16)
    up_proj = plain_dot(norm_one, full_up)
    active = gelu_exact(up_proj).astype(jnp.bfloat16)
    resid_two = norm_one.astype(jnp.float32) + plain_dot(active, full_down)
    norm_two = norm_rows(resid_two, gains[1], biases[1]).astype(jnp.bfloat16)
    vocab_rows = full_table.shape[0]
    char_rows = (groups[:, None, None] * SUBV + char_ids).reshape(tokens * nchar)
    onehot = (char_rows[:, None] == jnp.arange(vocab_rows)[None, :]).astype(jnp.bfloat16)
    char_emb = plain_dot(onehot, full_table).astype(jnp.bfloat16).reshape(tokens, nchar, -1)
    char_live = (char_ids > 0).reshape(tokens, nchar)
    steps_in = jnp.stack([char_emb, char_emb[:, ::-1]], 0).transpose(2, 0, 1, 3)
    steps_live = jnp.stack([char_live, char_live[:, ::-1]], 0).transpose(2, 0, 1)[..., None]
    inward = full_input.reshape(2, -1, full_input.shape[1])
    recurrent = full_recur.reshape(2, -1, full_recur.shape[1])
    hidden_units = recurrent.shape[1]
    gates_in = jnp.einsum("cdtz,dzg->cdtg", steps_in, inward, preferred_element_type=jnp.float32)

    def gru_step(carry_state, step_input):
        gate_input, is_live = step_input
        gate_recur = jnp.einsum(
            "dth,dhg->dtg",
            carry_state.astype(jnp.bfloat16),
            recurrent,
            preferred_element_type=jnp.float32,
        )
        return (cell(gate_input, gate_recur, carry_state, is_live), carry_state)

    start_state = jnp.zeros((2, tokens, hidden_units), jnp.float32)
    last_state, prior_states = lax.scan(gru_step, start_state, (gates_in, steps_live))
    char_vec = jnp.concatenate([last_state[0], last_state[1]], -1).astype(jnp.bfloat16)
    merge_mats = full_merge.reshape(2, features, features)
    merged_rows = jnp.concatenate(
        [plain_dot(norm_two, merge_mats[0]), plain_dot(char_vec, merge_mats[1])], -1
    ).astype(jnp.bfloat16)
    padded = with_halo(merged_rows.reshape(seq_count, local_len, 2 * features), (("seq", 1),), 1)
    kernel = full_conv.reshape(3, 2 * features, features)
    windows = [
        padded[:, offset : offset + local_len].reshape(tokens, 2 * features) for offset in range(3)
    ]
    conv_out = (
        plain_dot(windows[0], kernel[0])
        + plain_dot(windows[1], kernel[1])
        + plain_dot(windows[2], kernel[2])
    )
    resid_three = norm_two.astype(jnp.float32) + conv_out
    result_rows, pull_three = jax.vjp(norm_rows, resid_three, gains[2], biases[2])
    result = result_rows.astype(jnp.bfloat16).reshape(seq_count, local_len, features)
    back_qkv, back_out, back_up, back_down = full_qkv, full_out, full_up, full_down
    back_input, back_recur, back_merge, back_conv = full_input, full_recur, full_merge, full_conv
    merge_back = back_merge.reshape(2, features, features)
    kernel_back = back_conv.reshape(3, 2 * features, features)
    inward_back = back_input.reshape(2, -1, back_input.shape[1])
    recur_back = back_recur.reshape(2, -1, back_recur.shape[1])
    seed_rows = cotangent.reshape(tokens, features).astype(jnp.float32)
    grad_three, gain_three, bias_three = pull_three(seed_rows)
    conv_seed = grad_three.astype(jnp.bfloat16)
    conv_grad = jnp.concatenate([grad_dot(windows[offset], conv_seed) for offset in range(3)], 0)
    seed_padded = with_halo(conv_seed.reshape(seq_count, local_len, features), (("seq", 1),), 1)
    merged_grad = back_dot(
        seed_padded[:, 2 : 2 + local_len].reshape(tokens, features), kernel_back[0]
    )
    merged_grad = merged_grad + back_dot(
        seed_padded[:, 1 : 1 + local_len].reshape(tokens, features), kernel_back[1]
    )
    merged_grad = merged_grad + back_dot(
        seed_padded[:, 0:local_len].reshape(tokens, features), kernel_back[2]
    )
    merged_grad = merged_grad.astype(jnp.bfloat16)
    token_part = merged_grad[:, :features]
    char_part = merged_grad[:, features:]
    merge_grad = jnp.concatenate([grad_dot(norm_two, token_part), grad_dot(char_vec, char_part)], 0)
    two_grad = grad_three + back_dot(token_part, merge_back[0])
    charvec_grad = back_dot(char_part, merge_back[1])
    _, pull_two = jax.vjp(norm_rows, resid_two, gains[1], biases[1])
    grad_two, gain_two, bias_two = pull_two(two_grad)
    down_seed = grad_two.astype(jnp.bfloat16)
    down_grad = grad_dot(active, down_seed)
    active_grad = back_dot(down_seed, back_down)
    _, pull_gelu = jax.vjp(gelu_exact, up_proj)
    up_seed = pull_gelu(active_grad)[0].astype(jnp.bfloat16)
    up_grad = grad_dot(norm_one, up_seed)
    one_grad = grad_two + back_dot(up_seed, back_up)
    _, pull_one = jax.vjp(norm_rows, resid_one, gains[0], biases[0])
    grad_one, gain_one, bias_one = pull_one(one_grad)
    out_seed = grad_one.astype(jnp.bfloat16)
    out_grad = grad_dot(attended, out_seed)
    attn_seed = (
        back_dot(out_seed, back_out)
        .astype(jnp.bfloat16)
        .reshape(seq_count, local_len, head_count, HD)
    )
    probs_again = jnp.exp(score_block() - log_total)
    probs_grad = jnp.einsum(
        "sqhd,skhd->shqk", attn_seed, all_values, preferred_element_type=jnp.float32
    )
    score_grad = probs_again * (
        probs_grad - jnp.sum(probs_again * probs_grad, axis=-1, keepdims=True)
    )
    score_grad = score_grad.astype(jnp.bfloat16)
    query_grad = (
        jnp.einsum("shqk,skhd->sqhd", score_grad, all_keys, preferred_element_type=jnp.float32)
        * score_scale
    )
    key_grad = (
        jnp.einsum("shqk,sqhd->skhd", score_grad, queries, preferred_element_type=jnp.float32)
        * score_scale
    )
    value_grad = jnp.einsum(
        "shqk,sqhd->skhd",
        probs_again.astype(jnp.bfloat16),
        attn_seed,
        preferred_element_type=jnp.float32,
    )
    key_own, value_own = (
        lax.psum_scatter(
            key_grad.reshape(seq_count, key_span, features).astype(jnp.bfloat16),
            "seq",
            scatter_dimension=1,
            tiled=True,
        ).astype(jnp.float32),
        lax.psum_scatter(
            value_grad.reshape(seq_count, key_span, features).astype(jnp.bfloat16),
            "seq",
            scatter_dimension=1,
            tiled=True,
        ).astype(jnp.float32),
    )
    qkv_seed = jnp.concatenate(
        [
            query_grad.reshape(tokens, features),
            key_own.reshape(tokens, features),
            value_own.reshape(tokens, features),
        ],
        -1,
    ).astype(jnp.bfloat16)
    qkv_grad = grad_dot(flat_in, qkv_seed)
    hidden_grad = (
        (grad_one + back_dot(qkv_seed, back_qkv))
        .astype(jnp.bfloat16)
        .reshape(seq_count, local_len, features)
    )
    state_seed = jnp.stack([charvec_grad[:, :hidden_units], charvec_grad[:, hidden_units:]], 0)

    def back_step(carry_in, step_input):
        state_grad, recur_total = carry_in
        gate_input, is_live, carry_state = step_input
        state_low = carry_state.astype(jnp.bfloat16)
        gate_recur = jnp.einsum(
            "dth,dhg->dtg", state_low, recur_back, preferred_element_type=jnp.float32
        )

        def cell_local(given, recurred, previous):
            return cell(given, recurred, previous, is_live)

        _, pull_cell = jax.vjp(cell_local, gate_input, gate_recur, carry_state)
        input_part, recur_part, prior_part = pull_cell(state_grad)
        recur_low = recur_part.astype(jnp.bfloat16)
        prior_part = prior_part + jnp.einsum(
            "dtg,dhg->dth", recur_low, recur_back, preferred_element_type=jnp.float32
        )
        recur_total = recur_total + jnp.einsum(
            "dth,dtg->dhg", state_low, recur_low, preferred_element_type=jnp.float32
        )
        return ((prior_part, recur_total), input_part.astype(jnp.bfloat16))

    recur_zero = jnp.zeros((2, hidden_units, recur_back.shape[2]), jnp.float32)
    (_, recur_sum), input_seeds = lax.scan(
        back_step, (state_seed, recur_zero), (gates_in, steps_live, prior_states), reverse=True
    )
    input_mats = jnp.einsum(
        "cdtz,cdtg->dzg", steps_in, input_seeds, preferred_element_type=jnp.float32
    )
    step_chars = jnp.einsum(
        "cdtg,dzg->cdtz", input_seeds, inward_back, preferred_element_type=jnp.float32
    )
    char_grad = step_chars[:, 0].transpose(1, 0, 2) + step_chars[::-1, 1].transpose(1, 0, 2)
    char_grad = char_grad.astype(jnp.bfloat16).reshape(tokens * nchar, -1)
    table_grad = grad_dot(onehot, char_grad)
    gain_grad = jnp.stack([gain_one, gain_two, gain_three], 0)
    bias_grad = jnp.stack([bias_one, bias_two, bias_three], 0)
    input_flat = input_mats.reshape(-1, input_mats.shape[2])
    recur_flat = recur_sum.reshape(-1, recur_sum.shape[2])
    terms = [merge_grad, conv_grad, down_grad, up_grad, out_grad, qkv_grad, recur_flat, input_flat, table_grad]
    parts = [x.astype(jnp.bfloat16).reshape(devices, -1, x.shape[1]) for x in terms]
    parts.append(pack_norms(gain_grad, bias_grad, devices))
    sums = scatter_all(dp_size, parts)
    merge_sum, conv_sum, down_sum, up_sum, out_sum, qkv_sum, recur_total, input_total, table_sum, norm_sum = sums
    gain_sum, bias_sum = unpack_norms(norm_sum[None], norm_gain.shape)
    return (result, hidden_grad, qkv_sum, out_sum, up_sum, down_sum, gain_sum, bias_sum, table_sum, input_total, recur_total, merge_sum, conv_sum)


def solution(mesh):
    placed = (
        P("dp", "seq", None),
        P("dp", "seq", None),
        P("dp"),
        P("dp"),
        P("dp", "seq", None),
        P(("dp", "seq"), None),
        P(("dp", "seq"), None),
        P(("dp", "seq"), None),
        P(("dp", "seq"), None),
        P(None, ("dp", "seq")),
        P(None, ("dp", "seq")),
        P(("dp", "seq"), None),
        P(("dp", "seq"), None),
        P(("dp", "seq"), None),
        P(("dp", "seq"), None),
        P(("dp", "seq"), None),
    )
    return jax.shard_map(
        local,
        mesh=mesh,
        in_specs=placed,
        out_specs=(
            P("dp", "seq", None),
            P("dp", "seq", None),
            P(("dp", "seq"), None),
            P(("dp", "seq"), None),
            P(("dp", "seq"), None),
            P(("dp", "seq"), None),
            P(None, ("dp", "seq")),
            P(None, ("dp", "seq")),
            P(("dp", "seq"), None),
            P(("dp", "seq"), None),
            P(("dp", "seq"), None),
            P(("dp", "seq"), None),
            P(("dp", "seq"), None),
        ),
        check_vma=False,
    )
```

```python
import functools
import math

import jax
import jax.numpy as jnp
from jax import lax
from jax.experimental import pallas as pl
from jax.experimental.pallas import tpu as pltpu
from jax.sharding import PartitionSpec as P

MESH = pl.DeviceIdType.MESH

HD = 64
SUBV = 128

eps = 1e-05

class Place:
    def __init__(self, dp_size):
        dp, seq = lax.axis_index("dp"), lax.axis_index("seq")
        self.lines = dp_size // 2
        self.a, self.b = dp // 2, lax.rem(dp, 2)
        self.y, self.c = seq // 2, lax.rem(seq, 2)
        flip_b = (self.a * 2 + 1 - self.b, seq)
        flip_y = (dp, (1 - self.y) * 2 + self.c)
        pick = lambda u, v: tuple(i + self.c * (j - i) for i, j in zip(u, v))
        self.first, self.second = pick(flip_b, flip_y), pick(flip_y, flip_b)
        self.sibling = (dp, self.y * 2 + 1 - self.c)
        self.up, self.down = (dp + 2, seq), (dp - 2, seq)
        self.f = self.b + self.c * (self.y - self.b)
        self.s = self.y + self.c * (self.b - self.y)
        self.has_up, self.has_down = self.a < self.lines - 1, self.a > 0

    def unit(self, a, f, s, c=None):
        c = self.c if c is None else c
        return a * 8 + f * (4 - 2 * c) + s * (2 + 2 * c) + c

    def barrier(self):
        sem = pltpu.get_barrier_semaphore()
        for who in (self.first, self.second, self.sibling):
            pl.semaphore_signal(sem, inc=1, device_id=who, device_id_type=MESH)

        @pl.when(self.has_up)
        def _():
            pl.semaphore_signal(sem, inc=1, device_id=self.up, device_id_type=MESH)

        @pl.when(self.has_down)
        def _():
            pl.semaphore_signal(sem, inc=1, device_id=self.down, device_id_type=MESH)

        pl.semaphore_wait(sem, 3 + self.has_up.astype(jnp.int32) + self.has_down.astype(jnp.int32))


def push(src, dst, send, recv, who):
    return pltpu.make_async_remote_copy(
        src_ref=src, dst_ref=dst, send_sem=send, recv_sem=recv, device_id=who, device_id_type=MESH
    )


class Gather:
    def __init__(self, at, shard, full, sems):
        self.at, self.shard, self.full = at, shard, full
        self.up_s, self.down_s, self.sum_s, self.line_r, self.second_r, self.one = sems

    def to_lines(self, src, slot, index, up, down):
        at = self.at
        if up is not False:
            @pl.when(at.has_up if up is True else jnp.logical_and(up, at.has_up))
            def _():
                push(src, self.full.at[index], self.up_s.at[slot], self.line_r.at[slot], at.up).start()
        if down is not False:
            @pl.when(at.has_down if down is True else jnp.logical_and(down, at.has_down))
            def _():
                push(src, self.full.at[index], self.down_s.at[slot], self.line_r.at[slot], at.down).start()

    def across(self, src, slot, index):
        push(src, self.full.at[index], self.sum_s.at[0], self.second_r.at[slot], self.at.second).start()
        self.aside(src, index)

    def aside(self, src, index):
        push(src, self.full.at[index], self.sum_s.at[1], self.one.at[1], self.at.sibling).start()

    def begin(self):
        at = self.at
        me = at.unit(at.a, at.f, at.s)
        pltpu.make_async_copy(self.shard, self.full.at[me], self.one.at[3]).start()
        push(self.shard, self.full.at[me], self.one.at[2], self.one.at[0], at.first).start()
        slot = at.a * 2 + at.f
        self.to_lines(self.shard, slot, me, True, True)
        self.across(self.shard, slot, me)

    def after_first(self):
        at = self.at
        index = at.unit(at.a, 1 - at.f, at.s)
        ref = self.full.at[index]
        push(ref, ref, self.one.at[2], self.one.at[0], at.first).wait_recv()
        slot = at.a * 2 + 1 - at.f
        self.to_lines(ref, slot, index, True, True)
        self.across(ref, slot, index)

    def after_line(self, k, g):
        at = self.at
        for sign in (-1, 1):
            a = at.a + sign * k
            f = at.f if g == 0 else 1 - at.f

            @pl.when(a >= 0 if sign < 0 else a < at.lines)
            def _():
                index, slot = at.unit(a, f, at.s), a * 2 + f
                ref = self.full.at[index]
                push(ref, ref, self.up_s.at[slot], self.line_r.at[slot], at.up).wait_recv()
                self.to_lines(ref, slot, index, sign < 0, sign > 0)
                self.across(ref, slot, index)

    def after_second(self, k, g):
        at = self.at
        for sign in (-1, 1) if k else (1,):
            a = at.a + sign * k
            f = at.f if g == 0 else 1 - at.f

            @pl.when(a >= 0 if sign < 0 else a < at.lines)
            def _():
                index, slot = at.unit(a, f, 1 - at.s), a * 2 + f
                ref = self.full.at[index]
                push(ref, ref, self.sum_s.at[0], self.second_r.at[slot], at.second).wait_recv()
                self.aside(ref, index)

    def finish(self):
        at, n = self.at, self.at.lines
        me = at.unit(at.a, at.f, at.s)
        half = self.full.at[pl.ds(0, 4 * n)]
        push(half, half, self.sum_s.at[1], self.one.at[1], at.sibling).wait_recv()
        pltpu.make_async_copy(self.shard, self.full.at[me], self.one.at[3]).wait()
        push(self.shard, self.full.at[me], self.one.at[2], self.one.at[0], at.first).wait_send()
        push(half, half, self.sum_s.at[1], self.one.at[1], at.sibling).wait_send()
        part = self.full.at[pl.ds(0, 2 * n)]
        push(part, part, self.sum_s.at[0], self.one.at[0], at.second).wait_send()
        for a in range(n):
            for f in range(2):
                slot = a * 2 + f
                ref = self.full.at[0]

                @pl.when(jnp.logical_and(at.has_up, a <= at.a))
                def _():
                    push(ref, ref, self.up_s.at[slot], self.line_r.at[slot], at.up).wait_send()

                @pl.when(jnp.logical_and(at.has_down, a >= at.a))
                def _():
                    push(ref, ref, self.down_s.at[slot], self.line_r.at[slot], at.down).wait_send()


def gather_sems(n):
    dma = pltpu.SemaphoreType.DMA
    return [dma((2 * n,)), dma((2 * n,)), dma((2,)), dma((2 * n,)), dma((2 * n,)), dma((4,))]


def gather_kernel(dp_size, count, *refs):
    shards, fulls, sems = refs[:count], refs[count : 2 * count], refs[2 * count :]
    at = Place(dp_size)
    at.barrier()
    jobs = [Gather(at, shards[i], fulls[i], sems[6 * i : 6 * i + 6]) for i in range(count)]
    for job in jobs:
        job.begin()
    for job in jobs:
        job.after_first()
    for k in range(1, at.lines):
        for g in range(2):
            for job in jobs:
                job.after_line(k, g)
            for job in jobs:
                job.after_second(k - 1, g)
    for g in range(2):
        for job in jobs:
            job.after_second(at.lines - 1, g)
    for job in jobs:
        job.finish()


def gather_all(dp_size, devices, shards, cid=1):
    count = len(shards)
    return pl.pallas_call(
        functools.partial(gather_kernel, dp_size, count),
        out_shape=[jax.ShapeDtypeStruct((devices,) + x.shape, x.dtype) for x in shards],
        in_specs=[pl.BlockSpec(memory_space=pl.ANY)] * count,
        out_specs=[pl.BlockSpec(memory_space=pl.ANY)] * count,
        scratch_shapes=gather_sems(dp_size // 2) * count,
        compiler_params=pltpu.CompilerParams(collective_id=cid, has_side_effects=True),
    )(*shards)


def wide(x):
    return x.astype(jnp.float32)


def add_into(dst, src):
    dst[...] = (wide(dst[...]) + wide(src[...])).astype(dst.dtype)


class Scatter:
    def __init__(self, at, part, out, bufs, sems):
        self.at, self.part, self.out = at, part, out
        self.own, self.sib, self.sec, self.line, self.fst = bufs
        self.one, self.line_s, self.line_r = sems

    def begin(self):
        at = self.at

        def body(j, carry):
            a, f, s = j // 4, lax.rem(j // 2, 2), lax.rem(j, 2)
            push(self.part.at[at.unit(a, f, s, 1 - at.c)], self.sib.at[j], self.one.at[0], self.one.at[1], at.sibling).start()
            return carry

        lax.fori_loop(0, 4 * at.lines, body, 0)

        def load(j, carry):
            a, f, s = j // 4, lax.rem(j // 2, 2), lax.rem(j, 2)
            pltpu.make_async_copy(self.part.at[at.unit(a, f, s)], self.own.at[j], self.one.at[2]).start()
            return carry

        lax.fori_loop(0, 4 * at.lines, load, 0)

    def after_sibling(self):
        at = self.at
        n = 2 * at.lines
        pltpu.make_async_copy(self.part.at[pl.ds(0, 2 * n)], self.own, self.one.at[2]).wait()
        push(self.sib, self.sib, self.one.at[0], self.one.at[1], at.sibling).wait_recv()

        def far(q, carry):
            j = q * 2 + 1 - at.s
            add_into(self.own.at[j], self.sib.at[j])
            return carry

        def send(q, carry):
            push(self.own.at[q * 2 + 1 - at.s], self.sec.at[q], self.one.at[3], self.one.at[4], at.second).start()
            return carry

        def near(q, carry):
            j = q * 2 + at.s
            add_into(self.own.at[j], self.sib.at[j])
            return carry

        lax.fori_loop(0, n, far, 0)
        lax.fori_loop(0, n, send, 0)
        lax.fori_loop(0, n, near, 0)

    def after_second(self):
        at = self.at
        push(self.sec, self.sec, self.one.at[3], self.one.at[4], at.second).wait_recv()

        def body(q, carry):
            add_into(self.own.at[q * 2 + at.s], self.sec.at[q])
            return carry

        lax.fori_loop(0, 2 * at.lines, body, 0)

    def hop(self, low, high, inward, dst, extra):
        at = self.at
        has, who = (at.has_up, at.down) if dst < 0 else (at.has_down, at.up)

        def take(q, carry):
            push(self.line.at[q], self.line.at[q], self.line_s.at[q], self.line_r.at[q], who).wait_recv()
            add_into(self.own.at[q * 2 + at.s], self.line.at[q])
            return carry

        @pl.when(has)
        def _():
            lax.fori_loop(low, high, take, 0)

        def send(q, carry):
            slot = q if dst < 0 else jnp.where(q // 2 == at.a + 1, 2 * at.lines + lax.rem(q, 2), q)
            push(self.own.at[q * 2 + at.s], self.line.at[slot], self.line_s.at[q], self.line_r.at[slot], who).start()
            return carry

        lax.fori_loop(low, high, send, 0)

    def along(self, h):
        at = self.at
        n = at.lines
        hops = n - 1 if n <= 4 else 1

        @pl.when(jnp.logical_and(at.has_down, at.lines - 1 - at.a == h) if hops > 1 else at.has_down)
        def _():
            self.hop(0, 2 * at.a, at.up, -1, None)

        @pl.when(jnp.logical_and(at.has_up, at.a == h) if hops > 1 else at.has_up)
        def _():
            self.hop(2 * at.a + 2, 2 * n, at.down, 1, None)

    def ends(self, f, into):
        at = self.at
        for has, slot in ((at.has_up, 2 * at.a + f), (at.has_down, 2 * at.lines + f)):
            @pl.when(has)
            def _():
                ref = self.line.at[slot]
                push(ref, ref, self.line_s.at[0], self.line_r.at[slot], at.first).wait_recv()
                into[...] = (wide(into[...]) + wide(ref[...])).astype(into.dtype)

    def last_send(self):
        at = self.at
        mine = self.own.at[(2 * at.a + 1 - at.f) * 2 + at.s]
        self.ends(1 - at.f, mine)
        push(mine, self.fst, self.one.at[5], self.one.at[6], at.first).start()
        self.out[...] = wide(self.own[(2 * at.a + at.f) * 2 + at.s])
        self.ends(at.f, self.out)

    def finish(self):
        at = self.at
        push(self.fst, self.fst, self.one.at[5], self.one.at[6], at.first).wait_recv()
        self.out[...] = self.out[...] + wide(self.fst[...])

    def drain(self):
        at = self.at
        n = at.lines
        push(self.sib, self.sib, self.one.at[0], self.one.at[1], at.sibling).wait_send()
        push(self.sec, self.sec, self.one.at[3], self.one.at[4], at.second).wait_send()
        push(self.fst, self.fst, self.one.at[5], self.one.at[6], at.first).wait_send()

        def body(q, carry):
            @pl.when(q // 2 != at.a)
            def _():
                push(self.own.at[q], self.own.at[q], self.line_s.at[q], self.line_r.at[q], at.first).wait_send()
            return carry

        lax.fori_loop(0, 2 * n, body, 0)


def scatter_buffers(n, shape, dtype):
    v = lambda k: pltpu.VMEM((k,) + shape, dtype)
    return [v(4 * n), v(4 * n), v(2 * n), v(2 * n + 2), pltpu.VMEM(shape, dtype)]


def scatter_sems(n):
    dma = pltpu.SemaphoreType.DMA
    return [dma((7,)), dma((2 * n,)), dma((2 * n + 2,))]


def scatter_stages(lines):
    hops = lines - 1 if lines <= 4 else 1
    stages = [Scatter.after_sibling, Scatter.after_second]
    for h in range(hops):
        stages.append(functools.partial(Scatter.along, h=h))
    return stages + [Scatter.last_send, Scatter.finish]


def scatter_kernel(dp_size, count, *refs):
    parts, outs, rest = refs[:count], refs[count : 2 * count], refs[2 * count :]
    at = Place(dp_size)
    at.barrier()
    jobs = [Scatter(at, parts[i], outs[i], rest[8 * i : 8 * i + 5], rest[8 * i + 5 : 8 * i + 8]) for i in range(count)]
    for job in jobs:
        job.begin()
    stages = scatter_stages(at.lines)
    for t in range(count + len(stages) - 1):
        for k, stage in enumerate(stages):
            if 0 <= t - k < count:
                stage(jobs[t - k])
    for job in jobs:
        job.drain()


def scatter_all(dp_size, parts, cid=2):
    count = len(parts)
    n = dp_size // 2
    scratch = []
    for x in parts:
        scratch += scatter_buffers(n, x.shape[1:], x.dtype) + scatter_sems(n)
    return pl.pallas_call(
        functools.partial(scatter_kernel, dp_size, count),
        out_shape=[jax.ShapeDtypeStruct(x.shape[1:], jnp.float32) for x in parts],
        in_specs=[pl.BlockSpec(memory_space=pl.ANY)] * count,
        out_specs=[pl.BlockSpec(memory_space=pltpu.VMEM)] * count,
        scratch_shapes=scratch,
        compiler_params=pltpu.CompilerParams(collective_id=cid, has_side_effects=True, vmem_limit_bytes=64000000),
    )(*parts)


def with_halo(x, sides, width):
    for axis, dim in sides:
        devices, length = (lax.axis_size(axis), x.shape[dim])
        up = [(i, (i + 1) % devices) for i in range(devices - 1)]
        down = [(j, i) for i, j in up]
        last = lax.slice_in_dim(x, length - width, length, axis=dim)
        first = lax.slice_in_dim(x, 0, width, axis=dim)
        before = lax.ppermute(last, axis, up)
        after = lax.ppermute(first, axis, down)
        x = jnp.concatenate([before, x, after], axis=dim)
    return x


def norm_rows(residual, row_gain, row_bias):
    centered = residual - jnp.mean(residual, axis=-1, keepdims=True)
    spread = jnp.mean(centered * centered, axis=-1, keepdims=True)
    return centered * lax.rsqrt(spread + eps) * row_gain + row_bias


def gelu_exact(pre_act):
    return jax.nn.gelu(pre_act, approximate=False)


def plain_dot(left, right):
    return jnp.dot(left, right, preferred_element_type=jnp.float32)


def grad_dot(left, right):
    return lax.dot_general(
        left, right, (((0,), (0,)), ((), ())), preferred_element_type=jnp.float32
    )


def back_dot(left, right):
    return lax.dot_general(
        left, right, (((1,), (1,)), ((), ())), preferred_element_type=jnp.float32
    )


def squash(x):
    return 0.5 * jnp.tanh(0.5 * x) + 0.5


def slot_onehot(ids, slots, subset):
    cols = lax.broadcasted_iota(jnp.int32, (ids.shape[0], subset), 1)
    hots = [(ids[:, s : s + 1] == cols).astype(jnp.bfloat16) for s in slots]
    return jnp.concatenate(hots, 0)


def gru_embed(ids_ref, table, w_in, emb_ref, gates, chunk=4):
    rows, nchar = ids_ref.shape
    ids = ids_ref[...]
    for k in range(0, nchar, chunk):
        hot = slot_onehot(ids, range(k, k + chunk), table.shape[0])
        emb = plain_dot(hot, table[...]).astype(jnp.bfloat16)
        emb_ref[k : k + chunk] = emb.reshape(chunk, rows, -1)
        for d in range(2):
            gates[d, k : k + chunk] = plain_dot(emb, w_in[d]).reshape(chunk, rows, -1)


def gru_step(d, slot, count, gates, w_rec, state, factor, keep, prior):
    units = state.shape[2]
    old = state[d]
    low = old.astype(jnp.bfloat16)
    rec = plain_dot(low, w_rec[d])
    gi = gates[d, slot]
    reset = squash(gi[:, :units] + rec[:, :units])
    update = squash(gi[:, units : 2 * units] + rec[:, units : 2 * units])
    rec_n = rec[:, 2 * units :]
    cand = jnp.tanh(gi[:, 2 * units :] + reset * rec_n)
    live = slot < count
    state[d] = jnp.where(live, (1.0 - update) * cand + update * old, old)
    by_cand = jnp.where(live, (1.0 - update) * (1.0 - cand * cand), 0.0)
    by_update = jnp.where(live, (old - cand) * update * (1.0 - update), 0.0)
    by_reset = by_cand * rec_n * reset * (1.0 - reset)
    prior[...] = low
    keep[...] = jnp.where(live, update, 1.0)
    for k, x in enumerate((by_reset, by_update, by_cand, reset)):
        factor[:, k * units : (k + 1) * units] = x.astype(factor.dtype)


def gru_forward_kernel(ids_ref, table, w_in, w_rec, vec, emb, f0, f1, z0, z1, h0, h1, gates, state):
    i = pl.program_id(0)
    nchar = pl.num_programs(0)

    @pl.when(i == 0)
    def _():
        gru_embed(ids_ref, table, w_in, emb, gates)
        state[...] = jnp.zeros_like(state)

    count = jnp.sum((ids_ref[...] > 0).astype(jnp.int32), axis=1, keepdims=True)
    gru_step(0, i, count, gates, w_rec, state, f0.at[0], z0.at[0], h0.at[0])
    gru_step(1, nchar - 1 - i, count, gates, w_rec, state, f1.at[0], z1.at[0], h1.at[0])

    @pl.when(i == nchar - 1)
    def _():
        units = state.shape[2]
        vec[:, :units] = state[0].astype(vec.dtype)
        vec[:, units:] = state[1].astype(vec.dtype)


def slot_specs(nchar, rows, cols, backward):
    up = pl.BlockSpec((1, rows, cols), lambda i: (i, 0, 0))
    down = pl.BlockSpec((1, rows, cols), lambda i: (nchar - 1 - i, 0, 0))
    return [down, up] if backward else [up, down]


def gru_forward(ids, table, w_in, w_rec):
    rows, nchar = ids.shape
    width, units = table.shape[1], w_rec.shape[1]
    whole = lambda shape: pl.BlockSpec(shape, lambda i: (0,) * len(shape))
    slots = functools.partial(slot_specs, nchar, rows, backward=False)
    shape = jax.ShapeDtypeStruct
    factor = shape((nchar, rows, 4 * units), jnp.bfloat16)
    keep = shape((nchar, rows, units), jnp.float32)
    prior = shape((nchar, rows, units), jnp.bfloat16)
    return pl.pallas_call(
        gru_forward_kernel,
        grid=(nchar,),
        out_shape=[
            shape((rows, 2 * units), jnp.bfloat16),
            shape((nchar, rows, width), jnp.bfloat16),
            factor, factor, keep, keep, prior, prior,
        ],
        in_specs=[whole(x.shape) for x in (ids, table, w_in, w_rec)],
        out_specs=[whole((rows, 2 * units)), whole((nchar, rows, width))]
        + slots(4 * units) + slots(units) + slots(units),
        scratch_shapes=[
            pltpu.VMEM((2, nchar, rows, 3 * units), jnp.float32),
            pltpu.VMEM((2, rows, units), jnp.float32),
        ],
        compiler_params=pltpu.CompilerParams(vmem_limit_bytes=60000000),
    )(ids, table, w_in, w_rec)


def gru_back_step(d, slot, factor, keep, w_rec, grad, seeds):
    units = grad.shape[2]
    g = grad[d]
    part = lambda k: factor[:, k * units : (k + 1) * units].astype(jnp.float32)
    by_cand = g * part(2)
    seeds[d, slot, :, :units] = (g * part(0)).astype(seeds.dtype)
    seeds[d, slot, :, units : 2 * units] = (g * part(1)).astype(seeds.dtype)
    seeds[d, slot, :, 2 * units : 3 * units] = (by_cand * part(3)).astype(seeds.dtype)
    seeds[d, slot, :, 3 * units :] = by_cand.astype(seeds.dtype)
    grad[d] = g * keep[...] + back_dot(seeds[d, slot, :, : 3 * units], w_rec[d])


def gru_weight_grads(d, seeds, emb, prior, d_in, d_rec):
    _, nchar, rows, wide = seeds.shape
    units = wide // 4
    states = prior[...].reshape(nchar * rows, units)
    chars = emb[...].reshape(nchar * rows, -1)
    col = lambda k: seeds[d, :, :, k * units : (k + 1) * units].reshape(nchar * rows, units)
    for k in range(3):
        d_rec[d, :, k * units : (k + 1) * units] = grad_dot(states, col(k)).astype(d_rec.dtype)
        own = col(3 if k == 2 else k)
        d_in[d, :, k * units : (k + 1) * units] = grad_dot(chars, own).astype(d_in.dtype)


def gru_char_grads(ids_ref, seeds, w_in, d_table, chunk=4):
    _, nchar, rows, wide = seeds.shape
    units = wide // 4
    ids = ids_ref[...]
    total = jnp.zeros(d_table.shape, jnp.float32)
    for k in range(0, nchar, chunk):
        grad = None
        for d in range(2):
            both = seeds[d, k : k + chunk].reshape(chunk * rows, wide)
            part = back_dot(both[:, : 2 * units], w_in[d][:, : 2 * units])
            part = part + back_dot(both[:, 3 * units :], w_in[d][:, 2 * units :])
            grad = part if grad is None else grad + part
        hot = slot_onehot(ids, range(k, k + chunk), d_table.shape[0])
        total = total + grad_dot(hot, grad.astype(jnp.bfloat16))
    d_table[...] = total


def gru_backward_kernel(ids_ref, seed, w_in, w_rec, emb, h0, h1, f0, f1, z0, z1, d_in, d_rec, d_table, grad, seeds):
    i = pl.program_id(0)
    nchar = pl.num_programs(0)

    @pl.when(i == 0)
    def _():
        units = grad.shape[2]
        grad[0] = seed[:, :units]
        grad[1] = seed[:, units:]

    gru_back_step(0, nchar - 1 - i, f0.at[0], z0.at[0], w_rec, grad, seeds)
    gru_back_step(1, i, f1.at[0], z1.at[0], w_rec, grad, seeds)

    @pl.when(i == nchar - 1)
    def _():
        gru_weight_grads(0, seeds, emb, h0, d_in, d_rec)
        gru_weight_grads(1, seeds, emb, h1, d_in, d_rec)
        gru_char_grads(ids_ref, seeds, w_in, d_table)


def gru_backward(ids, seed, w_in, w_rec, emb, h0, h1, f0, f1, z0, z1, subset):
    nchar, rows, width = emb.shape
    units = w_rec.shape[1]
    whole = lambda shape: pl.BlockSpec(shape, lambda i: (0,) * len(shape))
    slots = functools.partial(slot_specs, nchar, rows, backward=True)
    shape = jax.ShapeDtypeStruct
    return pl.pallas_call(
        gru_backward_kernel,
        grid=(nchar,),
        out_shape=[
            shape(w_in.shape, jnp.bfloat16),
            shape(w_rec.shape, jnp.bfloat16),
            shape((subset, width), jnp.float32),
        ],
        in_specs=[whole(x.shape) for x in (ids, seed, w_in, w_rec, emb, h0, h1)] + slots(4 * units) + slots(units),
        out_specs=[whole(w_in.shape), whole(w_rec.shape), whole((subset, width))],
        scratch_shapes=[
            pltpu.VMEM((2, rows, units), jnp.float32),
            pltpu.VMEM((2, nchar, rows, 4 * units), jnp.bfloat16),
        ],
        compiler_params=pltpu.CompilerParams(vmem_limit_bytes=60000000),
    )(ids, seed, w_in, w_rec, emb, h0, h1, f0, f1, z0, z1)


def pack_norms(gain, bias, devices=1):
    both = jnp.stack([gain, bias], 0)
    both = both.reshape(2, 3, devices, -1).transpose(2, 0, 1, 3).reshape(devices, -1)
    both = jnp.pad(both, ((0, 0), (0, 1024 - both.shape[1]))).reshape(devices, 8, 128)
    return both[0] if devices == 1 else both


def unpack_norms(tiles, shape):
    devices = tiles.shape[0]
    flat = tiles.reshape(devices, -1)[:, : 2 * shape[0] * shape[1]].reshape(devices, 2, *shape)
    both = flat.transpose(1, 2, 0, 3).reshape(2, shape[0], -1)
    return both[0], both[1]


def local(
    hidden,
    char_ids,
    groups,
    lengths,
    cotangent,
    qkv_weight,
    out_weight,
    up_weight,
    down_weight,
    norm_gain,
    norm_bias,
    char_table,
    gru_input,
    gru_recur,
    merge_weight,
    conv_weight,
):
    dp_size, devices = lax.axis_size("dp"), lax.axis_size("dp") * lax.axis_size("seq")
    norms = pack_norms(norm_gain, norm_bias)
    order = (char_table, gru_input, gru_recur, norms, qkv_weight, out_weight, up_weight, down_weight, merge_weight, conv_weight)
    gathered = gather_all(dp_size, devices, order)
    full_norms = gathered[3]
    (full_table, full_input, full_recur, _, full_qkv, full_out, full_up, full_down, full_merge, full_conv) = [
        x.reshape(-1, x.shape[2]) for x in gathered
    ]
    full_gain, full_bias = unpack_norms(full_norms, norm_gain.shape)
    seq_count, local_len, features = hidden.shape
    nchar = char_ids.shape[2]
    tokens = seq_count * local_len
    head_count = features // HD
    key_span = local_len * lax.axis_size("seq")
    score_scale = 1.0 / math.sqrt(HD)
    gains = full_gain.astype(jnp.float32)
    biases = full_bias.astype(jnp.float32)
    flat_in = hidden.reshape(tokens, features)
    qkv = plain_dot(flat_in, full_qkv).astype(jnp.bfloat16)
    queries = qkv[:, :features].reshape(seq_count, local_len, head_count, HD)
    own_keys = qkv[:, features : 2 * features].reshape(seq_count, local_len, features)
    own_values = qkv[:, 2 * features :].reshape(seq_count, local_len, features)
    all_keys, all_values = (
        lax.all_gather(own_keys, "seq", axis=1, tiled=True),
        lax.all_gather(own_values, "seq", axis=1, tiled=True),
    )
    all_keys = all_keys.reshape(seq_count, key_span, head_count, HD)
    all_values = all_values.reshape(seq_count, key_span, head_count, HD)
    key_valid = jnp.arange(key_span)[None, None, None, :] < lengths[:, None, None, None]

    def score_block():
        raw_scores = (
            jnp.einsum("sqhd,skhd->shqk", queries, all_keys, preferred_element_type=jnp.float32)
            * score_scale
        )
        return jnp.where(key_valid, raw_scores, -1000000000.0)

    scores = score_block()
    log_total = jax.nn.logsumexp(scores, axis=-1, keepdims=True)
    attn_probs = jnp.exp(scores - log_total).astype(jnp.bfloat16)
    attended = jnp.einsum(
        "shqk,skhd->sqhd", attn_probs, all_values, preferred_element_type=jnp.float32
    )
    attended = attended.astype(jnp.bfloat16).reshape(tokens, features)
    resid_one = flat_in.astype(jnp.float32) + plain_dot(attended, full_out)
    norm_one = norm_rows(resid_one, gains[0], biases[0]).astype(jnp.bfloat16)
    up_proj = plain_dot(norm_one, full_up)
    active = gelu_exact(up_proj).astype(jnp.bfloat16)
    resid_two = norm_one.astype(jnp.float32) + plain_dot(active, full_down)
    norm_two = norm_rows(resid_two, gains[1], biases[1]).astype(jnp.bfloat16)
    assert seq_count == 1
    flat_ids = char_ids.reshape(tokens, nchar)
    table_start = groups[0] * SUBV
    own_table = lax.dynamic_slice_in_dim(full_table, table_start, SUBV, 0)
    inward = full_input.reshape(2, -1, full_input.shape[1])
    recurrent = full_recur.reshape(2, -1, full_recur.shape[1])
    char_vec, char_emb, *kept = gru_forward(flat_ids, own_table, inward, recurrent)
    factors, keeps, priors = kept[:2], kept[2:4], kept[4:]
    merge_mats = full_merge.reshape(2, features, features)
    merged_rows = jnp.concatenate(
        [plain_dot(norm_two, merge_mats[0]), plain_dot(char_vec, merge_mats[1])], -1
    ).astype(jnp.bfloat16)
    padded = with_halo(merged_rows.reshape(seq_count, local_len, 2 * features), (("seq", 1),), 1)
    kernel = full_conv.reshape(3, 2 * features, features)
    windows = [
        padded[:, offset : offset + local_len].reshape(tokens, 2 * features) for offset in range(3)
    ]
    conv_out = (
        plain_dot(windows[0], kernel[0])
        + plain_dot(windows[1], kernel[1])
        + plain_dot(windows[2], kernel[2])
    )
    resid_three = norm_two.astype(jnp.float32) + conv_out
    result_rows, pull_three = jax.vjp(norm_rows, resid_three, gains[2], biases[2])
    result = result_rows.astype(jnp.bfloat16).reshape(seq_count, local_len, features)
    back_qkv, back_out, back_up, back_down = full_qkv, full_out, full_up, full_down
    back_merge, back_conv = full_merge, full_conv
    merge_back = back_merge.reshape(2, features, features)
    kernel_back = back_conv.reshape(3, 2 * features, features)
    seed_rows = cotangent.reshape(tokens, features).astype(jnp.float32)
    grad_three, gain_three, bias_three = pull_three(seed_rows)
    conv_seed = grad_three.astype(jnp.bfloat16)
    conv_grad = jnp.concatenate([grad_dot(windows[offset], conv_seed) for offset in range(3)], 0)
    seed_padded = with_halo(conv_seed.reshape(seq_count, local_len, features), (("seq", 1),), 1)
    merged_grad = back_dot(
        seed_padded[:, 2 : 2 + local_len].reshape(tokens, features), kernel_back[0]
    )
    merged_grad = merged_grad + back_dot(
        seed_padded[:, 1 : 1 + local_len].reshape(tokens, features), kernel_back[1]
    )
    merged_grad = merged_grad + back_dot(
        seed_padded[:, 0:local_len].reshape(tokens, features), kernel_back[2]
    )
    merged_grad = merged_grad.astype(jnp.bfloat16)
    token_part = merged_grad[:, :features]
    char_part = merged_grad[:, features:]
    merge_grad = jnp.concatenate([grad_dot(norm_two, token_part), grad_dot(char_vec, char_part)], 0)
    two_grad = grad_three + back_dot(token_part, merge_back[0])
    charvec_grad = back_dot(char_part, merge_back[1])
    _, pull_two = jax.vjp(norm_rows, resid_two, gains[1], biases[1])
    grad_two, gain_two, bias_two = pull_two(two_grad)
    down_seed = grad_two.astype(jnp.bfloat16)
    down_grad = grad_dot(active, down_seed)
    active_grad = back_dot(down_seed, back_down)
    _, pull_gelu = jax.vjp(gelu_exact, up_proj)
    up_seed = pull_gelu(active_grad)[0].astype(jnp.bfloat16)
    up_grad = grad_dot(norm_one, up_seed)
    one_grad = grad_two + back_dot(up_seed, back_up)
    _, pull_one = jax.vjp(norm_rows, resid_one, gains[0], biases[0])
    grad_one, gain_one, bias_one = pull_one(one_grad)
    out_seed = grad_one.astype(jnp.bfloat16)
    out_grad = grad_dot(attended, out_seed)
    attn_seed = (
        back_dot(out_seed, back_out)
        .astype(jnp.bfloat16)
        .reshape(seq_count, local_len, head_count, HD)
    )
    probs_again = jnp.exp(score_block() - log_total)
    probs_grad = jnp.einsum(
        "sqhd,skhd->shqk", attn_seed, all_values, preferred_element_type=jnp.float32
    )
    score_grad = probs_again * (
        probs_grad - jnp.sum(probs_again * probs_grad, axis=-1, keepdims=True)
    )
    score_grad = score_grad.astype(jnp.bfloat16)
    query_grad = (
        jnp.einsum("shqk,skhd->sqhd", score_grad, all_keys, preferred_element_type=jnp.float32)
        * score_scale
    )
    key_grad = (
        jnp.einsum("shqk,sqhd->skhd", score_grad, queries, preferred_element_type=jnp.float32)
        * score_scale
    )
    value_grad = jnp.einsum(
        "shqk,sqhd->skhd",
        probs_again.astype(jnp.bfloat16),
        attn_seed,
        preferred_element_type=jnp.float32,
    )
    key_own, value_own = (
        lax.psum_scatter(
            key_grad.reshape(seq_count, key_span, features).astype(jnp.bfloat16),
            "seq",
            scatter_dimension=1,
            tiled=True,
        ).astype(jnp.float32),
        lax.psum_scatter(
            value_grad.reshape(seq_count, key_span, features).astype(jnp.bfloat16),
            "seq",
            scatter_dimension=1,
            tiled=True,
        ).astype(jnp.float32),
    )
    qkv_seed = jnp.concatenate(
        [
            query_grad.reshape(tokens, features),
            key_own.reshape(tokens, features),
            value_own.reshape(tokens, features),
        ],
        -1,
    ).astype(jnp.bfloat16)
    qkv_grad = grad_dot(flat_in, qkv_seed)
    hidden_grad = (
        (grad_one + back_dot(qkv_seed, back_qkv))
        .astype(jnp.bfloat16)
        .reshape(seq_count, local_len, features)
    )
    input_mats, recur_sum, own_grad = gru_backward(
        flat_ids, charvec_grad, inward, recurrent, char_emb, *priors, *factors, *keeps, SUBV
    )
    table_grad = jnp.zeros(full_table.shape, jnp.bfloat16)
    table_grad = lax.dynamic_update_slice_in_dim(table_grad, own_grad.astype(jnp.bfloat16), table_start, 0)
    gain_grad = jnp.stack([gain_one, gain_two, gain_three], 0)
    bias_grad = jnp.stack([bias_one, bias_two, bias_three], 0)
    input_flat = input_mats.reshape(-1, input_mats.shape[2])
    recur_flat = recur_sum.reshape(-1, recur_sum.shape[2])
    terms = [merge_grad, conv_grad, down_grad, up_grad, out_grad, qkv_grad, recur_flat, input_flat, table_grad]
    parts = [x.astype(jnp.bfloat16).reshape(devices, -1, x.shape[1]) for x in terms]
    parts.append(pack_norms(gain_grad, bias_grad, devices))
    sums = scatter_all(dp_size, parts)
    merge_sum, conv_sum, down_sum, up_sum, out_sum, qkv_sum, recur_total, input_total, table_sum, norm_sum = sums
    gain_sum, bias_sum = unpack_norms(norm_sum[None], norm_gain.shape)
    return (result, hidden_grad, qkv_sum, out_sum, up_sum, down_sum, gain_sum, bias_sum, table_sum, input_total, recur_total, merge_sum, conv_sum)


def solution(mesh):
    placed = (
        P("dp", "seq", None),
        P("dp", "seq", None),
        P("dp"),
        P("dp"),
        P("dp", "seq", None),
        P(("dp", "seq"), None),
        P(("dp", "seq"), None),
        P(("dp", "seq"), None),
        P(("dp", "seq"), None),
        P(None, ("dp", "seq")),
        P(None, ("dp", "seq")),
        P(("dp", "seq"), None),
        P(("dp", "seq"), None),
        P(("dp", "seq"), None),
        P(("dp", "seq"), None),
        P(("dp", "seq"), None),
    )
    return jax.shard_map(
        local,
        mesh=mesh,
        in_specs=placed,
        out_specs=(
            P("dp", "seq", None),
            P("dp", "seq", None),
            P(("dp", "seq"), None),
            P(("dp", "seq"), None),
            P(("dp", "seq"), None),
            P(("dp", "seq"), None),
            P(None, ("dp", "seq")),
            P(None, ("dp", "seq")),
            P(("dp", "seq"), None),
            P(("dp", "seq"), None),
            P(("dp", "seq"), None),
            P(("dp", "seq"), None),
            P(("dp", "seq"), None),
        ),
        check_vma=False,
    )
```

```python
import functools
import math

import jax
import jax.numpy as jnp
from jax import lax
from jax.experimental import pallas as pl
from jax.experimental.pallas import tpu as pltpu
from jax.sharding import PartitionSpec as P

MESH = pl.DeviceIdType.MESH

HD = 64
SUBV = 128

eps = 1e-05

class Place:
    def __init__(self, dp_size):
        dp, seq = lax.axis_index("dp"), lax.axis_index("seq")
        self.lines = dp_size // 2
        self.a, self.b = dp // 2, lax.rem(dp, 2)
        self.y, self.c = seq // 2, lax.rem(seq, 2)
        flip_b = (self.a * 2 + 1 - self.b, seq)
        flip_y = (dp, (1 - self.y) * 2 + self.c)
        pick = lambda u, v: tuple(i + self.c * (j - i) for i, j in zip(u, v))
        self.first, self.second = pick(flip_b, flip_y), pick(flip_y, flip_b)
        self.sibling = (dp, self.y * 2 + 1 - self.c)
        self.up, self.down = (dp + 2, seq), (dp - 2, seq)
        self.f = self.b + self.c * (self.y - self.b)
        self.s = self.y + self.c * (self.b - self.y)
        self.has_up, self.has_down = self.a < self.lines - 1, self.a > 0

    def unit(self, a, f, s, c=None):
        c = self.c if c is None else c
        return a * 8 + f * (4 - 2 * c) + s * (2 + 2 * c) + c

    def barrier(self):
        sem = pltpu.get_barrier_semaphore()
        for who in (self.first, self.second, self.sibling):
            pl.semaphore_signal(sem, inc=1, device_id=who, device_id_type=MESH)

        @pl.when(self.has_up)
        def _():
            pl.semaphore_signal(sem, inc=1, device_id=self.up, device_id_type=MESH)

        @pl.when(self.has_down)
        def _():
            pl.semaphore_signal(sem, inc=1, device_id=self.down, device_id_type=MESH)

        pl.semaphore_wait(sem, 3 + self.has_up.astype(jnp.int32) + self.has_down.astype(jnp.int32))


def push(src, dst, send, recv, who):
    return pltpu.make_async_remote_copy(
        src_ref=src, dst_ref=dst, send_sem=send, recv_sem=recv, device_id=who, device_id_type=MESH
    )


class Gather:
    def __init__(self, at, shard, full, sems):
        self.at, self.shard, self.full = at, shard, full
        self.up_s, self.down_s, self.sum_s, self.line_r, self.second_r, self.one = sems

    def to_lines(self, src, slot, index, up, down):
        at = self.at
        if up is not False:
            @pl.when(at.has_up if up is True else jnp.logical_and(up, at.has_up))
            def _():
                push(src, self.full.at[index], self.up_s.at[slot], self.line_r.at[slot], at.up).start()
        if down is not False:
            @pl.when(at.has_down if down is True else jnp.logical_and(down, at.has_down))
            def _():
                push(src, self.full.at[index], self.down_s.at[slot], self.line_r.at[slot], at.down).start()

    def across(self, src, slot, index):
        push(src, self.full.at[index], self.sum_s.at[0], self.second_r.at[slot], self.at.second).start()
        self.aside(src, index)

    def aside(self, src, index):
        push(src, self.full.at[index], self.sum_s.at[1], self.one.at[1], self.at.sibling).start()

    def begin(self):
        at = self.at
        me = at.unit(at.a, at.f, at.s)
        pltpu.make_async_copy(self.shard, self.full.at[me], self.one.at[3]).start()
        push(self.shard, self.full.at[me], self.one.at[2], self.one.at[0], at.first).start()
        slot = at.a * 2 + at.f
        self.to_lines(self.shard, slot, me, True, True)
        self.across(self.shard, slot, me)

    def after_first(self):
        at = self.at
        index = at.unit(at.a, 1 - at.f, at.s)
        ref = self.full.at[index]
        push(ref, ref, self.one.at[2], self.one.at[0], at.first).wait_recv()
        slot = at.a * 2 + 1 - at.f
        self.to_lines(ref, slot, index, True, True)
        self.across(ref, slot, index)

    def after_line(self, k, g):
        at = self.at
        for sign in (-1, 1):
            a = at.a + sign * k
            f = at.f if g == 0 else 1 - at.f

            @pl.when(a >= 0 if sign < 0 else a < at.lines)
            def _():
                index, slot = at.unit(a, f, at.s), a * 2 + f
                ref = self.full.at[index]
                push(ref, ref, self.up_s.at[slot], self.line_r.at[slot], at.up).wait_recv()
                self.to_lines(ref, slot, index, sign < 0, sign > 0)
                self.across(ref, slot, index)

    def after_second(self, k, g):
        at = self.at
        for sign in (-1, 1) if k else (1,):
            a = at.a + sign * k
            f = at.f if g == 0 else 1 - at.f

            @pl.when(a >= 0 if sign < 0 else a < at.lines)
            def _():
                index, slot = at.unit(a, f, 1 - at.s), a * 2 + f
                ref = self.full.at[index]
                push(ref, ref, self.sum_s.at[0], self.second_r.at[slot], at.second).wait_recv()
                self.aside(ref, index)

    def finish(self):
        at, n = self.at, self.at.lines
        me = at.unit(at.a, at.f, at.s)
        half = self.full.at[pl.ds(0, 4 * n)]
        push(half, half, self.sum_s.at[1], self.one.at[1], at.sibling).wait_recv()
        pltpu.make_async_copy(self.shard, self.full.at[me], self.one.at[3]).wait()
        push(self.shard, self.full.at[me], self.one.at[2], self.one.at[0], at.first).wait_send()
        push(half, half, self.sum_s.at[1], self.one.at[1], at.sibling).wait_send()
        part = self.full.at[pl.ds(0, 2 * n)]
        push(part, part, self.sum_s.at[0], self.one.at[0], at.second).wait_send()
        for a in range(n):
            for f in range(2):
                slot = a * 2 + f
                ref = self.full.at[0]

                @pl.when(jnp.logical_and(at.has_up, a <= at.a))
                def _():
                    push(ref, ref, self.up_s.at[slot], self.line_r.at[slot], at.up).wait_send()

                @pl.when(jnp.logical_and(at.has_down, a >= at.a))
                def _():
                    push(ref, ref, self.down_s.at[slot], self.line_r.at[slot], at.down).wait_send()


def gather_sems(n):
    dma = pltpu.SemaphoreType.DMA
    return [dma((2 * n,)), dma((2 * n,)), dma((2,)), dma((2 * n,)), dma((2 * n,)), dma((4,))]


def gather_kernel(dp_size, count, *refs):
    shards, fulls, sems = refs[:count], refs[count : 2 * count], refs[2 * count :]
    at = Place(dp_size)
    at.barrier()
    jobs = [Gather(at, shards[i], fulls[i], sems[6 * i : 6 * i + 6]) for i in range(count)]
    for job in jobs:
        job.begin()
    for job in jobs:
        job.after_first()
    for k in range(1, at.lines):
        for g in range(2):
            for job in jobs:
                job.after_line(k, g)
            for job in jobs:
                job.after_second(k - 1, g)
    for g in range(2):
        for job in jobs:
            job.after_second(at.lines - 1, g)
    for job in jobs:
        job.finish()


def gather_all(dp_size, devices, shards, cid=1):
    count = len(shards)
    return pl.pallas_call(
        functools.partial(gather_kernel, dp_size, count),
        out_shape=[jax.ShapeDtypeStruct((devices,) + x.shape, x.dtype) for x in shards],
        in_specs=[pl.BlockSpec(memory_space=pl.ANY)] * count,
        out_specs=[pl.BlockSpec(memory_space=pl.ANY)] * count,
        scratch_shapes=gather_sems(dp_size // 2) * count,
        compiler_params=pltpu.CompilerParams(collective_id=cid, has_side_effects=True),
    )(*shards)


def wide(x):
    return x.astype(jnp.float32)


def add_into(dst, src):
    dst[...] = (wide(dst[...]) + wide(src[...])).astype(dst.dtype)


class Scatter:
    def __init__(self, at, part, out, bufs, sems):
        self.at, self.part, self.out = at, part, out
        self.own, self.sib, self.sec, self.line, self.fst = bufs
        self.one, self.line_s, self.line_r = sems

    def begin(self):
        at = self.at

        def body(j, carry):
            a, f, s = j // 4, lax.rem(j // 2, 2), lax.rem(j, 2)
            push(self.part(at.unit(a, f, s, 1 - at.c)), self.sib.at[j], self.one.at[0], self.one.at[1], at.sibling).start()
            return carry

        lax.fori_loop(0, 4 * at.lines, body, 0)

        def load(j, carry):
            a, f, s = j // 4, lax.rem(j // 2, 2), lax.rem(j, 2)
            pltpu.make_async_copy(self.part(at.unit(a, f, s)), self.own.at[j], self.one.at[2]).start()
            return carry

        lax.fori_loop(0, 4 * at.lines, load, 0)

    def after_sibling(self):
        at = self.at
        n = 2 * at.lines
        pltpu.make_async_copy(self.own, self.own, self.one.at[2]).wait()
        push(self.sib, self.sib, self.one.at[0], self.one.at[1], at.sibling).wait_recv()

        def far(q, carry):
            j = q * 2 + 1 - at.s
            add_into(self.own.at[j], self.sib.at[j])
            return carry

        def send(q, carry):
            push(self.own.at[q * 2 + 1 - at.s], self.sec.at[q], self.one.at[3], self.one.at[4], at.second).start()
            return carry

        def near(q, carry):
            j = q * 2 + at.s
            add_into(self.own.at[j], self.sib.at[j])
            return carry

        lax.fori_loop(0, n, far, 0)
        lax.fori_loop(0, n, send, 0)
        lax.fori_loop(0, n, near, 0)

    def after_second(self):
        at = self.at
        push(self.sec, self.sec, self.one.at[3], self.one.at[4], at.second).wait_recv()

        def body(q, carry):
            add_into(self.own.at[q * 2 + at.s], self.sec.at[q])
            return carry

        lax.fori_loop(0, 2 * at.lines, body, 0)

    def hop(self, low, high, inward, dst, extra):
        at = self.at
        has, who = (at.has_up, at.down) if dst < 0 else (at.has_down, at.up)

        def take(q, carry):
            push(self.line.at[q], self.line.at[q], self.line_s.at[q], self.line_r.at[q], who).wait_recv()
            add_into(self.own.at[q * 2 + at.s], self.line.at[q])
            return carry

        @pl.when(has)
        def _():
            lax.fori_loop(low, high, take, 0)

        def send(q, carry):
            slot = q if dst < 0 else jnp.where(q // 2 == at.a + 1, 2 * at.lines + lax.rem(q, 2), q)
            push(self.own.at[q * 2 + at.s], self.line.at[slot], self.line_s.at[q], self.line_r.at[slot], who).start()
            return carry

        lax.fori_loop(low, high, send, 0)

    def along(self, h):
        at = self.at
        n = at.lines
        hops = n - 1 if n <= 4 else 1

        @pl.when(jnp.logical_and(at.has_down, at.lines - 1 - at.a == h) if hops > 1 else at.has_down)
        def _():
            self.hop(0, 2 * at.a, at.up, -1, None)

        @pl.when(jnp.logical_and(at.has_up, at.a == h) if hops > 1 else at.has_up)
        def _():
            self.hop(2 * at.a + 2, 2 * n, at.down, 1, None)

    def ends(self, f, into):
        at = self.at
        for has, slot in ((at.has_up, 2 * at.a + f), (at.has_down, 2 * at.lines + f)):
            @pl.when(has)
            def _():
                ref = self.line.at[slot]
                push(ref, ref, self.line_s.at[0], self.line_r.at[slot], at.first).wait_recv()
                into[...] = (wide(into[...]) + wide(ref[...])).astype(into.dtype)

    def last_send(self):
        at = self.at
        mine = self.own.at[(2 * at.a + 1 - at.f) * 2 + at.s]
        self.ends(1 - at.f, mine)
        push(mine, self.fst, self.one.at[5], self.one.at[6], at.first).start()
        self.out[...] = wide(self.own[(2 * at.a + at.f) * 2 + at.s])
        self.ends(at.f, self.out)

    def finish(self):
        at = self.at
        push(self.fst, self.fst, self.one.at[5], self.one.at[6], at.first).wait_recv()
        self.out[...] = self.out[...] + wide(self.fst[...])

    def drain(self):
        at = self.at
        n = at.lines
        push(self.sib, self.sib, self.one.at[0], self.one.at[1], at.sibling).wait_send()
        push(self.sec, self.sec, self.one.at[3], self.one.at[4], at.second).wait_send()
        push(self.fst, self.fst, self.one.at[5], self.one.at[6], at.first).wait_send()

        def body(q, carry):
            @pl.when(q // 2 != at.a)
            def _():
                push(self.own.at[q], self.own.at[q], self.line_s.at[q], self.line_r.at[q], at.first).wait_send()
            return carry

        lax.fori_loop(0, 2 * n, body, 0)


def scatter_buffers(n, shape, dtype):
    v = lambda k: pltpu.VMEM((k,) + shape, dtype)
    return [v(4 * n), v(4 * n), v(2 * n), v(2 * n + 2), pltpu.VMEM(shape, dtype)]


def scatter_sems(n):
    dma = pltpu.SemaphoreType.DMA
    return [dma((7,)), dma((2 * n,)), dma((2 * n + 2,))]


def scatter_stages(lines):
    hops = lines - 1 if lines <= 4 else 1
    stages = [Scatter.after_sibling, Scatter.after_second]
    for h in range(hops):
        stages.append(functools.partial(Scatter.along, h=h))
    return stages + [Scatter.last_send, Scatter.finish]


LANES = 128


def window_start(unit, width, features):
    tile = unit * width // LANES
    return (tile - tile // (features // LANES - 1)) * LANES


def whole_part(ref, rows, cols):
    return lambda unit: ref.at[unit, pl.ds(*rows), pl.ds(*cols)]


def window_part(ref, width):
    features = ref.shape[1]
    return lambda unit: ref.at[:, pl.ds(pl.multiple_of(window_start(unit, width, features), LANES), 2 * LANES)]


def cut(shape, cap):
    rows, cols = shape
    pieces = max(1, round(rows * cols / cap))
    while pieces > 1 and not (rows % (16 * pieces) == 0 or cols % (LANES * pieces) == 0):
        pieces -= 1
    if rows % (16 * pieces) == 0:
        step = rows // pieces
        return [((k * step, step), (0, cols)) for k in range(pieces)]
    step = cols // pieces
    return [((0, rows), (k * step, step)) for k in range(pieces)]


def scatter_kernel(dp_size, chunks, count, width, *refs):
    parts, outs, rest = refs[:count], refs[count : 2 * count], refs[2 * count :]
    at = Place(dp_size)
    at.barrier()
    jobs = []
    for k, (i, rows, cols) in enumerate(chunks):
        last = i == count - 1
        part = window_part(parts[i], width) if last else whole_part(parts[i], rows, cols)
        out = outs[i] if last else outs[i].at[pl.ds(*rows), pl.ds(*cols)]
        jobs.append(Scatter(at, part, out, rest[8 * k : 8 * k + 5], rest[8 * k + 5 : 8 * k + 8]))
    for job in jobs:
        job.begin()
    stages = scatter_stages(at.lines)
    total = len(jobs)
    for t in range(total + len(stages) - 1):
        for k, stage in enumerate(stages):
            if 0 <= t - k < total:
                stage(jobs[t - k])
    for job in jobs:
        job.drain()


def scatter_all(dp_size, parts, norm_rows, width, cap=36864, cid=2):
    count = len(parts) + 1
    n = dp_size // 2
    outs = [jax.ShapeDtypeStruct(x.shape[1:], jnp.float32) for x in parts]
    outs.append(jax.ShapeDtypeStruct((norm_rows.shape[0], 2 * LANES), jnp.float32))
    chunks, scratch = [], []
    for i, x in enumerate(parts):
        for rows, cols in cut(x.shape[1:], cap):
            chunks.append((i, rows, cols))
            scratch += scatter_buffers(n, (rows[1], cols[1]), x.dtype) + scatter_sems(n)
    chunks.append((count - 1, None, None))
    scratch += scatter_buffers(n, outs[-1].shape, jnp.float32) + scatter_sems(n)
    return pl.pallas_call(
        functools.partial(scatter_kernel, dp_size, chunks, count, width),
        out_shape=outs,
        in_specs=[pl.BlockSpec(memory_space=pl.ANY)] * count,
        out_specs=[pl.BlockSpec(memory_space=pltpu.VMEM)] * count,
        scratch_shapes=scratch,
        compiler_params=pltpu.CompilerParams(collective_id=cid, has_side_effects=True, vmem_limit_bytes=64000000),
    )(*parts, norm_rows)


def settle_kernel(*refs):
    half = len(refs) // 2
    for src, dst in zip(refs[:half], refs[half:]):
        dst[...] = src[...]


def settle(arrays):
    spec = [pl.BlockSpec(memory_space=pltpu.VMEM)] * len(arrays)
    return pl.pallas_call(
        settle_kernel,
        out_shape=[jax.ShapeDtypeStruct(x.shape, x.dtype) for x in arrays],
        in_specs=spec,
        out_specs=spec,
    )(*arrays)


def with_halo(x, sides, width):
    for axis, dim in sides:
        devices, length = (lax.axis_size(axis), x.shape[dim])
        up = [(i, (i + 1) % devices) for i in range(devices - 1)]
        down = [(j, i) for i, j in up]
        last = lax.slice_in_dim(x, length - width, length, axis=dim)
        first = lax.slice_in_dim(x, 0, width, axis=dim)
        before = lax.ppermute(last, axis, up)
        after = lax.ppermute(first, axis, down)
        x = jnp.concatenate([before, x, after], axis=dim)
    return x


def norm_rows(residual, row_gain, row_bias):
    centered = residual - jnp.mean(residual, axis=-1, keepdims=True)
    spread = jnp.mean(centered * centered, axis=-1, keepdims=True)
    return centered * lax.rsqrt(spread + eps) * row_gain + row_bias


def gelu_exact(pre_act):
    return jax.nn.gelu(pre_act, approximate=False)


def plain_dot(left, right):
    return jnp.dot(left, right, preferred_element_type=jnp.float32)


def grad_dot(left, right):
    return lax.dot_general(
        left, right, (((0,), (0,)), ((), ())), preferred_element_type=jnp.float32
    )


def back_dot(left, right):
    return lax.dot_general(
        left, right, (((1,), (1,)), ((), ())), preferred_element_type=jnp.float32
    )


def squash(x):
    return 0.5 * jnp.tanh(0.5 * x) + 0.5


def slot_onehot(ids, slots, subset):
    cols = lax.broadcasted_iota(jnp.int32, (ids.shape[0], subset), 1)
    hots = [(ids[:, s : s + 1] == cols).astype(jnp.bfloat16) for s in slots]
    return jnp.concatenate(hots, 0)


def gru_embed(ids_ref, table, w_in, emb_ref, gates, chunk=4):
    rows, nchar = ids_ref.shape
    ids = ids_ref[...]
    for k in range(0, nchar, chunk):
        hot = slot_onehot(ids, range(k, k + chunk), table.shape[0])
        emb = plain_dot(hot, table[...]).astype(jnp.bfloat16)
        emb_ref[k : k + chunk] = emb.reshape(chunk, rows, -1)
        for d in range(2):
            gates[d, k : k + chunk] = plain_dot(emb, w_in[d]).reshape(chunk, rows, -1)


def gru_step(d, slot, count, gates, w_rec, state, factor, keep, prior):
    units = state.shape[2]
    old = state[d]
    low = old.astype(jnp.bfloat16)
    rec = plain_dot(low, w_rec[d])
    gi = gates[d, slot]
    reset = squash(gi[:, :units] + rec[:, :units])
    update = squash(gi[:, units : 2 * units] + rec[:, units : 2 * units])
    rec_n = rec[:, 2 * units :]
    cand = jnp.tanh(gi[:, 2 * units :] + reset * rec_n)
    live = slot < count
    state[d] = jnp.where(live, (1.0 - update) * cand + update * old, old)
    by_cand = jnp.where(live, (1.0 - update) * (1.0 - cand * cand), 0.0)
    by_update = jnp.where(live, (old - cand) * update * (1.0 - update), 0.0)
    by_reset = by_cand * rec_n * reset * (1.0 - reset)
    prior[...] = low
    keep[...] = jnp.where(live, update, 1.0)
    for k, x in enumerate((by_reset, by_update, by_cand, reset)):
        factor[:, k * units : (k + 1) * units] = x.astype(factor.dtype)


def gru_forward_kernel(ids_ref, table, w_in, w_rec, vec, emb, f0, f1, z0, z1, h0, h1, gates, state):
    i = pl.program_id(0)
    nchar = pl.num_programs(0)

    @pl.when(i == 0)
    def _():
        gru_embed(ids_ref, table, w_in, emb, gates)
        state[...] = jnp.zeros_like(state)

    count = jnp.sum((ids_ref[...] > 0).astype(jnp.int32), axis=1, keepdims=True)
    gru_step(0, i, count, gates, w_rec, state, f0.at[0], z0.at[0], h0.at[0])
    gru_step(1, nchar - 1 - i, count, gates, w_rec, state, f1.at[0], z1.at[0], h1.at[0])

    @pl.when(i == nchar - 1)
    def _():
        units = state.shape[2]
        vec[:, :units] = state[0].astype(vec.dtype)
        vec[:, units:] = state[1].astype(vec.dtype)


def slot_specs(nchar, rows, cols, backward):
    up = pl.BlockSpec((1, rows, cols), lambda i: (i, 0, 0))
    down = pl.BlockSpec((1, rows, cols), lambda i: (nchar - 1 - i, 0, 0))
    return [down, up] if backward else [up, down]


def gru_forward(ids, table, w_in, w_rec):
    rows, nchar = ids.shape
    width, units = table.shape[1], w_rec.shape[1]
    whole = lambda shape: pl.BlockSpec(shape, lambda i: (0,) * len(shape))
    slots = functools.partial(slot_specs, nchar, rows, backward=False)
    shape = jax.ShapeDtypeStruct
    factor = shape((nchar, rows, 4 * units), jnp.bfloat16)
    keep = shape((nchar, rows, units), jnp.float32)
    prior = shape((nchar, rows, units), jnp.bfloat16)
    return pl.pallas_call(
        gru_forward_kernel,
        grid=(nchar,),
        out_shape=[
            shape((rows, 2 * units), jnp.bfloat16),
            shape((nchar, rows, width), jnp.bfloat16),
            factor, factor, keep, keep, prior, prior,
        ],
        in_specs=[whole(x.shape) for x in (ids, table, w_in, w_rec)],
        out_specs=[whole((rows, 2 * units)), whole((nchar, rows, width))]
        + slots(4 * units) + slots(units) + slots(units),
        scratch_shapes=[
            pltpu.VMEM((2, nchar, rows, 3 * units), jnp.float32),
            pltpu.VMEM((2, rows, units), jnp.float32),
        ],
        compiler_params=pltpu.CompilerParams(vmem_limit_bytes=60000000),
    )(ids, table, w_in, w_rec)


def gru_back_step(d, slot, factor, keep, w_rec, grad, seeds):
    units = grad.shape[2]
    g = grad[d]
    part = lambda k: factor[:, k * units : (k + 1) * units].astype(jnp.float32)
    by_cand = g * part(2)
    seeds[d, slot, :, :units] = (g * part(0)).astype(seeds.dtype)
    seeds[d, slot, :, units : 2 * units] = (g * part(1)).astype(seeds.dtype)
    seeds[d, slot, :, 2 * units : 3 * units] = (by_cand * part(3)).astype(seeds.dtype)
    seeds[d, slot, :, 3 * units :] = by_cand.astype(seeds.dtype)
    grad[d] = g * keep[...] + back_dot(seeds[d, slot, :, : 3 * units], w_rec[d])


def gru_weight_grads(d, seeds, emb, prior, d_in, d_rec):
    _, nchar, rows, wide = seeds.shape
    units = wide // 4
    states = prior[...].reshape(nchar * rows, units)
    chars = emb[...].reshape(nchar * rows, -1)
    col = lambda k: seeds[d, :, :, k * units : (k + 1) * units].reshape(nchar * rows, units)
    for k in range(3):
        d_rec[d, :, k * units : (k + 1) * units] = grad_dot(states, col(k)).astype(d_rec.dtype)
        own = col(3 if k == 2 else k)
        d_in[d, :, k * units : (k + 1) * units] = grad_dot(chars, own).astype(d_in.dtype)


def gru_char_grads(ids_ref, seeds, w_in, d_table, chunk=4):
    _, nchar, rows, wide = seeds.shape
    units = wide // 4
    ids = ids_ref[...]
    total = jnp.zeros(d_table.shape, jnp.float32)
    for k in range(0, nchar, chunk):
        grad = None
        for d in range(2):
            both = seeds[d, k : k + chunk].reshape(chunk * rows, wide)
            part = back_dot(both[:, : 2 * units], w_in[d][:, : 2 * units])
            part = part + back_dot(both[:, 3 * units :], w_in[d][:, 2 * units :])
            grad = part if grad is None else grad + part
        hot = slot_onehot(ids, range(k, k + chunk), d_table.shape[0])
        total = total + grad_dot(hot, grad.astype(jnp.bfloat16))
    d_table[...] = total


def gru_backward_kernel(ids_ref, seed, w_in, w_rec, emb, h0, h1, f0, f1, z0, z1, d_in, d_rec, d_table, grad, seeds):
    i = pl.program_id(0)
    nchar = pl.num_programs(0)

    @pl.when(i == 0)
    def _():
        units = grad.shape[2]
        grad[0] = seed[:, :units]
        grad[1] = seed[:, units:]

    gru_back_step(0, nchar - 1 - i, f0.at[0], z0.at[0], w_rec, grad, seeds)
    gru_back_step(1, i, f1.at[0], z1.at[0], w_rec, grad, seeds)

    @pl.when(i == nchar - 1)
    def _():
        gru_weight_grads(0, seeds, emb, h0, d_in, d_rec)
        gru_weight_grads(1, seeds, emb, h1, d_in, d_rec)
        gru_char_grads(ids_ref, seeds, w_in, d_table)


def gru_backward(ids, seed, w_in, w_rec, emb, h0, h1, f0, f1, z0, z1, subset):
    nchar, rows, width = emb.shape
    units = w_rec.shape[1]
    whole = lambda shape: pl.BlockSpec(shape, lambda i: (0,) * len(shape))
    slots = functools.partial(slot_specs, nchar, rows, backward=True)
    shape = jax.ShapeDtypeStruct
    return pl.pallas_call(
        gru_backward_kernel,
        grid=(nchar,),
        out_shape=[
            shape(w_in.shape, jnp.bfloat16),
            shape(w_rec.shape, jnp.bfloat16),
            shape((subset, width), jnp.float32),
        ],
        in_specs=[whole(x.shape) for x in (ids, seed, w_in, w_rec, emb, h0, h1)] + slots(4 * units) + slots(units),
        out_specs=[whole(w_in.shape), whole(w_rec.shape), whole((subset, width))],
        scratch_shapes=[
            pltpu.VMEM((2, rows, units), jnp.float32),
            pltpu.VMEM((2, nchar, rows, 4 * units), jnp.bfloat16),
        ],
        compiler_params=pltpu.CompilerParams(vmem_limit_bytes=60000000),
    )(ids, seed, w_in, w_rec, emb, h0, h1, f0, f1, z0, z1)


def norm_back(residual, row_gain, seed):
    centered = residual - jnp.mean(residual, axis=-1, keepdims=True)
    spread = jnp.mean(centered * centered, axis=-1, keepdims=True)
    scale = lax.rsqrt(spread + eps)
    unit = centered * scale
    inner = seed * row_gain
    drop = jnp.mean(inner, axis=-1, keepdims=True) + unit * jnp.mean(inner * unit, axis=-1, keepdims=True)
    gain_grad = jnp.sum(seed * unit, axis=0, keepdims=True)
    return scale * (inner - drop), gain_grad, jnp.sum(seed, axis=0, keepdims=True)


def place_norms(gain, bias, index, devices):
    both = jnp.concatenate([gain, bias], 0)
    width = both.shape[1]
    shape = (width, devices * width)
    spot = lax.broadcasted_iota(jnp.int32, shape, 0) + index * width == lax.broadcasted_iota(jnp.int32, shape, 1)
    placed = plain_dot(both, spot.astype(both.dtype)).astype(both.dtype)
    return jnp.pad(placed, ((0, 8 - both.shape[0]), (0, 0)))


def local(
    hidden,
    char_ids,
    groups,
    lengths,
    cotangent,
    qkv_weight,
    out_weight,
    up_weight,
    down_weight,
    norm_gain,
    norm_bias,
    char_table,
    gru_input,
    gru_recur,
    merge_weight,
    conv_weight,
):
    dp_size, devices = lax.axis_size("dp"), lax.axis_size("dp") * lax.axis_size("seq")
    me = lax.axis_index("dp") * lax.axis_size("seq") + lax.axis_index("seq")
    norms = place_norms(norm_gain, norm_bias, me, devices)
    order = (char_table, gru_input, gru_recur, norms, qkv_weight, out_weight, up_weight, down_weight, merge_weight, conv_weight)
    gathered = gather_all(dp_size, devices, order)
    all_norms = jnp.sum(gathered[3].astype(jnp.float32), axis=0)
    (full_table, full_input, full_recur, _, full_qkv, full_out, full_up, full_down, full_merge, full_conv) = [
        x.reshape(-1, x.shape[2]) for x in gathered
    ]
    seq_count, local_len, features = hidden.shape
    nchar = char_ids.shape[2]
    tokens = seq_count * local_len
    head_count = features // HD
    key_span = local_len * lax.axis_size("seq")
    score_scale = 1.0 / math.sqrt(HD)
    gains = [all_norms[k : k + 1] for k in range(3)]
    biases = [all_norms[k : k + 1] for k in range(3, 6)]
    flat_in = hidden.reshape(tokens, features)
    qkv = plain_dot(flat_in, full_qkv).astype(jnp.bfloat16)
    queries = qkv[:, :features].reshape(seq_count, local_len, head_count, HD)
    own_keys = qkv[:, features : 2 * features].reshape(seq_count, local_len, features)
    own_values = qkv[:, 2 * features :].reshape(seq_count, local_len, features)
    all_keys, all_values = (
        lax.all_gather(own_keys, "seq", axis=1, tiled=True),
        lax.all_gather(own_values, "seq", axis=1, tiled=True),
    )
    all_keys = all_keys.reshape(seq_count, key_span, head_count, HD)
    all_values = all_values.reshape(seq_count, key_span, head_count, HD)
    key_valid = jnp.arange(key_span)[None, None, None, :] < lengths[:, None, None, None]

    def score_block():
        raw_scores = (
            jnp.einsum("sqhd,skhd->shqk", queries, all_keys, preferred_element_type=jnp.float32)
            * score_scale
        )
        return jnp.where(key_valid, raw_scores, -1000000000.0)

    scores = score_block()
    log_total = jax.nn.logsumexp(scores, axis=-1, keepdims=True)
    attn_probs = jnp.exp(scores - log_total).astype(jnp.bfloat16)
    attended = jnp.einsum(
        "shqk,skhd->sqhd", attn_probs, all_values, preferred_element_type=jnp.float32
    )
    attended = attended.astype(jnp.bfloat16).reshape(tokens, features)
    resid_one = flat_in.astype(jnp.float32) + plain_dot(attended, full_out)
    norm_one = norm_rows(resid_one, gains[0], biases[0]).astype(jnp.bfloat16)
    up_proj = plain_dot(norm_one, full_up)
    active = gelu_exact(up_proj).astype(jnp.bfloat16)
    resid_two = norm_one.astype(jnp.float32) + plain_dot(active, full_down)
    norm_two = norm_rows(resid_two, gains[1], biases[1]).astype(jnp.bfloat16)
    assert seq_count == 1
    flat_ids = char_ids.reshape(tokens, nchar)
    table_start = groups[0] * SUBV
    own_table = lax.dynamic_slice_in_dim(full_table, table_start, SUBV, 0)
    inward = full_input.reshape(2, -1, full_input.shape[1])
    recurrent = full_recur.reshape(2, -1, full_recur.shape[1])
    char_vec, char_emb, *kept = gru_forward(flat_ids, own_table, inward, recurrent)
    factors, keeps, priors = kept[:2], kept[2:4], kept[4:]
    merge_mats = full_merge.reshape(2, features, features)
    streams = jnp.stack([norm_two, char_vec], 0)
    merged_pair = jnp.einsum("btd,bdf->btf", streams, merge_mats, preferred_element_type=jnp.float32)
    merged_rows = jnp.concatenate([merged_pair[0], merged_pair[1]], -1).astype(jnp.bfloat16)
    padded = with_halo(merged_rows.reshape(seq_count, local_len, 2 * features), (("seq", 1),), 1)
    kernel = full_conv.reshape(3, 2 * features, features)
    windows = [
        padded[:, offset : offset + local_len].reshape(tokens, 2 * features) for offset in range(3)
    ]
    conv_out = (
        plain_dot(windows[0], kernel[0])
        + plain_dot(windows[1], kernel[1])
        + plain_dot(windows[2], kernel[2])
    )
    resid_three = norm_two.astype(jnp.float32) + conv_out
    result = norm_rows(resid_three, gains[2], biases[2]).astype(jnp.bfloat16).reshape(seq_count, local_len, features)
    back_qkv, back_out, back_up, back_down = full_qkv, full_out, full_up, full_down
    back_merge, back_conv = full_merge, full_conv
    merge_back = back_merge.reshape(2, features, features)
    kernel_back = back_conv.reshape(3, 2 * features, features)
    seed_rows = cotangent.reshape(tokens, features).astype(jnp.float32)
    grad_three, gain_three, bias_three = norm_back(resid_three, gains[2], seed_rows)
    conv_seed = grad_three.astype(jnp.bfloat16)
    conv_grad = grad_dot(jnp.concatenate(windows, 1), conv_seed)
    seed_padded = with_halo(conv_seed.reshape(seq_count, local_len, features), (("seq", 1),), 1)
    merged_grad = back_dot(
        seed_padded[:, 2 : 2 + local_len].reshape(tokens, features), kernel_back[0]
    )
    merged_grad = merged_grad + back_dot(
        seed_padded[:, 1 : 1 + local_len].reshape(tokens, features), kernel_back[1]
    )
    merged_grad = merged_grad + back_dot(
        seed_padded[:, 0:local_len].reshape(tokens, features), kernel_back[2]
    )
    merged_grad = merged_grad.astype(jnp.bfloat16)
    pair_grad = jnp.stack([merged_grad[:, :features], merged_grad[:, features:]], 0)
    merge_grad = jnp.einsum("btd,btf->bdf", streams, pair_grad, preferred_element_type=jnp.float32)
    stream_grad = jnp.einsum("btf,bdf->btd", pair_grad, merge_back, preferred_element_type=jnp.float32)
    two_grad = grad_three + stream_grad[0]
    charvec_grad = stream_grad[1]
    grad_two, gain_two, bias_two = norm_back(resid_two, gains[1], two_grad)
    down_seed = grad_two.astype(jnp.bfloat16)
    down_grad = grad_dot(active, down_seed)
    active_grad = back_dot(down_seed, back_down)
    _, pull_gelu = jax.vjp(gelu_exact, up_proj)
    up_seed = pull_gelu(active_grad)[0].astype(jnp.bfloat16)
    up_grad = grad_dot(norm_one, up_seed)
    one_grad = grad_two + back_dot(up_seed, back_up)
    grad_one, gain_one, bias_one = norm_back(resid_one, gains[0], one_grad)
    out_seed = grad_one.astype(jnp.bfloat16)
    out_grad = grad_dot(attended, out_seed)
    attn_seed = (
        back_dot(out_seed, back_out)
        .astype(jnp.bfloat16)
        .reshape(seq_count, local_len, head_count, HD)
    )
    probs_again = jnp.exp(score_block() - log_total)
    probs_grad = jnp.einsum(
        "sqhd,skhd->shqk", attn_seed, all_values, preferred_element_type=jnp.float32
    )
    score_grad = probs_again * (
        probs_grad - jnp.sum(probs_again * probs_grad, axis=-1, keepdims=True)
    )
    score_grad = score_grad.astype(jnp.bfloat16)
    query_grad = (
        jnp.einsum("shqk,skhd->sqhd", score_grad, all_keys, preferred_element_type=jnp.float32)
        * score_scale
    )
    key_grad = (
        jnp.einsum("shqk,sqhd->skhd", score_grad, queries, preferred_element_type=jnp.float32)
        * score_scale
    )
    value_grad = jnp.einsum(
        "shqk,sqhd->skhd",
        probs_again.astype(jnp.bfloat16),
        attn_seed,
        preferred_element_type=jnp.float32,
    )
    key_own, value_own = (
        lax.psum_scatter(
            key_grad.reshape(seq_count, key_span, features).astype(jnp.bfloat16),
            "seq",
            scatter_dimension=1,
            tiled=True,
        ).astype(jnp.float32),
        lax.psum_scatter(
            value_grad.reshape(seq_count, key_span, features).astype(jnp.bfloat16),
            "seq",
            scatter_dimension=1,
            tiled=True,
        ).astype(jnp.float32),
    )
    qkv_seed = jnp.concatenate(
        [
            query_grad.reshape(tokens, features),
            key_own.reshape(tokens, features),
            value_own.reshape(tokens, features),
        ],
        -1,
    ).astype(jnp.bfloat16)
    qkv_grad = grad_dot(flat_in, qkv_seed)
    hidden_grad = (
        (grad_one + back_dot(qkv_seed, back_qkv))
        .astype(jnp.bfloat16)
        .reshape(seq_count, local_len, features)
    )
    input_mats, recur_sum, own_grad = gru_backward(
        flat_ids, charvec_grad, inward, recurrent, char_emb, *priors, *factors, *keeps, SUBV
    )
    table_grad = jnp.zeros(full_table.shape, jnp.bfloat16)
    table_grad = lax.dynamic_update_slice_in_dim(table_grad, own_grad.astype(jnp.bfloat16), table_start, 0)
    norm_grads = jnp.concatenate(
        [gain_one, gain_two, gain_three, bias_one, bias_two, bias_three, jnp.zeros((2, features), jnp.float32)], 0
    )
    terms = [input_mats, recur_sum, merge_grad, conv_grad, down_grad, up_grad, qkv_grad, out_grad, table_grad]
    parts = [x.astype(jnp.bfloat16).reshape(devices, -1, x.shape[-1]) for x in terms]
    width = norm_gain.shape[1]
    *sums, norm_sum = scatter_all(dp_size, parts, norm_grads, width)
    input_total, recur_total, merge_sum, conv_sum, down_sum, up_sum, qkv_sum, out_sum, table_sum = settle(sums)
    skip = me * width - window_start(me, width, features)
    gain_sum = lax.dynamic_slice(norm_sum, (0, skip), (3, width))
    bias_sum = lax.dynamic_slice(norm_sum, (3, skip), (3, width))
    return (result, hidden_grad, qkv_sum, out_sum, up_sum, down_sum, gain_sum, bias_sum, table_sum, input_total, recur_total, merge_sum, conv_sum)


def solution(mesh):
    placed = (
        P("dp", "seq", None),
        P("dp", "seq", None),
        P("dp"),
        P("dp"),
        P("dp", "seq", None),
        P(("dp", "seq"), None),
        P(("dp", "seq"), None),
        P(("dp", "seq"), None),
        P(("dp", "seq"), None),
        P(None, ("dp", "seq")),
        P(None, ("dp", "seq")),
        P(("dp", "seq"), None),
        P(("dp", "seq"), None),
        P(("dp", "seq"), None),
        P(("dp", "seq"), None),
        P(("dp", "seq"), None),
    )
    return jax.shard_map(
        local,
        mesh=mesh,
        in_specs=placed,
        out_specs=(
            P("dp", "seq", None),
            P("dp", "seq", None),
            P(("dp", "seq"), None),
            P(("dp", "seq"), None),
            P(("dp", "seq"), None),
            P(("dp", "seq"), None),
            P(None, ("dp", "seq")),
            P(None, ("dp", "seq")),
            P(("dp", "seq"), None),
            P(("dp", "seq"), None),
            P(("dp", "seq"), None),
            P(("dp", "seq"), None),
            P(("dp", "seq"), None),
        ),
        check_vma=False,
    )
```

```python
import functools
import math

import jax
import jax.numpy as jnp
from jax import lax
from jax.experimental import pallas as pl
from jax.experimental.pallas import tpu as pltpu
from jax.sharding import PartitionSpec as P

MESH = pl.DeviceIdType.MESH

HD = 64
SUBV = 128

eps = 1e-05

class Place:
    def __init__(self, dp_size):
        dp, seq = lax.axis_index("dp"), lax.axis_index("seq")
        self.lines = dp_size // 2
        self.a, self.b = dp // 2, lax.rem(dp, 2)
        self.y, self.c = seq // 2, lax.rem(seq, 2)
        flip_b = (self.a * 2 + 1 - self.b, seq)
        flip_y = (dp, (1 - self.y) * 2 + self.c)
        pick = lambda u, v: tuple(i + self.c * (j - i) for i, j in zip(u, v))
        self.first, self.second = pick(flip_b, flip_y), pick(flip_y, flip_b)
        self.sibling = (dp, self.y * 2 + 1 - self.c)
        self.up, self.down = (dp + 2, seq), (dp - 2, seq)
        self.f = self.b + self.c * (self.y - self.b)
        self.s = self.y + self.c * (self.b - self.y)
        self.has_up, self.has_down = self.a < self.lines - 1, self.a > 0

    def unit(self, a, f, s, c=None):
        c = self.c if c is None else c
        return a * 8 + f * (4 - 2 * c) + s * (2 + 2 * c) + c

    def barrier(self):
        sem = pltpu.get_barrier_semaphore()
        for who in (self.first, self.second, self.sibling):
            pl.semaphore_signal(sem, inc=1, device_id=who, device_id_type=MESH)

        @pl.when(self.has_up)
        def _():
            pl.semaphore_signal(sem, inc=1, device_id=self.up, device_id_type=MESH)

        @pl.when(self.has_down)
        def _():
            pl.semaphore_signal(sem, inc=1, device_id=self.down, device_id_type=MESH)

        pl.semaphore_wait(sem, 3 + self.has_up.astype(jnp.int32) + self.has_down.astype(jnp.int32))


def push(src, dst, send, recv, who):
    return pltpu.make_async_remote_copy(
        src_ref=src, dst_ref=dst, send_sem=send, recv_sem=recv, device_id=who, device_id_type=MESH
    )


class Gather:
    def __init__(self, at, shard, full, sems):
        self.at, self.shard, self.full = at, shard, full
        self.up_s, self.down_s, self.sum_s, self.line_r, self.second_r, self.one = sems

    def to_lines(self, src, slot, index, up, down):
        at = self.at
        if up is not False:
            @pl.when(at.has_up if up is True else jnp.logical_and(up, at.has_up))
            def _():
                push(src, self.full.at[index], self.up_s.at[slot], self.line_r.at[slot], at.up).start()
        if down is not False:
            @pl.when(at.has_down if down is True else jnp.logical_and(down, at.has_down))
            def _():
                push(src, self.full.at[index], self.down_s.at[slot], self.line_r.at[slot], at.down).start()

    def across(self, src, slot, index):
        push(src, self.full.at[index], self.sum_s.at[0], self.second_r.at[slot], self.at.second).start()
        self.aside(src, index)

    def aside(self, src, index):
        push(src, self.full.at[index], self.sum_s.at[1], self.one.at[1], self.at.sibling).start()

    def begin(self):
        at = self.at
        me = at.unit(at.a, at.f, at.s)
        pltpu.make_async_copy(self.shard, self.full.at[me], self.one.at[3]).start()
        push(self.shard, self.full.at[me], self.one.at[2], self.one.at[0], at.first).start()
        slot = at.a * 2 + at.f
        self.to_lines(self.shard, slot, me, True, True)
        self.across(self.shard, slot, me)

    def after_first(self):
        at = self.at
        index = at.unit(at.a, 1 - at.f, at.s)
        ref = self.full.at[index]
        push(ref, ref, self.one.at[2], self.one.at[0], at.first).wait_recv()
        slot = at.a * 2 + 1 - at.f
        self.to_lines(ref, slot, index, True, True)
        self.across(ref, slot, index)

    def after_line(self, k, g):
        at = self.at
        for sign in (-1, 1):
            a = at.a + sign * k
            f = at.f if g == 0 else 1 - at.f

            @pl.when(a >= 0 if sign < 0 else a < at.lines)
            def _():
                index, slot = at.unit(a, f, at.s), a * 2 + f
                ref = self.full.at[index]
                push(ref, ref, self.up_s.at[slot], self.line_r.at[slot], at.up).wait_recv()
                self.to_lines(ref, slot, index, sign < 0, sign > 0)
                self.across(ref, slot, index)

    def after_second(self, k, g):
        at = self.at
        for sign in (-1, 1) if k else (1,):
            a = at.a + sign * k
            f = at.f if g == 0 else 1 - at.f

            @pl.when(a >= 0 if sign < 0 else a < at.lines)
            def _():
                index, slot = at.unit(a, f, 1 - at.s), a * 2 + f
                ref = self.full.at[index]
                push(ref, ref, self.sum_s.at[0], self.second_r.at[slot], at.second).wait_recv()
                self.aside(ref, index)

    def finish(self):
        at, n = self.at, self.at.lines
        me = at.unit(at.a, at.f, at.s)
        half = self.full.at[pl.ds(0, 4 * n)]
        push(half, half, self.sum_s.at[1], self.one.at[1], at.sibling).wait_recv()
        pltpu.make_async_copy(self.shard, self.full.at[me], self.one.at[3]).wait()
        push(self.shard, self.full.at[me], self.one.at[2], self.one.at[0], at.first).wait_send()
        push(half, half, self.sum_s.at[1], self.one.at[1], at.sibling).wait_send()
        part = self.full.at[pl.ds(0, 2 * n)]
        push(part, part, self.sum_s.at[0], self.one.at[0], at.second).wait_send()
        for a in range(n):
            for f in range(2):
                slot = a * 2 + f
                ref = self.full.at[0]

                @pl.when(jnp.logical_and(at.has_up, a <= at.a))
                def _():
                    push(ref, ref, self.up_s.at[slot], self.line_r.at[slot], at.up).wait_send()

                @pl.when(jnp.logical_and(at.has_down, a >= at.a))
                def _():
                    push(ref, ref, self.down_s.at[slot], self.line_r.at[slot], at.down).wait_send()


def gather_sems(n):
    dma = pltpu.SemaphoreType.DMA
    return [dma((2 * n,)), dma((2 * n,)), dma((2,)), dma((2 * n,)), dma((2 * n,)), dma((4,))]


def gather_kernel(dp_size, count, *refs):
    shards, fulls, sems = refs[:count], refs[count : 2 * count], refs[2 * count :]
    at = Place(dp_size)
    at.barrier()
    jobs = [Gather(at, shards[i], fulls[i], sems[6 * i : 6 * i + 6]) for i in range(count)]
    for job in jobs:
        job.begin()
    for job in jobs:
        job.after_first()
    for k in range(1, at.lines):
        for g in range(2):
            for job in jobs:
                job.after_line(k, g)
            for job in jobs:
                job.after_second(k - 1, g)
    for g in range(2):
        for job in jobs:
            job.after_second(at.lines - 1, g)
    for job in jobs:
        job.finish()


def gather_all(dp_size, devices, shards, cid=1):
    count = len(shards)
    return pl.pallas_call(
        functools.partial(gather_kernel, dp_size, count),
        out_shape=[jax.ShapeDtypeStruct((devices,) + x.shape, x.dtype) for x in shards],
        in_specs=[pl.BlockSpec(memory_space=pl.ANY)] * count,
        out_specs=[pl.BlockSpec(memory_space=pl.ANY)] * count,
        scratch_shapes=gather_sems(dp_size // 2) * count,
        compiler_params=pltpu.CompilerParams(collective_id=cid, has_side_effects=True),
    )(*shards)


def wide(x):
    return x.astype(jnp.float32)


def add_into(dst, src):
    dst[...] = (wide(dst[...]) + wide(src[...])).astype(dst.dtype)


class Scatter:
    def __init__(self, at, part, out, bufs, sems):
        self.at, self.part, self.out = at, part, out
        self.own, self.sib, self.sec, self.line, self.fst = bufs
        self.one, self.line_s, self.line_r = sems

    def begin(self):
        at = self.at

        def body(j, carry):
            a, f, s = j // 4, lax.rem(j // 2, 2), lax.rem(j, 2)
            push(self.part(at.unit(a, f, s, 1 - at.c)), self.sib.at[j], self.one.at[0], self.one.at[1], at.sibling).start()
            return carry

        lax.fori_loop(0, 4 * at.lines, body, 0)

        def load(j, carry):
            a, f, s = j // 4, lax.rem(j // 2, 2), lax.rem(j, 2)
            pltpu.make_async_copy(self.part(at.unit(a, f, s)), self.own.at[j], self.one.at[2]).start()
            return carry

        lax.fori_loop(0, 4 * at.lines, load, 0)

    def after_sibling(self):
        at = self.at
        n = 2 * at.lines
        pltpu.make_async_copy(self.own, self.own, self.one.at[2]).wait()
        push(self.sib, self.sib, self.one.at[0], self.one.at[1], at.sibling).wait_recv()

        def far(q, carry):
            j = q * 2 + 1 - at.s
            add_into(self.own.at[j], self.sib.at[j])
            return carry

        def send(q, carry):
            push(self.own.at[q * 2 + 1 - at.s], self.sec.at[q], self.one.at[3], self.one.at[4], at.second).start()
            return carry

        def near(q, carry):
            j = q * 2 + at.s
            add_into(self.own.at[j], self.sib.at[j])
            return carry

        lax.fori_loop(0, n, far, 0)
        lax.fori_loop(0, n, send, 0)
        lax.fori_loop(0, n, near, 0)

    def after_second(self):
        at = self.at
        push(self.sec, self.sec, self.one.at[3], self.one.at[4], at.second).wait_recv()

        def body(q, carry):
            add_into(self.own.at[q * 2 + at.s], self.sec.at[q])
            return carry

        lax.fori_loop(0, 2 * at.lines, body, 0)

    def hop(self, low, high, inward, dst, extra):
        at = self.at
        has, who = (at.has_up, at.down) if dst < 0 else (at.has_down, at.up)

        def take(q, carry):
            push(self.line.at[q], self.line.at[q], self.line_s.at[q], self.line_r.at[q], who).wait_recv()
            add_into(self.own.at[q * 2 + at.s], self.line.at[q])
            return carry

        @pl.when(has)
        def _():
            lax.fori_loop(low, high, take, 0)

        def send(q, carry):
            slot = q if dst < 0 else jnp.where(q // 2 == at.a + 1, 2 * at.lines + lax.rem(q, 2), q)
            push(self.own.at[q * 2 + at.s], self.line.at[slot], self.line_s.at[q], self.line_r.at[slot], who).start()
            return carry

        lax.fori_loop(low, high, send, 0)

    def along(self, h):
        at = self.at
        n = at.lines
        hops = n - 1 if n <= 4 else 1

        @pl.when(jnp.logical_and(at.has_down, at.lines - 1 - at.a == h) if hops > 1 else at.has_down)
        def _():
            self.hop(0, 2 * at.a, at.up, -1, None)

        @pl.when(jnp.logical_and(at.has_up, at.a == h) if hops > 1 else at.has_up)
        def _():
            self.hop(2 * at.a + 2, 2 * n, at.down, 1, None)

    def ends(self, f, into):
        at = self.at
        for has, slot in ((at.has_up, 2 * at.a + f), (at.has_down, 2 * at.lines + f)):
            @pl.when(has)
            def _():
                ref = self.line.at[slot]
                push(ref, ref, self.line_s.at[0], self.line_r.at[slot], at.first).wait_recv()
                into[...] = (wide(into[...]) + wide(ref[...])).astype(into.dtype)

    def last_send(self):
        at = self.at
        mine = self.own.at[(2 * at.a + 1 - at.f) * 2 + at.s]
        self.ends(1 - at.f, mine)
        push(mine, self.fst, self.one.at[5], self.one.at[6], at.first).start()
        self.out[...] = wide(self.own[(2 * at.a + at.f) * 2 + at.s])
        self.ends(at.f, self.out)

    def finish(self):
        at = self.at
        push(self.fst, self.fst, self.one.at[5], self.one.at[6], at.first).wait_recv()
        self.out[...] = self.out[...] + wide(self.fst[...])

    def drain(self):
        at = self.at
        n = at.lines
        push(self.sib, self.sib, self.one.at[0], self.one.at[1], at.sibling).wait_send()
        push(self.sec, self.sec, self.one.at[3], self.one.at[4], at.second).wait_send()
        push(self.fst, self.fst, self.one.at[5], self.one.at[6], at.first).wait_send()

        def body(q, carry):
            @pl.when(q // 2 != at.a)
            def _():
                push(self.own.at[q], self.own.at[q], self.line_s.at[q], self.line_r.at[q], at.first).wait_send()
            return carry

        lax.fori_loop(0, 2 * n, body, 0)


def scatter_buffers(n, shape, dtype):
    v = lambda k: pltpu.VMEM((k,) + shape, dtype)
    return [v(4 * n), v(4 * n), v(2 * n), v(2 * n + 2), pltpu.VMEM(shape, dtype)]


def scatter_sems(n):
    dma = pltpu.SemaphoreType.DMA
    return [dma((7,)), dma((2 * n,)), dma((2 * n + 2,))]


def scatter_stages(lines):
    hops = lines - 1 if lines <= 4 else 1
    stages = [Scatter.after_sibling, Scatter.after_second]
    for h in range(hops):
        stages.append(functools.partial(Scatter.along, h=h))
    return stages + [Scatter.last_send, Scatter.finish]


LANES = 128


def window_start(unit, width, features):
    tile = unit * width // LANES
    return (tile - tile // (features // LANES - 1)) * LANES


def whole_part(ref, rows, cols):
    return lambda unit: ref.at[unit, pl.ds(*rows), pl.ds(*cols)]


def window_part(ref, width):
    features = ref.shape[1]
    return lambda unit: ref.at[:, pl.ds(pl.multiple_of(window_start(unit, width, features), LANES), 2 * LANES)]


def cut(shape, cap):
    rows, cols = shape
    pieces = max(1, round(rows * cols / cap))
    while pieces > 1 and not (rows % (16 * pieces) == 0 or cols % (LANES * pieces) == 0):
        pieces -= 1
    if rows % (16 * pieces) == 0:
        step = rows // pieces
        return [((k * step, step), (0, cols)) for k in range(pieces)]
    step = cols // pieces
    return [((0, rows), (k * step, step)) for k in range(pieces)]


def scatter_kernel(dp_size, chunks, count, width, *refs):
    parts, outs, rest = refs[:count], refs[count : 2 * count], refs[2 * count :]
    at = Place(dp_size)
    at.barrier()
    jobs = []
    for k, (i, rows, cols) in enumerate(chunks):
        last = i == count - 1
        part = window_part(parts[i], width) if last else whole_part(parts[i], rows, cols)
        out = outs[i] if last else outs[i].at[pl.ds(*rows), pl.ds(*cols)]
        jobs.append(Scatter(at, part, out, rest[8 * k : 8 * k + 5], rest[8 * k + 5 : 8 * k + 8]))
    for job in jobs:
        job.begin()
    stages = scatter_stages(at.lines)
    total = len(jobs)
    for t in range(total + len(stages) - 1):
        for k, stage in enumerate(stages):
            if 0 <= t - k < total:
                stage(jobs[t - k])
    for job in jobs:
        job.drain()


def scatter_all(dp_size, parts, norm_rows, width, cap=36864, cid=2):
    count = len(parts) + 1
    n = dp_size // 2
    outs = [jax.ShapeDtypeStruct(x.shape[1:], jnp.float32) for x in parts]
    outs.append(jax.ShapeDtypeStruct((norm_rows.shape[0], 2 * LANES), jnp.float32))
    chunks, scratch = [], []
    for i, x in enumerate(parts):
        for rows, cols in cut(x.shape[1:], cap):
            chunks.append((i, rows, cols))
            scratch += scatter_buffers(n, (rows[1], cols[1]), x.dtype) + scatter_sems(n)
    chunks.append((count - 1, None, None))
    scratch += scatter_buffers(n, outs[-1].shape, jnp.float32) + scatter_sems(n)
    return pl.pallas_call(
        functools.partial(scatter_kernel, dp_size, chunks, count, width),
        out_shape=outs,
        in_specs=[pl.BlockSpec(memory_space=pl.ANY)] * count,
        out_specs=[pl.BlockSpec(memory_space=pltpu.VMEM)] * count,
        scratch_shapes=scratch,
        compiler_params=pltpu.CompilerParams(collective_id=cid, has_side_effects=True, vmem_limit_bytes=64000000),
    )(*parts, norm_rows)


def settle_kernel(*refs):
    half = len(refs) // 2
    for src, dst in zip(refs[:half], refs[half:]):
        dst[...] = src[...]


def settle(arrays):
    spec = [pl.BlockSpec(memory_space=pltpu.VMEM)] * len(arrays)
    return pl.pallas_call(
        settle_kernel,
        out_shape=[jax.ShapeDtypeStruct(x.shape, x.dtype) for x in arrays],
        in_specs=spec,
        out_specs=spec,
    )(*arrays)


def with_halo(x, sides, width):
    for axis, dim in sides:
        devices, length = (lax.axis_size(axis), x.shape[dim])
        up = [(i, (i + 1) % devices) for i in range(devices - 1)]
        down = [(j, i) for i, j in up]
        last = lax.slice_in_dim(x, length - width, length, axis=dim)
        first = lax.slice_in_dim(x, 0, width, axis=dim)
        before = lax.ppermute(last, axis, up)
        after = lax.ppermute(first, axis, down)
        x = jnp.concatenate([before, x, after], axis=dim)
    return x


def norm_rows(residual, row_gain, row_bias):
    centered = residual - jnp.mean(residual, axis=-1, keepdims=True)
    spread = jnp.mean(centered * centered, axis=-1, keepdims=True)
    return centered * lax.rsqrt(spread + eps) * row_gain + row_bias


def gelu_exact(pre_act):
    return jax.nn.gelu(pre_act, approximate=False)


def plain_dot(left, right):
    return jnp.dot(left, right, preferred_element_type=jnp.float32)


def grad_dot(left, right):
    return lax.dot_general(
        left, right, (((0,), (0,)), ((), ())), preferred_element_type=jnp.float32
    )


def back_dot(left, right):
    return lax.dot_general(
        left, right, (((1,), (1,)), ((), ())), preferred_element_type=jnp.float32
    )


def squash(x):
    return 0.5 * jnp.tanh(0.5 * x) + 0.5


def slot_onehot(ids, slots, subset):
    cols = lax.broadcasted_iota(jnp.int32, (ids.shape[0], subset), 1)
    hots = [(ids[:, s : s + 1] == cols).astype(jnp.bfloat16) for s in slots]
    return jnp.concatenate(hots, 0)


def gru_embed(ids_ref, table, w_in, emb_ref, gates, chunk=4):
    rows, nchar = ids_ref.shape
    ids = ids_ref[...]
    for k in range(0, nchar, chunk):
        hot = slot_onehot(ids, range(k, k + chunk), table.shape[0])
        emb = plain_dot(hot, table[...]).astype(jnp.bfloat16)
        emb_ref[k : k + chunk] = emb.reshape(chunk, rows, -1)
        for d in range(2):
            gates[d, k : k + chunk] = plain_dot(emb, w_in[d]).reshape(chunk, rows, -1)


def gru_step(d, slot, count, gates, w_rec, state, factor, keep, prior):
    units = state.shape[2]
    old = state[d]
    low = old.astype(jnp.bfloat16)
    rec = plain_dot(low, w_rec[d])
    gi = gates[d, slot]
    reset = squash(gi[:, :units] + rec[:, :units])
    update = squash(gi[:, units : 2 * units] + rec[:, units : 2 * units])
    rec_n = rec[:, 2 * units :]
    cand = jnp.tanh(gi[:, 2 * units :] + reset * rec_n)
    live = slot < count
    state[d] = jnp.where(live, (1.0 - update) * cand + update * old, old)
    by_cand = jnp.where(live, (1.0 - update) * (1.0 - cand * cand), 0.0)
    by_update = jnp.where(live, (old - cand) * update * (1.0 - update), 0.0)
    by_reset = by_cand * rec_n * reset * (1.0 - reset)
    prior[...] = low
    keep[...] = jnp.where(live, update, 1.0)
    for k, x in enumerate((by_reset, by_update, by_cand, reset)):
        factor[:, k * units : (k + 1) * units] = x.astype(factor.dtype)


def gru_forward_kernel(ids_ref, table, w_in, w_rec, vec, emb, f0, f1, z0, z1, h0, h1, gates, state):
    i = pl.program_id(0)
    nchar = pl.num_programs(0)

    @pl.when(i == 0)
    def _():
        gru_embed(ids_ref, table, w_in, emb, gates)
        state[...] = jnp.zeros_like(state)

    count = jnp.sum((ids_ref[...] > 0).astype(jnp.int32), axis=1, keepdims=True)
    gru_step(0, i, count, gates, w_rec, state, f0.at[0], z0.at[0], h0.at[0])
    gru_step(1, nchar - 1 - i, count, gates, w_rec, state, f1.at[0], z1.at[0], h1.at[0])

    @pl.when(i == nchar - 1)
    def _():
        units = state.shape[2]
        vec[:, :units] = state[0].astype(vec.dtype)
        vec[:, units:] = state[1].astype(vec.dtype)


def slot_specs(nchar, rows, cols, backward):
    up = pl.BlockSpec((1, rows, cols), lambda i: (i, 0, 0))
    down = pl.BlockSpec((1, rows, cols), lambda i: (nchar - 1 - i, 0, 0))
    return [down, up] if backward else [up, down]


def gru_cost(nchar, rows, width, units, products):
    steps = 2 * nchar * rows
    return pl.CostEstimate(
        flops=12 * products * steps * (width + units) * units,
        bytes_accessed=16 * steps * units,
        transcendentals=3 * steps * units,
    )


def gru_forward(ids, table, w_in, w_rec):
    rows, nchar = ids.shape
    width, units = table.shape[1], w_rec.shape[1]
    whole = lambda shape: pl.BlockSpec(shape, lambda i: (0,) * len(shape))
    slots = functools.partial(slot_specs, nchar, rows, backward=False)
    shape = jax.ShapeDtypeStruct
    factor = shape((nchar, rows, 4 * units), jnp.bfloat16)
    keep = shape((nchar, rows, units), jnp.float32)
    prior = shape((nchar, rows, units), jnp.bfloat16)
    return pl.pallas_call(
        gru_forward_kernel,
        grid=(nchar,),
        out_shape=[
            shape((rows, 2 * units), jnp.bfloat16),
            shape((nchar, rows, width), jnp.bfloat16),
            factor, factor, keep, keep, prior, prior,
        ],
        in_specs=[whole(x.shape) for x in (ids, table, w_in, w_rec)],
        out_specs=[whole((rows, 2 * units)), whole((nchar, rows, width))]
        + slots(4 * units) + slots(units) + slots(units),
        scratch_shapes=[
            pltpu.VMEM((2, nchar, rows, 3 * units), jnp.float32),
            pltpu.VMEM((2, rows, units), jnp.float32),
        ],
        compiler_params=pltpu.CompilerParams(vmem_limit_bytes=60000000),
        cost_estimate=gru_cost(nchar, rows, width, units, 1),
    )(ids, table, w_in, w_rec)


def gru_back_step(d, slot, factor, keep, w_rec, grad, seeds):
    units = grad.shape[2]
    g = grad[d]
    part = lambda k: factor[:, k * units : (k + 1) * units].astype(jnp.float32)
    by_cand = g * part(2)
    seeds[d, slot, :, :units] = (g * part(0)).astype(seeds.dtype)
    seeds[d, slot, :, units : 2 * units] = (g * part(1)).astype(seeds.dtype)
    seeds[d, slot, :, 2 * units : 3 * units] = (by_cand * part(3)).astype(seeds.dtype)
    seeds[d, slot, :, 3 * units :] = by_cand.astype(seeds.dtype)
    grad[d] = g * keep[...] + back_dot(seeds[d, slot, :, : 3 * units], w_rec[d])


def gru_weight_grads(d, seeds, emb, prior, d_in, d_rec):
    _, nchar, rows, wide = seeds.shape
    units = wide // 4
    states = prior[...].reshape(nchar * rows, units)
    chars = emb[...].reshape(nchar * rows, -1)
    col = lambda k: seeds[d, :, :, k * units : (k + 1) * units].reshape(nchar * rows, units)
    for k in range(3):
        d_rec[d, :, k * units : (k + 1) * units] = grad_dot(states, col(k)).astype(d_rec.dtype)
        own = col(3 if k == 2 else k)
        d_in[d, :, k * units : (k + 1) * units] = grad_dot(chars, own).astype(d_in.dtype)


def gru_char_grads(ids_ref, seeds, w_in, d_table, chunk=4):
    _, nchar, rows, wide = seeds.shape
    units = wide // 4
    ids = ids_ref[...]
    total = jnp.zeros(d_table.shape, jnp.float32)
    for k in range(0, nchar, chunk):
        grad = None
        for d in range(2):
            both = seeds[d, k : k + chunk].reshape(chunk * rows, wide)
            part = back_dot(both[:, : 2 * units], w_in[d][:, : 2 * units])
            part = part + back_dot(both[:, 3 * units :], w_in[d][:, 2 * units :])
            grad = part if grad is None else grad + part
        hot = slot_onehot(ids, range(k, k + chunk), d_table.shape[0])
        total = total + grad_dot(hot, grad.astype(jnp.bfloat16))
    d_table[...] = total


def gru_backward_kernel(ids_ref, seed, w_in, w_rec, emb, h0, h1, f0, f1, z0, z1, d_in, d_rec, d_table, grad, seeds):
    i = pl.program_id(0)
    nchar = pl.num_programs(0)

    @pl.when(i == 0)
    def _():
        units = grad.shape[2]
        grad[0] = seed[:, :units]
        grad[1] = seed[:, units:]

    gru_back_step(0, nchar - 1 - i, f0.at[0], z0.at[0], w_rec, grad, seeds)
    gru_back_step(1, i, f1.at[0], z1.at[0], w_rec, grad, seeds)

    @pl.when(i == nchar - 1)
    def _():
        gru_weight_grads(0, seeds, emb, h0, d_in, d_rec)
        gru_weight_grads(1, seeds, emb, h1, d_in, d_rec)
        gru_char_grads(ids_ref, seeds, w_in, d_table)


def gru_backward(ids, seed, w_in, w_rec, emb, h0, h1, f0, f1, z0, z1, subset):
    nchar, rows, width = emb.shape
    units = w_rec.shape[1]
    whole = lambda shape: pl.BlockSpec(shape, lambda i: (0,) * len(shape))
    slots = functools.partial(slot_specs, nchar, rows, backward=True)
    shape = jax.ShapeDtypeStruct
    return pl.pallas_call(
        gru_backward_kernel,
        grid=(nchar,),
        out_shape=[
            shape(w_in.shape, jnp.bfloat16),
            shape(w_rec.shape, jnp.bfloat16),
            shape((subset, width), jnp.float32),
        ],
        in_specs=[whole(x.shape) for x in (ids, seed, w_in, w_rec, emb, h0, h1)] + slots(4 * units) + slots(units),
        out_specs=[whole(w_in.shape), whole(w_rec.shape), whole((subset, width))],
        scratch_shapes=[
            pltpu.VMEM((2, rows, units), jnp.float32),
            pltpu.VMEM((2, nchar, rows, 4 * units), jnp.bfloat16),
        ],
        compiler_params=pltpu.CompilerParams(vmem_limit_bytes=60000000),
        cost_estimate=gru_cost(nchar, rows, width, units, 2),
    )(ids, seed, w_in, w_rec, emb, h0, h1, f0, f1, z0, z1)


def head_pair(q_ref, blocks, valid, pair, half):
    features = q_ref.shape[1]
    cols = pl.ds(pair * 2 * HD, 2 * HD)
    queries = q_ref[:, cols]
    keys = jnp.concatenate([b[:, cols] for b in blocks], 0)
    values = jnp.concatenate([b[:, pl.ds(features + pair * 2 * HD, 2 * HD)] for b in blocks], 0)
    scores = back_dot(one_head(queries, half), keys) * (1.0 / math.sqrt(HD))
    scores = jnp.where(valid, scores, -1000000000.0)
    weight = jnp.exp(scores - jnp.max(scores, axis=-1, keepdims=True))
    return weight / jnp.sum(weight, axis=-1, keepdims=True), queries, keys, values


def first_lanes(shape):
    return lax.broadcasted_iota(jnp.int32, shape, 1) < HD


def one_head(x, half):
    keep = first_lanes(x.shape) if half == 0 else jnp.logical_not(first_lanes(x.shape))
    return jnp.where(keep, x, jnp.zeros_like(x))


def side_by_side(left, right):
    return jnp.where(first_lanes(left.shape), left, right)


def attention_kernel(count, q_ref, valid_ref, *refs):
    blocks, out = refs[:count], refs[count]
    valid = jnp.broadcast_to(valid_ref[...] > 0, (q_ref.shape[0], valid_ref.shape[1]))
    for pair in range(q_ref.shape[1] // (2 * HD)):
        both = []
        for half in range(2):
            probs, _, _, values = head_pair(q_ref, blocks, valid, pair, half)
            both.append(plain_dot(probs.astype(jnp.bfloat16), values))
        out[:, pl.ds(pair * 2 * HD, 2 * HD)] = side_by_side(*both).astype(out.dtype)


def attention_back_kernel(count, q_ref, valid_ref, seed_ref, *refs):
    blocks, q_out, outs = refs[:count], refs[count], refs[count + 1 :]
    rows, features = q_ref.shape
    scale = 1.0 / math.sqrt(HD)
    valid = jnp.broadcast_to(valid_ref[...] > 0, (rows, valid_ref.shape[1]))
    for pair in range(features // (2 * HD)):
        cols = pl.ds(pair * 2 * HD, 2 * HD)
        seed = seed_ref[:, cols]
        q_both, k_both, v_both = [], [], []
        for half in range(2):
            probs, queries, keys, values = head_pair(q_ref, blocks, valid, pair, half)
            probs_grad = back_dot(one_head(seed, half), values)
            inner = jnp.sum(probs * probs_grad, axis=-1, keepdims=True)
            score_grad = (probs * (probs_grad - inner)).astype(jnp.bfloat16)
            q_both.append(plain_dot(score_grad, keys))
            k_both.append(grad_dot(score_grad, queries))
            v_both.append(grad_dot(probs.astype(jnp.bfloat16), seed))
        q_out[:, cols] = (side_by_side(*q_both) * scale).astype(q_out.dtype)
        k_grad = (side_by_side(*k_both) * scale).astype(jnp.bfloat16)
        v_grad = side_by_side(*v_both).astype(jnp.bfloat16)
        for j, out in enumerate(outs):
            out[:, cols] = k_grad[j * rows : (j + 1) * rows]
            out[:, pl.ds(features + pair * 2 * HD, 2 * HD)] = v_grad[j * rows : (j + 1) * rows]


def attention_cost(rows, blocks, features, products):
    span = rows * len(blocks)
    return pl.CostEstimate(
        flops=2 * products * rows * span * features,
        bytes_accessed=8 * span * features,
        transcendentals=rows * span * (features // HD),
    )


def attention(queries, valid, blocks):
    rows, features = queries.shape
    vmem = pl.BlockSpec(memory_space=pltpu.VMEM)
    return pl.pallas_call(
        functools.partial(attention_kernel, len(blocks)),
        out_shape=jax.ShapeDtypeStruct((rows, features), jnp.bfloat16),
        in_specs=[vmem] * (2 + len(blocks)),
        out_specs=vmem,
        cost_estimate=attention_cost(rows, blocks, features, 2),
    )(queries, valid, *blocks)


def attention_back(queries, valid, seed, blocks):
    rows, features = queries.shape
    vmem = pl.BlockSpec(memory_space=pltpu.VMEM)
    return pl.pallas_call(
        functools.partial(attention_back_kernel, len(blocks)),
        out_shape=[jax.ShapeDtypeStruct((rows, features), jnp.bfloat16)]
        + [jax.ShapeDtypeStruct((rows, 2 * features), jnp.bfloat16)] * len(blocks),
        in_specs=[vmem] * (3 + len(blocks)),
        out_specs=[vmem] * (1 + len(blocks)),
        cost_estimate=attention_cost(rows, blocks, features, 5),
    )(queries, valid, seed, *blocks)


def from_next(x, axis, step):
    size = lax.axis_size(axis)
    return lax.ppermute(x, axis, [((i + step) % size, i) for i in range(size)])


def to_next(x, axis, step):
    size = lax.axis_size(axis)
    return lax.ppermute(x, axis, [(i, (i + step) % size) for i in range(size)])


def norm_back(residual, row_gain, seed):
    centered = residual - jnp.mean(residual, axis=-1, keepdims=True)
    spread = jnp.mean(centered * centered, axis=-1, keepdims=True)
    scale = lax.rsqrt(spread + eps)
    unit = centered * scale
    inner = seed * row_gain
    drop = jnp.mean(inner, axis=-1, keepdims=True) + unit * jnp.mean(inner * unit, axis=-1, keepdims=True)
    gain_grad = jnp.sum(seed * unit, axis=0, keepdims=True)
    return scale * (inner - drop), gain_grad, jnp.sum(seed, axis=0, keepdims=True)


def place_norms(gain, bias, index, devices):
    both = jnp.concatenate([gain, bias], 0)
    width = both.shape[1]
    shape = (width, devices * width)
    spot = lax.broadcasted_iota(jnp.int32, shape, 0) + index * width == lax.broadcasted_iota(jnp.int32, shape, 1)
    placed = plain_dot(both, spot.astype(both.dtype)).astype(both.dtype)
    return jnp.pad(placed, ((0, 8 - both.shape[0]), (0, 0)))


def local(
    hidden,
    char_ids,
    groups,
    lengths,
    cotangent,
    qkv_weight,
    out_weight,
    up_weight,
    down_weight,
    norm_gain,
    norm_bias,
    char_table,
    gru_input,
    gru_recur,
    merge_weight,
    conv_weight,
):
    dp_size, devices = lax.axis_size("dp"), lax.axis_size("dp") * lax.axis_size("seq")
    me = lax.axis_index("dp") * lax.axis_size("seq") + lax.axis_index("seq")
    norms = place_norms(norm_gain, norm_bias, me, devices)
    order = (char_table, gru_input, gru_recur, norms, qkv_weight, out_weight, up_weight, down_weight, merge_weight, conv_weight)
    gathered = gather_all(dp_size, devices, order)
    all_norms = jnp.sum(gathered[3].astype(jnp.float32), axis=0)
    (full_table, full_input, full_recur, _, full_qkv, full_out, full_up, full_down, full_merge, full_conv) = [
        x.reshape(-1, x.shape[2]) for x in gathered
    ]
    seq_count, local_len, features = hidden.shape
    nchar = char_ids.shape[2]
    tokens = seq_count * local_len
    key_span = local_len * lax.axis_size("seq")
    gains = [all_norms[k : k + 1] for k in range(3)]
    biases = [all_norms[k : k + 1] for k in range(3, 6)]
    flat_in = hidden.reshape(tokens, features)
    qkv = plain_dot(flat_in, full_qkv).astype(jnp.bfloat16)
    queries, own_kv = qkv[:, :features], qkv[:, features:]
    peers = lax.axis_size("seq")
    kv_blocks = [own_kv] + [from_next(own_kv, "seq", j) for j in range(1, peers)]
    place = lax.rem(lax.axis_index("seq") + jnp.arange(peers), peers) * local_len
    positions = place[:, None] + jnp.arange(local_len)[None, :]
    key_valid = (positions < lengths[0]).astype(jnp.int32).reshape(1, key_span)
    assert seq_count == 1
    flat_ids = char_ids.reshape(tokens, nchar)
    table_start = groups[0] * SUBV
    own_table = lax.dynamic_slice_in_dim(full_table, table_start, SUBV, 0)
    inward = full_input.reshape(2, -1, full_input.shape[1])
    recurrent = full_recur.reshape(2, -1, full_recur.shape[1])
    char_vec, char_emb, *kept = gru_forward(flat_ids, own_table, inward, recurrent)
    factors, keeps, priors = kept[:2], kept[2:4], kept[4:]
    attended = attention(queries, key_valid, kv_blocks)
    resid_one = flat_in.astype(jnp.float32) + plain_dot(attended, full_out)
    norm_one = norm_rows(resid_one, gains[0], biases[0]).astype(jnp.bfloat16)
    up_proj = plain_dot(norm_one, full_up)
    active = gelu_exact(up_proj).astype(jnp.bfloat16)
    resid_two = norm_one.astype(jnp.float32) + plain_dot(active, full_down)
    norm_two = norm_rows(resid_two, gains[1], biases[1]).astype(jnp.bfloat16)
    merge_mats = full_merge.reshape(2, features, features)
    streams = jnp.stack([norm_two, char_vec], 0)
    merged_pair = jnp.einsum("btd,bdf->btf", streams, merge_mats, preferred_element_type=jnp.float32)
    merged_rows = jnp.concatenate([merged_pair[0], merged_pair[1]], -1).astype(jnp.bfloat16)
    padded = with_halo(merged_rows.reshape(seq_count, local_len, 2 * features), (("seq", 1),), 1)
    kernel = full_conv.reshape(3, 2 * features, features)
    windows = [
        padded[:, offset : offset + local_len].reshape(tokens, 2 * features) for offset in range(3)
    ]
    conv_out = (
        plain_dot(windows[0], kernel[0])
        + plain_dot(windows[1], kernel[1])
        + plain_dot(windows[2], kernel[2])
    )
    resid_three = norm_two.astype(jnp.float32) + conv_out
    result = norm_rows(resid_three, gains[2], biases[2]).astype(jnp.bfloat16).reshape(seq_count, local_len, features)
    back_qkv, back_out, back_up, back_down = full_qkv, full_out, full_up, full_down
    back_merge, back_conv = full_merge, full_conv
    merge_back = back_merge.reshape(2, features, features)
    kernel_back = back_conv.reshape(3, 2 * features, features)
    seed_rows = cotangent.reshape(tokens, features).astype(jnp.float32)
    grad_three, gain_three, bias_three = norm_back(resid_three, gains[2], seed_rows)
    conv_seed = grad_three.astype(jnp.bfloat16)
    conv_grad = grad_dot(jnp.concatenate(windows, 1), conv_seed)
    seed_padded = with_halo(conv_seed.reshape(seq_count, local_len, features), (("seq", 1),), 1)
    merged_grad = back_dot(
        seed_padded[:, 2 : 2 + local_len].reshape(tokens, features), kernel_back[0]
    )
    merged_grad = merged_grad + back_dot(
        seed_padded[:, 1 : 1 + local_len].reshape(tokens, features), kernel_back[1]
    )
    merged_grad = merged_grad + back_dot(
        seed_padded[:, 0:local_len].reshape(tokens, features), kernel_back[2]
    )
    merged_grad = merged_grad.astype(jnp.bfloat16)
    pair_grad = jnp.stack([merged_grad[:, :features], merged_grad[:, features:]], 0)
    merge_grad = jnp.einsum("btd,btf->bdf", streams, pair_grad, preferred_element_type=jnp.float32)
    stream_grad = jnp.einsum("btf,bdf->btd", pair_grad, merge_back, preferred_element_type=jnp.float32)
    two_grad = grad_three + stream_grad[0]
    charvec_grad = stream_grad[1]
    grad_two, gain_two, bias_two = norm_back(resid_two, gains[1], two_grad)
    down_seed = grad_two.astype(jnp.bfloat16)
    down_grad = grad_dot(active, down_seed)
    active_grad = back_dot(down_seed, back_down)
    _, pull_gelu = jax.vjp(gelu_exact, up_proj)
    up_seed = pull_gelu(active_grad)[0].astype(jnp.bfloat16)
    up_grad = grad_dot(norm_one, up_seed)
    one_grad = grad_two + back_dot(up_seed, back_up)
    grad_one, gain_one, bias_one = norm_back(resid_one, gains[0], one_grad)
    out_seed = grad_one.astype(jnp.bfloat16)
    out_grad = grad_dot(attended, out_seed)
    attn_seed = back_dot(out_seed, back_out).astype(jnp.bfloat16)
    query_grad, *kv_grads = attention_back(queries, key_valid, attn_seed, kv_blocks)
    kv_own = kv_grads[0].astype(jnp.float32)
    for j in range(1, peers):
        kv_own = kv_own + to_next(kv_grads[j], "seq", j).astype(jnp.float32)
    qkv_seed = jnp.concatenate([query_grad, kv_own.astype(jnp.bfloat16)], -1)
    qkv_grad = grad_dot(flat_in, qkv_seed)
    hidden_grad = (
        (grad_one + back_dot(qkv_seed, back_qkv))
        .astype(jnp.bfloat16)
        .reshape(seq_count, local_len, features)
    )
    input_mats, recur_sum, own_grad = gru_backward(
        flat_ids, charvec_grad, inward, recurrent, char_emb, *priors, *factors, *keeps, SUBV
    )
    table_grad = jnp.zeros(full_table.shape, jnp.bfloat16)
    table_grad = lax.dynamic_update_slice_in_dim(table_grad, own_grad.astype(jnp.bfloat16), table_start, 0)
    norm_grads = jnp.concatenate(
        [gain_one, gain_two, gain_three, bias_one, bias_two, bias_three, jnp.zeros((2, features), jnp.float32)], 0
    )
    terms = [input_mats, recur_sum, merge_grad, conv_grad, down_grad, up_grad, qkv_grad, out_grad, table_grad]
    parts = [x.astype(jnp.bfloat16).reshape(devices, -1, x.shape[-1]) for x in terms]
    width = norm_gain.shape[1]
    *sums, norm_sum = scatter_all(dp_size, parts, norm_grads, width)
    input_total, recur_total, merge_sum, conv_sum, down_sum, up_sum, qkv_sum, out_sum, table_sum = settle(sums)
    skip = me * width - window_start(me, width, features)
    gain_sum = lax.dynamic_slice(norm_sum, (0, skip), (3, width))
    bias_sum = lax.dynamic_slice(norm_sum, (3, skip), (3, width))
    return (result, hidden_grad, qkv_sum, out_sum, up_sum, down_sum, gain_sum, bias_sum, table_sum, input_total, recur_total, merge_sum, conv_sum)


def solution(mesh):
    placed = (
        P("dp", "seq", None),
        P("dp", "seq", None),
        P("dp"),
        P("dp"),
        P("dp", "seq", None),
        P(("dp", "seq"), None),
        P(("dp", "seq"), None),
        P(("dp", "seq"), None),
        P(("dp", "seq"), None),
        P(None, ("dp", "seq")),
        P(None, ("dp", "seq")),
        P(("dp", "seq"), None),
        P(("dp", "seq"), None),
        P(("dp", "seq"), None),
        P(("dp", "seq"), None),
        P(("dp", "seq"), None),
    )
    return jax.shard_map(
        local,
        mesh=mesh,
        in_specs=placed,
        out_specs=(
            P("dp", "seq", None),
            P("dp", "seq", None),
            P(("dp", "seq"), None),
            P(("dp", "seq"), None),
            P(("dp", "seq"), None),
            P(("dp", "seq"), None),
            P(None, ("dp", "seq")),
            P(None, ("dp", "seq")),
            P(("dp", "seq"), None),
            P(("dp", "seq"), None),
            P(("dp", "seq"), None),
            P(("dp", "seq"), None),
            P(("dp", "seq"), None),
        ),
        check_vma=False,
    )
```

```python
import functools
import math

import jax
import jax.numpy as jnp
from jax import lax
from jax.experimental import pallas as pl
from jax.experimental.pallas import tpu as pltpu
from jax.sharding import PartitionSpec as P

MESH = pl.DeviceIdType.MESH

HD = 64
SUBV = 128

eps = 1e-05

class Place:
    def __init__(self, dp_size):
        dp, seq = lax.axis_index("dp"), lax.axis_index("seq")
        self.lines = dp_size // 2
        self.a, self.b = dp // 2, lax.rem(dp, 2)
        self.y, self.c = seq // 2, lax.rem(seq, 2)
        flip_b = (self.a * 2 + 1 - self.b, seq)
        flip_y = (dp, (1 - self.y) * 2 + self.c)
        pick = lambda u, v: tuple(i + self.c * (j - i) for i, j in zip(u, v))
        self.first, self.second = pick(flip_b, flip_y), pick(flip_y, flip_b)
        self.sibling = (dp, self.y * 2 + 1 - self.c)
        self.up, self.down = (dp + 2, seq), (dp - 2, seq)
        self.f = self.b + self.c * (self.y - self.b)
        self.s = self.y + self.c * (self.b - self.y)
        self.has_up, self.has_down = self.a < self.lines - 1, self.a > 0

    def unit(self, a, f, s, c=None):
        c = self.c if c is None else c
        return a * 8 + f * (4 - 2 * c) + s * (2 + 2 * c) + c

    def barrier(self):
        sem = pltpu.get_barrier_semaphore()
        for who in (self.first, self.second, self.sibling):
            pl.semaphore_signal(sem, inc=1, device_id=who, device_id_type=MESH)

        @pl.when(self.has_up)
        def _():
            pl.semaphore_signal(sem, inc=1, device_id=self.up, device_id_type=MESH)

        @pl.when(self.has_down)
        def _():
            pl.semaphore_signal(sem, inc=1, device_id=self.down, device_id_type=MESH)

        pl.semaphore_wait(sem, 3 + self.has_up.astype(jnp.int32) + self.has_down.astype(jnp.int32))


def push(src, dst, send, recv, who):
    return pltpu.make_async_remote_copy(
        src_ref=src, dst_ref=dst, send_sem=send, recv_sem=recv, device_id=who, device_id_type=MESH
    )


class Gather:
    def __init__(self, at, shard, full, sems):
        self.at, self.shard, self.full = at, shard, full
        self.up_s, self.down_s, self.sum_s, self.line_r, self.second_r, self.one = sems

    def to_lines(self, src, slot, index, up, down):
        at = self.at
        if up is not False:
            @pl.when(at.has_up if up is True else jnp.logical_and(up, at.has_up))
            def _():
                push(src, self.full.at[index], self.up_s.at[slot], self.line_r.at[slot], at.up).start()
        if down is not False:
            @pl.when(at.has_down if down is True else jnp.logical_and(down, at.has_down))
            def _():
                push(src, self.full.at[index], self.down_s.at[slot], self.line_r.at[slot], at.down).start()

    def across(self, src, slot, index):
        push(src, self.full.at[index], self.sum_s.at[0], self.second_r.at[slot], self.at.second).start()
        self.aside(src, index)

    def aside(self, src, index):
        push(src, self.full.at[index], self.sum_s.at[1], self.one.at[1], self.at.sibling).start()

    def begin(self):
        at = self.at
        me = at.unit(at.a, at.f, at.s)
        pltpu.make_async_copy(self.shard, self.full.at[me], self.one.at[3]).start()
        push(self.shard, self.full.at[me], self.one.at[2], self.one.at[0], at.first).start()
        slot = at.a * 2 + at.f
        self.to_lines(self.shard, slot, me, True, True)
        self.across(self.shard, slot, me)

    def after_first(self):
        at = self.at
        index = at.unit(at.a, 1 - at.f, at.s)
        ref = self.full.at[index]
        push(ref, ref, self.one.at[2], self.one.at[0], at.first).wait_recv()
        slot = at.a * 2 + 1 - at.f
        self.to_lines(ref, slot, index, True, True)
        self.across(ref, slot, index)

    def after_line(self, k, g):
        at = self.at
        for sign in (-1, 1):
            a = at.a + sign * k
            f = at.f if g == 0 else 1 - at.f

            @pl.when(a >= 0 if sign < 0 else a < at.lines)
            def _():
                index, slot = at.unit(a, f, at.s), a * 2 + f
                ref = self.full.at[index]
                push(ref, ref, self.up_s.at[slot], self.line_r.at[slot], at.up).wait_recv()
                self.to_lines(ref, slot, index, sign < 0, sign > 0)
                self.across(ref, slot, index)

    def after_second(self, k, g):
        at = self.at
        for sign in (-1, 1) if k else (1,):
            a = at.a + sign * k
            f = at.f if g == 0 else 1 - at.f

            @pl.when(a >= 0 if sign < 0 else a < at.lines)
            def _():
                index, slot = at.unit(a, f, 1 - at.s), a * 2 + f
                ref = self.full.at[index]
                push(ref, ref, self.sum_s.at[0], self.second_r.at[slot], at.second).wait_recv()
                self.aside(ref, index)

    def finish(self):
        at, n = self.at, self.at.lines
        me = at.unit(at.a, at.f, at.s)
        half = self.full.at[pl.ds(0, 4 * n)]
        push(half, half, self.sum_s.at[1], self.one.at[1], at.sibling).wait_recv()
        pltpu.make_async_copy(self.shard, self.full.at[me], self.one.at[3]).wait()
        push(self.shard, self.full.at[me], self.one.at[2], self.one.at[0], at.first).wait_send()
        push(half, half, self.sum_s.at[1], self.one.at[1], at.sibling).wait_send()
        part = self.full.at[pl.ds(0, 2 * n)]
        push(part, part, self.sum_s.at[0], self.one.at[0], at.second).wait_send()
        for a in range(n):
            for f in range(2):
                slot = a * 2 + f
                ref = self.full.at[0]

                @pl.when(jnp.logical_and(at.has_up, a <= at.a))
                def _():
                    push(ref, ref, self.up_s.at[slot], self.line_r.at[slot], at.up).wait_send()

                @pl.when(jnp.logical_and(at.has_down, a >= at.a))
                def _():
                    push(ref, ref, self.down_s.at[slot], self.line_r.at[slot], at.down).wait_send()


def gather_sems(n):
    dma = pltpu.SemaphoreType.DMA
    return [dma((2 * n,)), dma((2 * n,)), dma((2,)), dma((2 * n,)), dma((2 * n,)), dma((4,))]


def gather_kernel(dp_size, count, *refs):
    shards, fulls, sems = refs[:count], refs[count : 2 * count], refs[2 * count :]
    at = Place(dp_size)
    at.barrier()
    jobs = [Gather(at, shards[i], fulls[i], sems[6 * i : 6 * i + 6]) for i in range(count)]
    for job in jobs:
        job.begin()
    for job in jobs:
        job.after_first()
    for k in range(1, at.lines):
        for g in range(2):
            for job in jobs:
                job.after_line(k, g)
            for job in jobs:
                job.after_second(k - 1, g)
    for g in range(2):
        for job in jobs:
            job.after_second(at.lines - 1, g)
    for job in jobs:
        job.finish()


def gather_all(dp_size, devices, shards, cid=1):
    count = len(shards)
    return pl.pallas_call(
        functools.partial(gather_kernel, dp_size, count),
        out_shape=[jax.ShapeDtypeStruct((devices,) + x.shape, x.dtype) for x in shards],
        in_specs=[pl.BlockSpec(memory_space=pl.ANY)] * count,
        out_specs=[pl.BlockSpec(memory_space=pl.ANY)] * count,
        scratch_shapes=gather_sems(dp_size // 2) * count,
        compiler_params=pltpu.CompilerParams(collective_id=cid, has_side_effects=True),
    )(*shards)


def wide(x):
    return x.astype(jnp.float32)


def add_into(dst, src):
    dst[...] = dst[...] + src[...]


class Scatter:
    def __init__(self, at, part, out, bufs, sems):
        self.at, self.part, self.out = at, part, out
        self.own, self.sib, self.sec, self.line, self.fst = bufs
        self.one, self.line_s, self.line_r = sems

    def begin(self):
        at = self.at

        def body(j, carry):
            a, f, s = j // 4, lax.rem(j // 2, 2), lax.rem(j, 2)
            push(self.part(at.unit(a, f, s, 1 - at.c)), self.sib.at[j], self.one.at[0], self.one.at[1], at.sibling).start()
            return carry

        lax.fori_loop(0, 4 * at.lines, body, 0)

        def load(j, carry):
            a, f, s = j // 4, lax.rem(j // 2, 2), lax.rem(j, 2)
            pltpu.make_async_copy(self.part(at.unit(a, f, s)), self.own.at[j], self.one.at[2]).start()
            return carry

        lax.fori_loop(0, 4 * at.lines, load, 0)

    def after_sibling(self):
        at = self.at
        n = 2 * at.lines
        pltpu.make_async_copy(self.own, self.own, self.one.at[2]).wait()
        push(self.sib, self.sib, self.one.at[0], self.one.at[1], at.sibling).wait_recv()

        def far(q, carry):
            j = q * 2 + 1 - at.s
            add_into(self.own.at[j], self.sib.at[j])
            return carry

        def send(q, carry):
            push(self.own.at[q * 2 + 1 - at.s], self.sec.at[q], self.one.at[3], self.one.at[4], at.second).start()
            return carry

        def near(q, carry):
            j = q * 2 + at.s
            add_into(self.own.at[j], self.sib.at[j])
            return carry

        lax.fori_loop(0, n, far, 0)
        lax.fori_loop(0, n, send, 0)
        lax.fori_loop(0, n, near, 0)

    def after_second(self):
        at = self.at
        push(self.sec, self.sec, self.one.at[3], self.one.at[4], at.second).wait_recv()

        def body(q, carry):
            add_into(self.own.at[q * 2 + at.s], self.sec.at[q])
            return carry

        lax.fori_loop(0, 2 * at.lines, body, 0)

    def hop(self, low, high, inward, dst, extra):
        at = self.at
        has, who = (at.has_up, at.down) if dst < 0 else (at.has_down, at.up)

        def take(q, carry):
            push(self.line.at[q], self.line.at[q], self.line_s.at[q], self.line_r.at[q], who).wait_recv()
            add_into(self.own.at[q * 2 + at.s], self.line.at[q])
            return carry

        @pl.when(has)
        def _():
            lax.fori_loop(low, high, take, 0)

        def send(q, carry):
            slot = q if dst < 0 else jnp.where(q // 2 == at.a + 1, 2 * at.lines + lax.rem(q, 2), q)
            push(self.own.at[q * 2 + at.s], self.line.at[slot], self.line_s.at[q], self.line_r.at[slot], who).start()
            return carry

        lax.fori_loop(low, high, send, 0)

    def along(self, h):
        at = self.at
        n = at.lines
        hops = n - 1 if n <= 4 else 1

        @pl.when(jnp.logical_and(at.has_down, at.lines - 1 - at.a == h) if hops > 1 else at.has_down)
        def _():
            self.hop(0, 2 * at.a, at.up, -1, None)

        @pl.when(jnp.logical_and(at.has_up, at.a == h) if hops > 1 else at.has_up)
        def _():
            self.hop(2 * at.a + 2, 2 * n, at.down, 1, None)

    def ends(self, f, into):
        at = self.at
        for has, slot in ((at.has_up, 2 * at.a + f), (at.has_down, 2 * at.lines + f)):
            @pl.when(has)
            def _():
                ref = self.line.at[slot]
                push(ref, ref, self.line_s.at[0], self.line_r.at[slot], at.first).wait_recv()
                into[...] = (wide(into[...]) + wide(ref[...])).astype(into.dtype)

    def last_send(self):
        at = self.at
        mine = self.own.at[(2 * at.a + 1 - at.f) * 2 + at.s]
        self.ends(1 - at.f, mine)
        push(mine, self.fst, self.one.at[5], self.one.at[6], at.first).start()
        self.out[...] = wide(self.own[(2 * at.a + at.f) * 2 + at.s])
        self.ends(at.f, self.out)

    def finish(self):
        at = self.at
        push(self.fst, self.fst, self.one.at[5], self.one.at[6], at.first).wait_recv()
        self.out[...] = self.out[...] + wide(self.fst[...])

    def drain(self):
        at = self.at
        n = at.lines
        push(self.sib, self.sib, self.one.at[0], self.one.at[1], at.sibling).wait_send()
        push(self.sec, self.sec, self.one.at[3], self.one.at[4], at.second).wait_send()
        push(self.fst, self.fst, self.one.at[5], self.one.at[6], at.first).wait_send()

        def body(q, carry):
            @pl.when(q // 2 != at.a)
            def _():
                push(self.own.at[q], self.own.at[q], self.line_s.at[q], self.line_r.at[q], at.first).wait_send()
            return carry

        lax.fori_loop(0, 2 * n, body, 0)


def scatter_buffers(n, shape, dtype):
    v = lambda k: pltpu.VMEM((k,) + shape, dtype)
    return [v(4 * n), v(4 * n), v(2 * n), v(2 * n + 2), pltpu.VMEM(shape, dtype)]


def scatter_sems(n):
    dma = pltpu.SemaphoreType.DMA
    return [dma((7,)), dma((2 * n,)), dma((2 * n + 2,))]


def scatter_stages(lines):
    hops = lines - 1 if lines <= 4 else 1
    stages = [Scatter.after_sibling, Scatter.after_second]
    for h in range(hops):
        stages.append(functools.partial(Scatter.along, h=h))
    return stages + [Scatter.last_send, Scatter.finish]


LANES = 128


def window_start(unit, width, features):
    tile = unit * width // LANES
    return (tile - tile // (features // LANES - 1)) * LANES


def whole_part(ref, rows, cols):
    return lambda unit: ref.at[unit, pl.ds(*rows), pl.ds(*cols)]


def window_part(ref, width):
    features = ref.shape[1]
    return lambda unit: ref.at[:, pl.ds(pl.multiple_of(window_start(unit, width, features), LANES), 2 * LANES)]


def cut(shape, cap):
    rows, cols = shape
    pieces = max(1, round(rows * cols / cap))
    while pieces > 1 and not (rows % (16 * pieces) == 0 or cols % (LANES * pieces) == 0):
        pieces -= 1
    if rows % (16 * pieces) == 0:
        step = rows // pieces
        return [((k * step, step), (0, cols)) for k in range(pieces)]
    step = cols // pieces
    return [((0, rows), (k * step, step)) for k in range(pieces)]


def scatter_kernel(dp_size, chunks, count, width, *refs):
    parts, outs, rest = refs[:count], refs[count : 2 * count], refs[2 * count :]
    at = Place(dp_size)
    at.barrier()
    jobs = []
    for k, (i, rows, cols) in enumerate(chunks):
        last = i == count - 1
        part = window_part(parts[i], width) if last else whole_part(parts[i], rows, cols)
        out = outs[i] if last else outs[i].at[pl.ds(*rows), pl.ds(*cols)]
        jobs.append(Scatter(at, part, out, rest[8 * k : 8 * k + 5], rest[8 * k + 5 : 8 * k + 8]))
    for job in jobs:
        job.begin()
    stages = scatter_stages(at.lines)
    total = len(jobs)
    for t in range(total + len(stages) - 1):
        for k, stage in enumerate(stages):
            if 0 <= t - k < total:
                stage(jobs[t - k])
    for job in jobs:
        job.drain()


def scatter_all(dp_size, parts, norm_rows, width, cap=36864, cid=2):
    count = len(parts) + 1
    n = dp_size // 2
    outs = [jax.ShapeDtypeStruct(x.shape[1:], jnp.float32) for x in parts]
    outs.append(jax.ShapeDtypeStruct((norm_rows.shape[0], 2 * LANES), jnp.float32))
    chunks, scratch = [], []
    for i, x in enumerate(parts):
        for rows, cols in cut(x.shape[1:], cap):
            chunks.append((i, rows, cols))
            scratch += scatter_buffers(n, (rows[1], cols[1]), x.dtype) + scatter_sems(n)
    chunks.append((count - 1, None, None))
    scratch += scatter_buffers(n, outs[-1].shape, jnp.float32) + scatter_sems(n)
    return pl.pallas_call(
        functools.partial(scatter_kernel, dp_size, chunks, count, width),
        out_shape=outs,
        in_specs=[pl.BlockSpec(memory_space=pl.ANY)] * count,
        out_specs=[pl.BlockSpec(memory_space=pltpu.VMEM)] * count,
        scratch_shapes=scratch,
        compiler_params=pltpu.CompilerParams(collective_id=cid, has_side_effects=True, vmem_limit_bytes=64000000),
    )(*parts, norm_rows)


def settle_kernel(*refs):
    half = len(refs) // 2
    for src, dst in zip(refs[:half], refs[half:]):
        dst[...] = src[...]


def settle(arrays):
    spec = [pl.BlockSpec(memory_space=pltpu.VMEM)] * len(arrays)
    return pl.pallas_call(
        settle_kernel,
        out_shape=[jax.ShapeDtypeStruct(x.shape, x.dtype) for x in arrays],
        in_specs=spec,
        out_specs=spec,
    )(*arrays)


def with_halo(x, sides, width):
    for axis, dim in sides:
        devices, length = (lax.axis_size(axis), x.shape[dim])
        up = [(i, (i + 1) % devices) for i in range(devices - 1)]
        down = [(j, i) for i, j in up]
        last = lax.slice_in_dim(x, length - width, length, axis=dim)
        first = lax.slice_in_dim(x, 0, width, axis=dim)
        before = lax.ppermute(last, axis, up)
        after = lax.ppermute(first, axis, down)
        x = jnp.concatenate([before, x, after], axis=dim)
    return x


def norm_rows(residual, row_gain, row_bias):
    centered = residual - jnp.mean(residual, axis=-1, keepdims=True)
    spread = jnp.mean(centered * centered, axis=-1, keepdims=True)
    return centered * lax.rsqrt(spread + eps) * row_gain + row_bias


def gelu_exact(pre_act):
    return jax.nn.gelu(pre_act, approximate=False)


def plain_dot(left, right):
    return jnp.dot(left, right, preferred_element_type=jnp.float32)


def grad_dot(left, right):
    return lax.dot_general(
        left, right, (((0,), (0,)), ((), ())), preferred_element_type=jnp.float32
    )


def back_dot(left, right):
    return lax.dot_general(
        left, right, (((1,), (1,)), ((), ())), preferred_element_type=jnp.float32
    )


def squash(x):
    return 0.5 * jnp.tanh(0.5 * x) + 0.5


def slot_onehot(ids, slots, subset):
    cols = lax.broadcasted_iota(jnp.int32, (ids.shape[0], subset), 1)
    hots = [(ids[:, s : s + 1] == cols).astype(jnp.bfloat16) for s in slots]
    return jnp.concatenate(hots, 0)


def gru_embed(ids_ref, table, w_in, emb_ref, gates, chunk=4):
    rows, nchar = ids_ref.shape
    ids = ids_ref[...]
    for k in range(0, nchar, chunk):
        hot = slot_onehot(ids, range(k, k + chunk), table.shape[0])
        emb = plain_dot(hot, table[...]).astype(jnp.bfloat16)
        emb_ref[k : k + chunk] = emb.reshape(chunk, rows, -1)
        for d in range(2):
            gates[d, k : k + chunk] = plain_dot(emb, w_in[d]).reshape(chunk, rows, -1)


def gru_step(d, slot, count, gates, w_rec, state, factor, keep, prior):
    units = state.shape[2]
    old = state[d]
    low = old.astype(jnp.bfloat16)
    rec = plain_dot(low, w_rec[d])
    gi = gates[d, slot]
    reset = squash(gi[:, :units] + rec[:, :units])
    update = squash(gi[:, units : 2 * units] + rec[:, units : 2 * units])
    rec_n = rec[:, 2 * units :]
    cand = jnp.tanh(gi[:, 2 * units :] + reset * rec_n)
    live = slot < count
    state[d] = jnp.where(live, (1.0 - update) * cand + update * old, old)
    by_cand = jnp.where(live, (1.0 - update) * (1.0 - cand * cand), 0.0)
    by_update = jnp.where(live, (old - cand) * update * (1.0 - update), 0.0)
    by_reset = by_cand * rec_n * reset * (1.0 - reset)
    prior[...] = low
    keep[...] = jnp.where(live, update, 1.0)
    for k, x in enumerate((by_reset, by_update, by_cand, reset)):
        factor[:, k * units : (k + 1) * units] = x.astype(factor.dtype)


def gru_forward_kernel(ids_ref, table, w_in, w_rec, vec, emb, f0, f1, z0, z1, h0, h1, gates, state):
    i = pl.program_id(0)
    nchar = pl.num_programs(0)

    @pl.when(i == 0)
    def _():
        gru_embed(ids_ref, table, w_in, emb, gates)
        state[...] = jnp.zeros_like(state)

    count = jnp.sum((ids_ref[...] > 0).astype(jnp.int32), axis=1, keepdims=True)
    gru_step(0, i, count, gates, w_rec, state, f0.at[0], z0.at[0], h0.at[0])
    gru_step(1, nchar - 1 - i, count, gates, w_rec, state, f1.at[0], z1.at[0], h1.at[0])

    @pl.when(i == nchar - 1)
    def _():
        units = state.shape[2]
        vec[:, :units] = state[0].astype(vec.dtype)
        vec[:, units:] = state[1].astype(vec.dtype)


def slot_specs(nchar, rows, cols, backward):
    up = pl.BlockSpec((1, rows, cols), lambda i: (i, 0, 0))
    down = pl.BlockSpec((1, rows, cols), lambda i: (nchar - 1 - i, 0, 0))
    return [down, up] if backward else [up, down]


def gru_cost(nchar, rows, width, units, products):
    steps = 2 * nchar * rows
    return pl.CostEstimate(
        flops=12 * products * steps * (width + units) * units,
        bytes_accessed=16 * steps * units,
        transcendentals=3 * steps * units,
    )


def gru_forward(ids, table, w_in, w_rec):
    rows, nchar = ids.shape
    width, units = table.shape[1], w_rec.shape[1]
    whole = lambda shape: pl.BlockSpec(shape, lambda i: (0,) * len(shape))
    slots = functools.partial(slot_specs, nchar, rows, backward=False)
    shape = jax.ShapeDtypeStruct
    factor = shape((nchar, rows, 4 * units), jnp.bfloat16)
    keep = shape((nchar, rows, units), jnp.float32)
    prior = shape((nchar, rows, units), jnp.bfloat16)
    return pl.pallas_call(
        gru_forward_kernel,
        grid=(nchar,),
        out_shape=[
            shape((rows, 2 * units), jnp.bfloat16),
            shape((nchar, rows, width), jnp.bfloat16),
            factor, factor, keep, keep, prior, prior,
        ],
        in_specs=[whole(x.shape) for x in (ids, table, w_in, w_rec)],
        out_specs=[whole((rows, 2 * units)), whole((nchar, rows, width))]
        + slots(4 * units) + slots(units) + slots(units),
        scratch_shapes=[
            pltpu.VMEM((2, nchar, rows, 3 * units), jnp.float32),
            pltpu.VMEM((2, rows, units), jnp.float32),
        ],
        compiler_params=pltpu.CompilerParams(vmem_limit_bytes=60000000),
        cost_estimate=gru_cost(nchar, rows, width, units, 1),
    )(ids, table, w_in, w_rec)


def gru_back_step(d, slot, factor, keep, w_rec, grad, seeds):
    units = grad.shape[2]
    g = grad[d]
    part = lambda k: factor[:, k * units : (k + 1) * units].astype(jnp.float32)
    by_cand = g * part(2)
    seeds[d, slot, :, :units] = (g * part(0)).astype(seeds.dtype)
    seeds[d, slot, :, units : 2 * units] = (g * part(1)).astype(seeds.dtype)
    seeds[d, slot, :, 2 * units : 3 * units] = (by_cand * part(3)).astype(seeds.dtype)
    seeds[d, slot, :, 3 * units :] = by_cand.astype(seeds.dtype)
    grad[d] = g * keep[...] + back_dot(seeds[d, slot, :, : 3 * units], w_rec[d])


def gru_weight_grads(d, seeds, emb, prior, d_in, d_rec):
    _, nchar, rows, wide = seeds.shape
    units = wide // 4
    states = prior[...].reshape(nchar * rows, units)
    chars = emb[...].reshape(nchar * rows, -1)
    col = lambda k: seeds[d, :, :, k * units : (k + 1) * units].reshape(nchar * rows, units)
    for k in range(3):
        d_rec[d, :, k * units : (k + 1) * units] = grad_dot(states, col(k)).astype(d_rec.dtype)
        own = col(3 if k == 2 else k)
        d_in[d, :, k * units : (k + 1) * units] = grad_dot(chars, own).astype(d_in.dtype)


def gru_char_grads(ids_ref, seeds, w_in, d_table, chunk=4):
    _, nchar, rows, wide = seeds.shape
    units = wide // 4
    ids = ids_ref[...]
    total = jnp.zeros(d_table.shape, jnp.float32)
    for k in range(0, nchar, chunk):
        grad = None
        for d in range(2):
            both = seeds[d, k : k + chunk].reshape(chunk * rows, wide)
            part = back_dot(both[:, : 2 * units], w_in[d][:, : 2 * units])
            part = part + back_dot(both[:, 3 * units :], w_in[d][:, 2 * units :])
            grad = part if grad is None else grad + part
        hot = slot_onehot(ids, range(k, k + chunk), d_table.shape[0])
        total = total + grad_dot(hot, grad.astype(jnp.bfloat16))
    d_table[...] = total


def gru_backward_kernel(ids_ref, seed, w_in, w_rec, emb, h0, h1, f0, f1, z0, z1, d_in, d_rec, d_table, grad, seeds):
    i = pl.program_id(0)
    nchar = pl.num_programs(0)

    @pl.when(i == 0)
    def _():
        units = grad.shape[2]
        grad[0] = seed[:, :units]
        grad[1] = seed[:, units:]

    gru_back_step(0, nchar - 1 - i, f0.at[0], z0.at[0], w_rec, grad, seeds)
    gru_back_step(1, i, f1.at[0], z1.at[0], w_rec, grad, seeds)

    @pl.when(i == nchar - 1)
    def _():
        gru_weight_grads(0, seeds, emb, h0, d_in, d_rec)
        gru_weight_grads(1, seeds, emb, h1, d_in, d_rec)
        gru_char_grads(ids_ref, seeds, w_in, d_table)


def gru_backward(ids, seed, w_in, w_rec, emb, h0, h1, f0, f1, z0, z1, subset):
    nchar, rows, width = emb.shape
    units = w_rec.shape[1]
    whole = lambda shape: pl.BlockSpec(shape, lambda i: (0,) * len(shape))
    slots = functools.partial(slot_specs, nchar, rows, backward=True)
    shape = jax.ShapeDtypeStruct
    return pl.pallas_call(
        gru_backward_kernel,
        grid=(nchar,),
        out_shape=[
            shape(w_in.shape, jnp.bfloat16),
            shape(w_rec.shape, jnp.bfloat16),
            shape((subset, width), jnp.float32),
        ],
        in_specs=[whole(x.shape) for x in (ids, seed, w_in, w_rec, emb, h0, h1)] + slots(4 * units) + slots(units),
        out_specs=[whole(w_in.shape), whole(w_rec.shape), whole((subset, width))],
        scratch_shapes=[
            pltpu.VMEM((2, rows, units), jnp.float32),
            pltpu.VMEM((2, nchar, rows, 4 * units), jnp.bfloat16),
        ],
        compiler_params=pltpu.CompilerParams(vmem_limit_bytes=60000000),
        cost_estimate=gru_cost(nchar, rows, width, units, 2),
    )(ids, seed, w_in, w_rec, emb, h0, h1, f0, f1, z0, z1)


def head_pair(q_ref, blocks, valid, pair, half):
    features = q_ref.shape[1]
    cols = pl.ds(pair * 2 * HD, 2 * HD)
    queries = q_ref[:, cols]
    keys = jnp.concatenate([b[:, cols] for b in blocks], 0)
    values = jnp.concatenate([b[:, pl.ds(features + pair * 2 * HD, 2 * HD)] for b in blocks], 0)
    scores = back_dot(one_head(queries, half), keys) * (1.0 / math.sqrt(HD))
    scores = jnp.where(valid, scores, -1000000000.0)
    weight = jnp.exp(scores - jnp.max(scores, axis=-1, keepdims=True))
    return weight / jnp.sum(weight, axis=-1, keepdims=True), queries, keys, values


def first_lanes(shape):
    return lax.broadcasted_iota(jnp.int32, shape, 1) < HD


def one_head(x, half):
    keep = first_lanes(x.shape) if half == 0 else jnp.logical_not(first_lanes(x.shape))
    return jnp.where(keep, x, jnp.zeros_like(x))


def side_by_side(left, right):
    return jnp.where(first_lanes(left.shape), left, right)


def attention_kernel(count, q_ref, valid_ref, *refs):
    blocks, out = refs[:count], refs[count]
    valid = jnp.broadcast_to(valid_ref[...] > 0, (q_ref.shape[0], valid_ref.shape[1]))
    for pair in range(q_ref.shape[1] // (2 * HD)):
        both = []
        for half in range(2):
            probs, _, _, values = head_pair(q_ref, blocks, valid, pair, half)
            both.append(plain_dot(probs.astype(jnp.bfloat16), values))
        out[:, pl.ds(pair * 2 * HD, 2 * HD)] = side_by_side(*both).astype(out.dtype)


def attention_back_kernel(count, q_ref, valid_ref, seed_ref, *refs):
    blocks, q_out, outs = refs[:count], refs[count], refs[count + 1 :]
    rows, features = q_ref.shape
    scale = 1.0 / math.sqrt(HD)
    valid = jnp.broadcast_to(valid_ref[...] > 0, (rows, valid_ref.shape[1]))
    for pair in range(features // (2 * HD)):
        cols = pl.ds(pair * 2 * HD, 2 * HD)
        seed = seed_ref[:, cols]
        q_both, k_both, v_both = [], [], []
        for half in range(2):
            probs, queries, keys, values = head_pair(q_ref, blocks, valid, pair, half)
            probs_grad = back_dot(one_head(seed, half), values)
            inner = jnp.sum(probs * probs_grad, axis=-1, keepdims=True)
            score_grad = (probs * (probs_grad - inner)).astype(jnp.bfloat16)
            q_both.append(plain_dot(score_grad, keys))
            k_both.append(grad_dot(score_grad, queries))
            v_both.append(grad_dot(probs.astype(jnp.bfloat16), seed))
        q_out[:, cols] = (side_by_side(*q_both) * scale).astype(q_out.dtype)
        k_grad = (side_by_side(*k_both) * scale).astype(jnp.bfloat16)
        v_grad = side_by_side(*v_both).astype(jnp.bfloat16)
        for j, out in enumerate(outs):
            out[:, cols] = k_grad[j * rows : (j + 1) * rows]
            out[:, pl.ds(features + pair * 2 * HD, 2 * HD)] = v_grad[j * rows : (j + 1) * rows]


def attention_cost(rows, blocks, features, products):
    span = rows * len(blocks)
    return pl.CostEstimate(
        flops=2 * products * rows * span * features,
        bytes_accessed=8 * span * features,
        transcendentals=rows * span * (features // HD),
    )


def attention(queries, valid, blocks):
    rows, features = queries.shape
    vmem = pl.BlockSpec(memory_space=pltpu.VMEM)
    return pl.pallas_call(
        functools.partial(attention_kernel, len(blocks)),
        out_shape=jax.ShapeDtypeStruct((rows, features), jnp.bfloat16),
        in_specs=[vmem] * (2 + len(blocks)),
        out_specs=vmem,
        cost_estimate=attention_cost(rows, blocks, features, 2),
    )(queries, valid, *blocks)


def attention_back(queries, valid, seed, blocks):
    rows, features = queries.shape
    vmem = pl.BlockSpec(memory_space=pltpu.VMEM)
    return pl.pallas_call(
        functools.partial(attention_back_kernel, len(blocks)),
        out_shape=[jax.ShapeDtypeStruct((rows, features), jnp.bfloat16)]
        + [jax.ShapeDtypeStruct((rows, 2 * features), jnp.bfloat16)] * len(blocks),
        in_specs=[vmem] * (3 + len(blocks)),
        out_specs=[vmem] * (1 + len(blocks)),
        cost_estimate=attention_cost(rows, blocks, features, 5),
    )(queries, valid, seed, *blocks)


def from_next(x, axis, step):
    size = lax.axis_size(axis)
    return lax.ppermute(x, axis, [((i + step) % size, i) for i in range(size)])


def to_next(x, axis, step):
    size = lax.axis_size(axis)
    return lax.ppermute(x, axis, [(i, (i + step) % size) for i in range(size)])


def norm_back(residual, row_gain, seed):
    centered = residual - jnp.mean(residual, axis=-1, keepdims=True)
    spread = jnp.mean(centered * centered, axis=-1, keepdims=True)
    scale = lax.rsqrt(spread + eps)
    unit = centered * scale
    inner = seed * row_gain
    drop = jnp.mean(inner, axis=-1, keepdims=True) + unit * jnp.mean(inner * unit, axis=-1, keepdims=True)
    gain_grad = jnp.sum(seed * unit, axis=0, keepdims=True)
    return scale * (inner - drop), gain_grad, jnp.sum(seed, axis=0, keepdims=True)


def place_norms(gain, bias, index, devices):
    both = jnp.concatenate([gain, bias], 0)
    width = both.shape[1]
    shape = (width, devices * width)
    spot = lax.broadcasted_iota(jnp.int32, shape, 0) + index * width == lax.broadcasted_iota(jnp.int32, shape, 1)
    placed = plain_dot(both, spot.astype(both.dtype)).astype(both.dtype)
    return jnp.pad(placed, ((0, 8 - both.shape[0]), (0, 0)))


def local(
    hidden,
    char_ids,
    groups,
    lengths,
    cotangent,
    qkv_weight,
    out_weight,
    up_weight,
    down_weight,
    norm_gain,
    norm_bias,
    char_table,
    gru_input,
    gru_recur,
    merge_weight,
    conv_weight,
):
    dp_size, devices = lax.axis_size("dp"), lax.axis_size("dp") * lax.axis_size("seq")
    me = lax.axis_index("dp") * lax.axis_size("seq") + lax.axis_index("seq")
    norms = place_norms(norm_gain, norm_bias, me, devices)
    order = (char_table, gru_input, gru_recur, norms, qkv_weight, out_weight, up_weight, down_weight, merge_weight)
    full_conv = lax.all_gather(conv_weight, ("dp", "seq"), axis=0, tiled=True)
    gathered = gather_all(dp_size, devices, order)
    all_norms = jnp.sum(gathered[3].astype(jnp.float32), axis=0)
    (full_table, full_input, full_recur, _, full_qkv, full_out, full_up, full_down, full_merge) = [
        x.reshape(-1, x.shape[2]) for x in gathered
    ]
    seq_count, local_len, features = hidden.shape
    nchar = char_ids.shape[2]
    tokens = seq_count * local_len
    key_span = local_len * lax.axis_size("seq")
    gains = [all_norms[k : k + 1] for k in range(3)]
    biases = [all_norms[k : k + 1] for k in range(3, 6)]
    flat_in = hidden.reshape(tokens, features)
    qkv = plain_dot(flat_in, full_qkv).astype(jnp.bfloat16)
    queries, own_kv = qkv[:, :features], qkv[:, features:]
    peers = lax.axis_size("seq")
    kv_blocks = [own_kv] + [from_next(own_kv, "seq", j) for j in range(1, peers)]
    place = lax.rem(lax.axis_index("seq") + jnp.arange(peers), peers) * local_len
    positions = place[:, None] + jnp.arange(local_len)[None, :]
    key_valid = (positions < lengths[0]).astype(jnp.int32).reshape(1, key_span)
    assert seq_count == 1
    flat_ids = char_ids.reshape(tokens, nchar)
    table_start = groups[0] * SUBV
    own_table = lax.dynamic_slice_in_dim(full_table, table_start, SUBV, 0)
    inward = full_input.reshape(2, -1, full_input.shape[1])
    recurrent = full_recur.reshape(2, -1, full_recur.shape[1])
    char_vec, char_emb, *kept = gru_forward(flat_ids, own_table, inward, recurrent)
    factors, keeps, priors = kept[:2], kept[2:4], kept[4:]
    attended = attention(queries, key_valid, kv_blocks)
    resid_one = flat_in.astype(jnp.float32) + plain_dot(attended, full_out)
    norm_one = norm_rows(resid_one, gains[0], biases[0]).astype(jnp.bfloat16)
    up_proj = plain_dot(norm_one, full_up)
    active = gelu_exact(up_proj).astype(jnp.bfloat16)
    resid_two = norm_one.astype(jnp.float32) + plain_dot(active, full_down)
    norm_two = norm_rows(resid_two, gains[1], biases[1]).astype(jnp.bfloat16)
    merge_mats = full_merge.reshape(2, features, features)
    streams = jnp.stack([norm_two, char_vec], 0)
    merged_pair = jnp.einsum("btd,bdf->btf", streams, merge_mats, preferred_element_type=jnp.float32)
    merged_rows = jnp.concatenate([merged_pair[0], merged_pair[1]], -1).astype(jnp.bfloat16)
    padded = with_halo(merged_rows.reshape(seq_count, local_len, 2 * features), (("seq", 1),), 1)
    kernel = full_conv.reshape(3, 2 * features, features)
    windows = [
        padded[:, offset : offset + local_len].reshape(tokens, 2 * features) for offset in range(3)
    ]
    conv_out = (
        plain_dot(windows[0], kernel[0])
        + plain_dot(windows[1], kernel[1])
        + plain_dot(windows[2], kernel[2])
    )
    resid_three = norm_two.astype(jnp.float32) + conv_out
    result = norm_rows(resid_three, gains[2], biases[2]).astype(jnp.bfloat16).reshape(seq_count, local_len, features)
    back_qkv, back_out, back_up, back_down = full_qkv, full_out, full_up, full_down
    back_merge, back_conv = full_merge, full_conv
    merge_back = back_merge.reshape(2, features, features)
    kernel_back = back_conv.reshape(3, 2 * features, features)
    seed_rows = cotangent.reshape(tokens, features).astype(jnp.float32)
    grad_three, gain_three, bias_three = norm_back(resid_three, gains[2], seed_rows)
    conv_seed = grad_three.astype(jnp.bfloat16)
    conv_grad = grad_dot(jnp.concatenate(windows, 1), conv_seed)
    conv_sum = lax.psum_scatter(conv_grad.astype(jnp.bfloat16), ("dp", "seq"), scatter_dimension=0, tiled=True).astype(jnp.float32)
    seed_padded = with_halo(conv_seed.reshape(seq_count, local_len, features), (("seq", 1),), 1)
    merged_grad = back_dot(
        seed_padded[:, 2 : 2 + local_len].reshape(tokens, features), kernel_back[0]
    )
    merged_grad = merged_grad + back_dot(
        seed_padded[:, 1 : 1 + local_len].reshape(tokens, features), kernel_back[1]
    )
    merged_grad = merged_grad + back_dot(
        seed_padded[:, 0:local_len].reshape(tokens, features), kernel_back[2]
    )
    merged_grad = merged_grad.astype(jnp.bfloat16)
    pair_grad = jnp.stack([merged_grad[:, :features], merged_grad[:, features:]], 0)
    merge_grad = jnp.einsum("btd,btf->bdf", streams, pair_grad, preferred_element_type=jnp.float32)
    stream_grad = jnp.einsum("btf,bdf->btd", pair_grad, merge_back, preferred_element_type=jnp.float32)
    two_grad = grad_three + stream_grad[0]
    charvec_grad = stream_grad[1]
    grad_two, gain_two, bias_two = norm_back(resid_two, gains[1], two_grad)
    down_seed = grad_two.astype(jnp.bfloat16)
    down_grad = grad_dot(active, down_seed)
    active_grad = back_dot(down_seed, back_down)
    _, pull_gelu = jax.vjp(gelu_exact, up_proj)
    up_seed = pull_gelu(active_grad)[0].astype(jnp.bfloat16)
    up_grad = grad_dot(norm_one, up_seed)
    one_grad = grad_two + back_dot(up_seed, back_up)
    grad_one, gain_one, bias_one = norm_back(resid_one, gains[0], one_grad)
    out_seed = grad_one.astype(jnp.bfloat16)
    out_grad = grad_dot(attended, out_seed)
    attn_seed = back_dot(out_seed, back_out).astype(jnp.bfloat16)
    query_grad, *kv_grads = attention_back(queries, key_valid, attn_seed, kv_blocks)
    kv_own = kv_grads[0].astype(jnp.float32)
    for j in range(1, peers):
        kv_own = kv_own + to_next(kv_grads[j], "seq", j).astype(jnp.float32)
    qkv_seed = jnp.concatenate([query_grad, kv_own.astype(jnp.bfloat16)], -1)
    qkv_grad = grad_dot(flat_in, qkv_seed)
    hidden_grad = (
        (grad_one + back_dot(qkv_seed, back_qkv))
        .astype(jnp.bfloat16)
        .reshape(seq_count, local_len, features)
    )
    input_mats, recur_sum, own_grad = gru_backward(
        flat_ids, charvec_grad, inward, recurrent, char_emb, *priors, *factors, *keeps, SUBV
    )
    table_grad = jnp.zeros(full_table.shape, jnp.bfloat16)
    table_grad = lax.dynamic_update_slice_in_dim(table_grad, own_grad.astype(jnp.bfloat16), table_start, 0)
    norm_grads = jnp.concatenate(
        [gain_one, gain_two, gain_three, bias_one, bias_two, bias_three, jnp.zeros((2, features), jnp.float32)], 0
    )
    terms = [input_mats, recur_sum, merge_grad, down_grad, up_grad, qkv_grad, out_grad, table_grad]
    parts = [x.astype(jnp.bfloat16).reshape(devices, -1, x.shape[-1]) for x in terms]
    width = norm_gain.shape[1]
    *sums, norm_sum = scatter_all(dp_size, parts, norm_grads, width)
    input_total, recur_total, merge_sum, down_sum, up_sum, qkv_sum, out_sum, table_sum = settle(sums)
    skip = me * width - window_start(me, width, features)
    gain_sum = lax.dynamic_slice(norm_sum, (0, skip), (3, width))
    bias_sum = lax.dynamic_slice(norm_sum, (3, skip), (3, width))
    return (result, hidden_grad, qkv_sum, out_sum, up_sum, down_sum, gain_sum, bias_sum, table_sum, input_total, recur_total, merge_sum, conv_sum)


def solution(mesh):
    placed = (
        P("dp", "seq", None),
        P("dp", "seq", None),
        P("dp"),
        P("dp"),
        P("dp", "seq", None),
        P(("dp", "seq"), None),
        P(("dp", "seq"), None),
        P(("dp", "seq"), None),
        P(("dp", "seq"), None),
        P(None, ("dp", "seq")),
        P(None, ("dp", "seq")),
        P(("dp", "seq"), None),
        P(("dp", "seq"), None),
        P(("dp", "seq"), None),
        P(("dp", "seq"), None),
        P(("dp", "seq"), None),
    )
    return jax.shard_map(
        local,
        mesh=mesh,
        in_specs=placed,
        out_specs=(
            P("dp", "seq", None),
            P("dp", "seq", None),
            P(("dp", "seq"), None),
            P(("dp", "seq"), None),
            P(("dp", "seq"), None),
            P(("dp", "seq"), None),
            P(None, ("dp", "seq")),
            P(None, ("dp", "seq")),
            P(("dp", "seq"), None),
            P(("dp", "seq"), None),
            P(("dp", "seq"), None),
            P(("dp", "seq"), None),
            P(("dp", "seq"), None),
        ),
        check_vma=False,
    )
```

```python
import functools
import math

import jax
import jax.numpy as jnp
from jax import lax
from jax.experimental import pallas as pl
from jax.experimental.pallas import tpu as pltpu
from jax.sharding import PartitionSpec as P

MESH = pl.DeviceIdType.MESH

HD = 64
SUBV = 128

eps = 1e-05

class Place:
    def __init__(self, dp_size):
        dp, seq = lax.axis_index("dp"), lax.axis_index("seq")
        self.lines = dp_size // 2
        self.a, self.b = dp // 2, lax.rem(dp, 2)
        self.y, self.c = seq // 2, lax.rem(seq, 2)
        flip_b = (self.a * 2 + 1 - self.b, seq)
        flip_y = (dp, (1 - self.y) * 2 + self.c)
        pick = lambda u, v: tuple(i + self.c * (j - i) for i, j in zip(u, v))
        self.first, self.second = pick(flip_b, flip_y), pick(flip_y, flip_b)
        self.sibling = (dp, self.y * 2 + 1 - self.c)
        self.up, self.down = (dp + 2, seq), (dp - 2, seq)
        self.f = self.b + self.c * (self.y - self.b)
        self.s = self.y + self.c * (self.b - self.y)
        self.has_up, self.has_down = self.a < self.lines - 1, self.a > 0

    def unit(self, a, f, s, c=None):
        c = self.c if c is None else c
        return a * 8 + f * (4 - 2 * c) + s * (2 + 2 * c) + c

    def barrier(self):
        sem = pltpu.get_barrier_semaphore()
        for who in (self.first, self.second, self.sibling):
            pl.semaphore_signal(sem, inc=1, device_id=who, device_id_type=MESH)

        @pl.when(self.has_up)
        def _():
            pl.semaphore_signal(sem, inc=1, device_id=self.up, device_id_type=MESH)

        @pl.when(self.has_down)
        def _():
            pl.semaphore_signal(sem, inc=1, device_id=self.down, device_id_type=MESH)

        pl.semaphore_wait(sem, 3 + self.has_up.astype(jnp.int32) + self.has_down.astype(jnp.int32))


def push(src, dst, send, recv, who):
    return pltpu.make_async_remote_copy(
        src_ref=src, dst_ref=dst, send_sem=send, recv_sem=recv, device_id=who, device_id_type=MESH
    )


class Gather:
    def __init__(self, at, shard, full, sems):
        self.at, self.shard, self.full = at, shard, full
        self.up_s, self.down_s, self.sum_s, self.line_r, self.second_r, self.one = sems

    def to_lines(self, src, slot, index, up, down):
        at = self.at
        if up is not False:
            @pl.when(at.has_up if up is True else jnp.logical_and(up, at.has_up))
            def _():
                push(src, self.full.at[index], self.up_s.at[slot], self.line_r.at[slot], at.up).start()
        if down is not False:
            @pl.when(at.has_down if down is True else jnp.logical_and(down, at.has_down))
            def _():
                push(src, self.full.at[index], self.down_s.at[slot], self.line_r.at[slot], at.down).start()

    def across(self, src, slot, index):
        push(src, self.full.at[index], self.sum_s.at[0], self.second_r.at[slot], self.at.second).start()
        self.aside(src, index)

    def aside(self, src, index):
        push(src, self.full.at[index], self.sum_s.at[1], self.one.at[1], self.at.sibling).start()

    def begin(self):
        at = self.at
        me = at.unit(at.a, at.f, at.s)
        pltpu.make_async_copy(self.shard, self.full.at[me], self.one.at[3]).start()
        push(self.shard, self.full.at[me], self.one.at[2], self.one.at[0], at.first).start()
        slot = at.a * 2 + at.f
        self.to_lines(self.shard, slot, me, True, True)
        self.across(self.shard, slot, me)

    def after_first(self):
        at = self.at
        index = at.unit(at.a, 1 - at.f, at.s)
        ref = self.full.at[index]
        push(ref, ref, self.one.at[2], self.one.at[0], at.first).wait_recv()
        slot = at.a * 2 + 1 - at.f
        self.to_lines(ref, slot, index, True, True)
        self.across(ref, slot, index)

    def after_line(self, k, g):
        at = self.at
        for sign in (-1, 1):
            a = at.a + sign * k
            f = at.f if g == 0 else 1 - at.f

            @pl.when(a >= 0 if sign < 0 else a < at.lines)
            def _():
                index, slot = at.unit(a, f, at.s), a * 2 + f
                ref = self.full.at[index]
                push(ref, ref, self.up_s.at[slot], self.line_r.at[slot], at.up).wait_recv()
                self.to_lines(ref, slot, index, sign < 0, sign > 0)
                self.across(ref, slot, index)

    def after_second(self, k, g):
        at = self.at
        for sign in (-1, 1) if k else (1,):
            a = at.a + sign * k
            f = at.f if g == 0 else 1 - at.f

            @pl.when(a >= 0 if sign < 0 else a < at.lines)
            def _():
                index, slot = at.unit(a, f, 1 - at.s), a * 2 + f
                ref = self.full.at[index]
                push(ref, ref, self.sum_s.at[0], self.second_r.at[slot], at.second).wait_recv()
                self.aside(ref, index)

    def finish(self):
        at, n = self.at, self.at.lines
        me = at.unit(at.a, at.f, at.s)
        half = self.full.at[pl.ds(0, 4 * n)]
        push(half, half, self.sum_s.at[1], self.one.at[1], at.sibling).wait_recv()
        pltpu.make_async_copy(self.shard, self.full.at[me], self.one.at[3]).wait()
        push(self.shard, self.full.at[me], self.one.at[2], self.one.at[0], at.first).wait_send()
        push(half, half, self.sum_s.at[1], self.one.at[1], at.sibling).wait_send()
        part = self.full.at[pl.ds(0, 2 * n)]
        push(part, part, self.sum_s.at[0], self.one.at[0], at.second).wait_send()
        for a in range(n):
            for f in range(2):
                slot = a * 2 + f
                ref = self.full.at[0]

                @pl.when(jnp.logical_and(at.has_up, a <= at.a))
                def _():
                    push(ref, ref, self.up_s.at[slot], self.line_r.at[slot], at.up).wait_send()

                @pl.when(jnp.logical_and(at.has_down, a >= at.a))
                def _():
                    push(ref, ref, self.down_s.at[slot], self.line_r.at[slot], at.down).wait_send()


class LineGather(Gather):
    def begin(self):
        at = self.at
        me = at.unit(at.a, at.f, at.s)
        pltpu.make_async_copy(self.shard, self.full.at[me], self.one.at[3]).start()
        self.to_lines(self.shard, at.a, me, True, True)
        self.to_pairs(self.shard, at.a, me)

    def to_pairs(self, src, a, index):
        at = self.at
        push(src, self.full.at[index], self.one.at[2], self.line_r.at[at.lines + a], at.first).start()
        self.across(src, a * 2 + at.f, index)

    def after_first(self):
        self.from_first(0)

    def from_first(self, k):
        at = self.at
        for sign in (-1, 1) if k else (1,):
            a = at.a + sign * k

            @pl.when(a >= 0 if sign < 0 else a < at.lines)
            def _():
                index = at.unit(a, 1 - at.f, at.s)
                ref = self.full.at[index]
                push(ref, ref, self.one.at[2], self.line_r.at[at.lines + a], at.first).wait_recv()
                self.across(ref, a * 2 + 1 - at.f, index)

    def after_line(self, k, g):
        at = self.at
        if g:
            self.from_first(k)
            return
        for sign in (-1, 1):
            a = at.a + sign * k

            @pl.when(a >= 0 if sign < 0 else a < at.lines)
            def _():
                index = at.unit(a, at.f, at.s)
                ref = self.full.at[index]
                push(ref, ref, self.up_s.at[a], self.line_r.at[a], at.up).wait_recv()
                self.to_lines(ref, a, index, sign < 0, sign > 0)
                self.to_pairs(ref, a, index)

    def finish(self):
        at, n = self.at, self.at.lines
        me = at.unit(at.a, at.f, at.s)
        half = self.full.at[pl.ds(0, 4 * n)]
        push(half, half, self.sum_s.at[1], self.one.at[1], at.sibling).wait_recv()
        pltpu.make_async_copy(self.shard, self.full.at[me], self.one.at[3]).wait()
        push(half, half, self.sum_s.at[1], self.one.at[1], at.sibling).wait_send()
        line = self.full.at[pl.ds(0, n)]
        push(line, line, self.one.at[2], self.one.at[0], at.first).wait_send()
        part = self.full.at[pl.ds(0, 2 * n)]
        push(part, part, self.sum_s.at[0], self.one.at[0], at.second).wait_send()
        ref = self.full.at[0]
        for a in range(n):
            @pl.when(jnp.logical_and(at.has_up, a <= at.a))
            def _():
                push(ref, ref, self.up_s.at[a], self.line_r.at[a], at.up).wait_send()

            @pl.when(jnp.logical_and(at.has_down, a >= at.a))
            def _():
                push(ref, ref, self.down_s.at[a], self.line_r.at[a], at.down).wait_send()


def gather_sems(n):
    dma = pltpu.SemaphoreType.DMA
    return [dma((2 * n,)), dma((2 * n,)), dma((2,)), dma((2 * n,)), dma((2 * n,)), dma((4,))]


def gather_kernel(dp_size, count, early, *refs):
    shards, fulls, sems = refs[:count], refs[count : 2 * count], refs[2 * count :]
    at = Place(dp_size)
    at.barrier()
    kinds = [LineGather if i in early else Gather for i in range(count)]
    jobs = [kinds[i](at, shards[i], fulls[i], sems[6 * i : 6 * i + 6]) for i in range(count)]
    for job in jobs:
        job.begin()
    for job in jobs:
        job.after_first()
    for k in range(1, at.lines):
        for g in range(2):
            for job in jobs:
                job.after_line(k, g)
            for job in jobs:
                job.after_second(k - 1, g)
    for g in range(2):
        for job in jobs:
            job.after_second(at.lines - 1, g)
    for job in jobs:
        job.finish()


def gather_all(dp_size, devices, shards, early, cid=1):
    count = len(shards)
    return pl.pallas_call(
        functools.partial(gather_kernel, dp_size, count, early),
        out_shape=[jax.ShapeDtypeStruct((devices,) + x.shape, x.dtype) for x in shards],
        in_specs=[pl.BlockSpec(memory_space=pl.ANY)] * count,
        out_specs=[pl.BlockSpec(memory_space=pl.ANY)] * count,
        scratch_shapes=gather_sems(dp_size // 2) * count,
        compiler_params=pltpu.CompilerParams(collective_id=cid, has_side_effects=True),
    )(*shards)


def wide(x):
    return x.astype(jnp.float32)


def add_into(dst, src):
    dst[...] = dst[...] + src[...]


class Scatter:
    def __init__(self, at, part, out, bufs, sems):
        self.at, self.part, self.out = at, part, out
        self.own, self.sib, self.sec, self.line, self.fst = bufs
        self.per = 2
        self.one, self.line_s, self.line_r = sems

    def begin(self):
        at = self.at

        def body(j, carry):
            a, f, s = j // 4, lax.rem(j // 2, 2), lax.rem(j, 2)
            push(self.part(at.unit(a, f, s, 1 - at.c)), self.sib.at[j], self.one.at[0], self.one.at[1], at.sibling).start()
            return carry

        lax.fori_loop(0, 4 * at.lines, body, 0)

        def load(j, carry):
            a, f, s = j // 4, lax.rem(j // 2, 2), lax.rem(j, 2)
            pltpu.make_async_copy(self.part(at.unit(a, f, s)), self.own.at[j], self.one.at[2]).start()
            return carry

        lax.fori_loop(0, 4 * at.lines, load, 0)

    def after_sibling(self):
        at = self.at
        n = 2 * at.lines
        pltpu.make_async_copy(self.own, self.own, self.one.at[2]).wait()
        push(self.sib, self.sib, self.one.at[0], self.one.at[1], at.sibling).wait_recv()

        def far(q, carry):
            j = q * 2 + 1 - at.s
            add_into(self.own.at[j], self.sib.at[j])
            return carry

        def send(q, carry):
            push(self.own.at[q * 2 + 1 - at.s], self.sec.at[q], self.one.at[3], self.one.at[4], at.second).start()
            return carry

        def near(q, carry):
            j = q * 2 + at.s
            add_into(self.own.at[j], self.sib.at[j])
            return carry

        lax.fori_loop(0, n, far, 0)
        lax.fori_loop(0, n, send, 0)
        lax.fori_loop(0, n, near, 0)

    def after_second(self):
        at = self.at
        push(self.sec, self.sec, self.one.at[3], self.one.at[4], at.second).wait_recv()

        def body(q, carry):
            add_into(self.own.at[q * 2 + at.s], self.sec.at[q])
            return carry

        lax.fori_loop(0, 2 * at.lines, body, 0)

    def spot(self, q):
        return q * 2 + self.at.s

    def hop(self, low, high, inward, dst, extra):
        at = self.at
        has, who = (at.has_up, at.down) if dst < 0 else (at.has_down, at.up)

        def take(q, carry):
            push(self.line.at[q], self.line.at[q], self.line_s.at[q], self.line_r.at[q], who).wait_recv()
            add_into(self.own.at[self.spot(q)], self.line.at[q])
            return carry

        @pl.when(has)
        def _():
            lax.fori_loop(low, high, take, 0)

        def send(q, carry):
            per = self.per
            slot = q if dst < 0 else jnp.where(q // per == at.a + 1, per * at.lines + lax.rem(q, per), q)
            push(self.own.at[self.spot(q)], self.line.at[slot], self.line_s.at[q], self.line_r.at[slot], who).start()
            return carry

        lax.fori_loop(low, high, send, 0)

    def along(self, h):
        at = self.at
        n = at.lines
        hops = n - 1 if n <= 4 else 1

        @pl.when(jnp.logical_and(at.has_down, at.lines - 1 - at.a == h) if hops > 1 else at.has_down)
        def _():
            self.hop(0, self.per * at.a, at.up, -1, None)

        @pl.when(jnp.logical_and(at.has_up, at.a == h) if hops > 1 else at.has_up)
        def _():
            self.hop(self.per * (at.a + 1), self.per * n, at.down, 1, None)

    def ends(self, f, into):
        at = self.at
        for has, slot in ((at.has_up, 2 * at.a + f), (at.has_down, 2 * at.lines + f)):
            @pl.when(has)
            def _():
                ref = self.line.at[slot]
                push(ref, ref, self.line_s.at[0], self.line_r.at[slot], at.first).wait_recv()
                into[...] = (wide(into[...]) + wide(ref[...])).astype(into.dtype)

    def last_send(self):
        at = self.at
        mine = self.own.at[(2 * at.a + 1 - at.f) * 2 + at.s]
        self.ends(1 - at.f, mine)
        push(mine, self.fst, self.one.at[5], self.one.at[6], at.first).start()
        self.out[...] = wide(self.own[(2 * at.a + at.f) * 2 + at.s])
        self.ends(at.f, self.out)

    def finish(self):
        at = self.at
        push(self.fst, self.fst, self.one.at[5], self.one.at[6], at.first).wait_recv()
        self.out[...] = self.out[...] + wide(self.fst[...])

    def drain(self):
        at = self.at
        n = at.lines
        push(self.sib, self.sib, self.one.at[0], self.one.at[1], at.sibling).wait_send()
        push(self.sec, self.sec, self.one.at[3], self.one.at[4], at.second).wait_send()
        push(self.fst, self.fst, self.one.at[5], self.one.at[6], at.first).wait_send()

        def body(q, carry):
            @pl.when(q // self.per != at.a)
            def _():
                push(self.own.at[q], self.own.at[q], self.line_s.at[q], self.line_r.at[q], at.first).wait_send()
            return carry

        lax.fori_loop(0, self.per * n, body, 0)

    def stages(self):
        return [type(self).after_sibling, type(self).after_second] + self.hops() + [type(self).last_send, type(self).finish]

    def hops(self):
        lines = self.at.lines
        return [functools.partial(type(self).along, h=h) for h in range(lines - 1 if lines <= 4 else 1)]


class LineScatter(Scatter):
    def __init__(self, *args):
        super().__init__(*args)
        self.per = 1

    def spot(self, q):
        return (2 * q + self.at.f) * 2 + self.at.s

    def after_second(self):
        super().after_second()
        at = self.at

        def send(a, carry):
            push(self.own.at[(2 * a + 1 - at.f) * 2 + at.s], self.fst.at[a], self.one.at[5], self.one.at[6], at.first).start()
            return carry

        lax.fori_loop(0, at.lines, send, 0)

    def after_first(self):
        at = self.at
        push(self.fst, self.fst, self.one.at[5], self.one.at[6], at.first).wait_recv()

        def body(a, carry):
            add_into(self.own.at[self.spot(a)], self.fst.at[a])
            return carry

        lax.fori_loop(0, at.lines, body, 0)

    def finish(self):
        at = self.at
        self.out[...] = wide(self.own[self.spot(at.a)])
        for has, slot in ((at.has_up, at.a), (at.has_down, at.lines)):
            @pl.when(has)
            def _():
                ref = self.line.at[slot]
                push(ref, ref, self.line_s.at[0], self.line_r.at[slot], at.first).wait_recv()
                self.out[...] = self.out[...] + wide(ref[...])

    def stages(self):
        kind = type(self)
        return [kind.after_sibling, kind.after_second, kind.after_first] + self.hops() + [kind.finish]


def scatter_buffers(n, shape, dtype, late):
    v = lambda k: pltpu.VMEM((k,) + shape, dtype)
    return [v(4 * n), v(4 * n), v(2 * n)] + ([v(n + 1), v(n)] if late else [v(2 * n + 2), pltpu.VMEM(shape, dtype)])


def scatter_sems(n):
    dma = pltpu.SemaphoreType.DMA
    return [dma((7,)), dma((2 * n,)), dma((2 * n + 2,))]


LANES = 128
AHEAD = 2


def window_start(unit, width, features):
    tile = unit * width // LANES
    return (tile - tile // (features // LANES - 1)) * LANES


def whole_part(ref, rows, cols):
    return lambda unit: ref.at[unit, pl.ds(*rows), pl.ds(*cols)]


def window_part(ref, width):
    features = ref.shape[1]
    return lambda unit: ref.at[:, pl.ds(pl.multiple_of(window_start(unit, width, features), LANES), 2 * LANES)]


def cut(shape, cap):
    rows, cols = shape
    pieces = max(1, round(rows * cols / cap))
    while pieces > 1 and not (rows % (16 * pieces) == 0 or cols % (LANES * pieces) == 0):
        pieces -= 1
    if rows % (16 * pieces) == 0:
        step = rows // pieces
        return [((k * step, step), (0, cols)) for k in range(pieces)]
    step = cols // pieces
    return [((0, rows), (k * step, step)) for k in range(pieces)]


def weave(many, few):
    order, i, j = [], 0, 0
    while i < len(many) or j < len(few):
        if j < len(few) and (2 * j + 1) * len(many) <= (2 * i + 1) * len(few):
            order.append(few[j])
            j += 1
        else:
            order.append(many[i])
            i += 1
    return order


def scatter_kernel(dp_size, chunks, count, width, late, *refs):
    parts, outs, rest = refs[:count], refs[count : 2 * count], refs[2 * count :]
    at = Place(dp_size)
    at.barrier()
    jobs = []
    for k, (i, rows, cols) in enumerate(chunks):
        last = i == count - 1
        part = window_part(parts[i], width) if last else whole_part(parts[i], rows, cols)
        out = outs[i] if last else outs[i].at[pl.ds(*rows), pl.ds(*cols)]
        kind = LineScatter if i in late else Scatter
        jobs.append(kind(at, part, out, rest[8 * k : 8 * k + 5], rest[8 * k + 5 : 8 * k + 8]))
    total = len(jobs)
    for job in jobs[:AHEAD]:
        job.begin()
    stages = [job.stages() for job in jobs]
    depth = len(stages[0])
    for t in range(total + depth - 1):
        if t + AHEAD < total:
            jobs[t + AHEAD].begin()
        for k in range(depth):
            if 0 <= t - k < total:
                stages[t - k][k](jobs[t - k])
    for job in jobs:
        job.drain()


def scatter_all(dp_size, parts, norm_rows, width, late, cap=36864, cid=2):
    count = len(parts) + 1
    n = dp_size // 2
    outs = [jax.ShapeDtypeStruct(x.shape[1:], jnp.float32) for x in parts]
    outs.append(jax.ShapeDtypeStruct((norm_rows.shape[0], 2 * LANES), jnp.float32))
    pieces = [(i, *piece) for i, x in enumerate(parts) for piece in cut(x.shape[1:], cap)]
    chunks = weave([p for p in pieces if p[0] not in late], [p for p in pieces if p[0] in late])
    scratch = []
    for i, rows, cols in chunks:
        scratch += scatter_buffers(n, (rows[1], cols[1]), parts[i].dtype, i in late) + scatter_sems(n)
    chunks.append((count - 1, None, None))
    scratch += scatter_buffers(n, outs[-1].shape, jnp.float32, count - 1 in late) + scatter_sems(n)
    return pl.pallas_call(
        functools.partial(scatter_kernel, dp_size, chunks, count, width, late),
        out_shape=outs,
        in_specs=[pl.BlockSpec(memory_space=pl.ANY)] * count,
        out_specs=[pl.BlockSpec(memory_space=pltpu.VMEM)] * count,
        scratch_shapes=scratch,
        compiler_params=pltpu.CompilerParams(collective_id=cid, has_side_effects=True, vmem_limit_bytes=64000000),
    )(*parts, norm_rows)


def settle_kernel(*refs):
    half = len(refs) // 2
    for src, dst in zip(refs[:half], refs[half:]):
        dst[...] = src[...]


def settle(arrays):
    spec = [pl.BlockSpec(memory_space=pltpu.VMEM)] * len(arrays)
    return pl.pallas_call(
        settle_kernel,
        out_shape=[jax.ShapeDtypeStruct(x.shape, x.dtype) for x in arrays],
        in_specs=spec,
        out_specs=spec,
    )(*arrays)


def with_halo(x, sides, width):
    for axis, dim in sides:
        devices, length = (lax.axis_size(axis), x.shape[dim])
        up = [(i, (i + 1) % devices) for i in range(devices - 1)]
        down = [(j, i) for i, j in up]
        last = lax.slice_in_dim(x, length - width, length, axis=dim)
        first = lax.slice_in_dim(x, 0, width, axis=dim)
        before = lax.ppermute(last, axis, up)
        after = lax.ppermute(first, axis, down)
        x = jnp.concatenate([before, x, after], axis=dim)
    return x


def norm_rows(residual, row_gain, row_bias):
    centered = residual - jnp.mean(residual, axis=-1, keepdims=True)
    spread = jnp.mean(centered * centered, axis=-1, keepdims=True)
    return centered * lax.rsqrt(spread + eps) * row_gain + row_bias


def gelu_exact(pre_act):
    return jax.nn.gelu(pre_act, approximate=False)


def plain_dot(left, right):
    return jnp.dot(left, right, preferred_element_type=jnp.float32)


def grad_dot(left, right):
    return lax.dot_general(
        left, right, (((0,), (0,)), ((), ())), preferred_element_type=jnp.float32
    )


def back_dot(left, right):
    return lax.dot_general(
        left, right, (((1,), (1,)), ((), ())), preferred_element_type=jnp.float32
    )


def squash(x):
    return 0.5 * jnp.tanh(0.5 * x) + 0.5


def slot_onehot(ids, slots, subset):
    cols = lax.broadcasted_iota(jnp.int32, (ids.shape[0], subset), 1)
    hots = [(ids[:, s : s + 1] == cols).astype(jnp.bfloat16) for s in slots]
    return jnp.concatenate(hots, 0)


def gru_embed(ids_ref, table, w_in, emb_ref, gates, chunk=4):
    rows, nchar = ids_ref.shape
    ids = ids_ref[...]
    for k in range(0, nchar, chunk):
        hot = slot_onehot(ids, range(k, k + chunk), table.shape[0])
        emb = plain_dot(hot, table[...]).astype(jnp.bfloat16)
        emb_ref[k : k + chunk] = emb.reshape(chunk, rows, -1)
        for d in range(2):
            gates[d, k : k + chunk] = plain_dot(emb, w_in[d]).reshape(chunk, rows, -1)


def gru_step(d, slot, count, gates, w_rec, state, factor, keep, prior):
    units = state.shape[2]
    old = state[d]
    low = old.astype(jnp.bfloat16)
    rec = plain_dot(low, w_rec[d])
    gi = gates[d, slot]
    reset = squash(gi[:, :units] + rec[:, :units])
    update = squash(gi[:, units : 2 * units] + rec[:, units : 2 * units])
    rec_n = rec[:, 2 * units :]
    cand = jnp.tanh(gi[:, 2 * units :] + reset * rec_n)
    live = slot < count
    state[d] = jnp.where(live, (1.0 - update) * cand + update * old, old)
    by_cand = jnp.where(live, (1.0 - update) * (1.0 - cand * cand), 0.0)
    by_update = jnp.where(live, (old - cand) * update * (1.0 - update), 0.0)
    by_reset = by_cand * rec_n * reset * (1.0 - reset)
    prior[...] = low
    keep[...] = jnp.where(live, update, 1.0)
    for k, x in enumerate((by_reset, by_update, by_cand, reset)):
        factor[:, k * units : (k + 1) * units] = x.astype(factor.dtype)


def gru_forward_kernel(ids_ref, table, w_in, w_rec, vec, emb, f0, f1, z0, z1, h0, h1, gates, state):
    i = pl.program_id(0)
    nchar = pl.num_programs(0)

    @pl.when(i == 0)
    def _():
        gru_embed(ids_ref, table, w_in, emb, gates)
        state[...] = jnp.zeros_like(state)

    count = jnp.sum((ids_ref[...] > 0).astype(jnp.int32), axis=1, keepdims=True)
    gru_step(0, i, count, gates, w_rec, state, f0.at[0], z0.at[0], h0.at[0])
    gru_step(1, nchar - 1 - i, count, gates, w_rec, state, f1.at[0], z1.at[0], h1.at[0])

    @pl.when(i == nchar - 1)
    def _():
        units = state.shape[2]
        vec[:, :units] = state[0].astype(vec.dtype)
        vec[:, units:] = state[1].astype(vec.dtype)


def slot_specs(nchar, rows, cols, backward):
    up = pl.BlockSpec((1, rows, cols), lambda i: (i, 0, 0))
    down = pl.BlockSpec((1, rows, cols), lambda i: (nchar - 1 - i, 0, 0))
    return [down, up] if backward else [up, down]


def gru_cost(nchar, rows, width, units, products):
    steps = 2 * nchar * rows
    return pl.CostEstimate(
        flops=12 * products * steps * (width + units) * units,
        bytes_accessed=16 * steps * units,
        transcendentals=3 * steps * units,
    )


def gru_forward(ids, table, w_in, w_rec):
    rows, nchar = ids.shape
    width, units = table.shape[1], w_rec.shape[1]
    whole = lambda shape: pl.BlockSpec(shape, lambda i: (0,) * len(shape))
    slots = functools.partial(slot_specs, nchar, rows, backward=False)
    shape = jax.ShapeDtypeStruct
    factor = shape((nchar, rows, 4 * units), jnp.bfloat16)
    keep = shape((nchar, rows, units), jnp.float32)
    prior = shape((nchar, rows, units), jnp.bfloat16)
    return pl.pallas_call(
        gru_forward_kernel,
        grid=(nchar,),
        out_shape=[
            shape((rows, 2 * units), jnp.bfloat16),
            shape((nchar, rows, width), jnp.bfloat16),
            factor, factor, keep, keep, prior, prior,
        ],
        in_specs=[whole(x.shape) for x in (ids, table, w_in, w_rec)],
        out_specs=[whole((rows, 2 * units)), whole((nchar, rows, width))]
        + slots(4 * units) + slots(units) + slots(units),
        scratch_shapes=[
            pltpu.VMEM((2, nchar, rows, 3 * units), jnp.float32),
            pltpu.VMEM((2, rows, units), jnp.float32),
        ],
        compiler_params=pltpu.CompilerParams(vmem_limit_bytes=60000000),
        cost_estimate=gru_cost(nchar, rows, width, units, 1),
    )(ids, table, w_in, w_rec)


def gru_back_step(d, slot, factor, keep, w_rec, grad, seeds):
    units = grad.shape[2]
    g = grad[d]
    part = lambda k: factor[:, k * units : (k + 1) * units].astype(jnp.float32)
    by_cand = g * part(2)
    seeds[d, slot, :, :units] = (g * part(0)).astype(seeds.dtype)
    seeds[d, slot, :, units : 2 * units] = (g * part(1)).astype(seeds.dtype)
    seeds[d, slot, :, 2 * units : 3 * units] = (by_cand * part(3)).astype(seeds.dtype)
    seeds[d, slot, :, 3 * units :] = by_cand.astype(seeds.dtype)
    grad[d] = g * keep[...] + back_dot(seeds[d, slot, :, : 3 * units], w_rec[d])


def gru_weight_grads(d, seeds, emb, prior, d_in, d_rec):
    _, nchar, rows, wide = seeds.shape
    units = wide // 4
    states = prior[...].reshape(nchar * rows, units)
    chars = emb[...].reshape(nchar * rows, -1)
    col = lambda k: seeds[d, :, :, k * units : (k + 1) * units].reshape(nchar * rows, units)
    for k in range(3):
        d_rec[d, :, k * units : (k + 1) * units] = grad_dot(states, col(k)).astype(d_rec.dtype)
        own = col(3 if k == 2 else k)
        d_in[d, :, k * units : (k + 1) * units] = grad_dot(chars, own).astype(d_in.dtype)


def gru_char_grads(ids_ref, seeds, w_in, d_table, chunk=4):
    _, nchar, rows, wide = seeds.shape
    units = wide // 4
    ids = ids_ref[...]
    total = jnp.zeros(d_table.shape, jnp.float32)
    for k in range(0, nchar, chunk):
        grad = None
        for d in range(2):
            both = seeds[d, k : k + chunk].reshape(chunk * rows, wide)
            part = back_dot(both[:, : 2 * units], w_in[d][:, : 2 * units])
            part = part + back_dot(both[:, 3 * units :], w_in[d][:, 2 * units :])
            grad = part if grad is None else grad + part
        hot = slot_onehot(ids, range(k, k + chunk), d_table.shape[0])
        total = total + grad_dot(hot, grad.astype(jnp.bfloat16))
    d_table[...] = total


def gru_backward_kernel(ids_ref, seed, w_in, w_rec, emb, h0, h1, f0, f1, z0, z1, d_in, d_rec, d_table, grad, seeds):
    i = pl.program_id(0)
    nchar = pl.num_programs(0)

    @pl.when(i == 0)
    def _():
        units = grad.shape[2]
        grad[0] = seed[:, :units]
        grad[1] = seed[:, units:]

    gru_back_step(0, nchar - 1 - i, f0.at[0], z0.at[0], w_rec, grad, seeds)
    gru_back_step(1, i, f1.at[0], z1.at[0], w_rec, grad, seeds)

    @pl.when(i == nchar - 1)
    def _():
        gru_weight_grads(0, seeds, emb, h0, d_in, d_rec)
        gru_weight_grads(1, seeds, emb, h1, d_in, d_rec)
        gru_char_grads(ids_ref, seeds, w_in, d_table)


def gru_backward(ids, seed, w_in, w_rec, emb, h0, h1, f0, f1, z0, z1, subset):
    nchar, rows, width = emb.shape
    units = w_rec.shape[1]
    whole = lambda shape: pl.BlockSpec(shape, lambda i: (0,) * len(shape))
    slots = functools.partial(slot_specs, nchar, rows, backward=True)
    shape = jax.ShapeDtypeStruct
    return pl.pallas_call(
        gru_backward_kernel,
        grid=(nchar,),
        out_shape=[
            shape(w_in.shape, jnp.bfloat16),
            shape(w_rec.shape, jnp.bfloat16),
            shape((subset, width), jnp.float32),
        ],
        in_specs=[whole(x.shape) for x in (ids, seed, w_in, w_rec, emb, h0, h1)] + slots(4 * units) + slots(units),
        out_specs=[whole(w_in.shape), whole(w_rec.shape), whole((subset, width))],
        scratch_shapes=[
            pltpu.VMEM((2, rows, units), jnp.float32),
            pltpu.VMEM((2, nchar, rows, 4 * units), jnp.bfloat16),
        ],
        compiler_params=pltpu.CompilerParams(vmem_limit_bytes=60000000),
        cost_estimate=gru_cost(nchar, rows, width, units, 2),
    )(ids, seed, w_in, w_rec, emb, h0, h1, f0, f1, z0, z1)


def head_pair(q_ref, blocks, valid, pair, half):
    features = q_ref.shape[1]
    cols = pl.ds(pair * 2 * HD, 2 * HD)
    queries = q_ref[:, cols]
    keys = jnp.concatenate([b[:, cols] for b in blocks], 0)
    values = jnp.concatenate([b[:, pl.ds(features + pair * 2 * HD, 2 * HD)] for b in blocks], 0)
    scores = back_dot(one_head(queries, half), keys) * (1.0 / math.sqrt(HD))
    scores = jnp.where(valid, scores, -1000000000.0)
    weight = jnp.exp(scores - jnp.max(scores, axis=-1, keepdims=True))
    return weight / jnp.sum(weight, axis=-1, keepdims=True), queries, keys, values


def first_lanes(shape):
    return lax.broadcasted_iota(jnp.int32, shape, 1) < HD


def one_head(x, half):
    keep = first_lanes(x.shape) if half == 0 else jnp.logical_not(first_lanes(x.shape))
    return jnp.where(keep, x, jnp.zeros_like(x))


def side_by_side(left, right):
    return jnp.where(first_lanes(left.shape), left, right)


def attention_kernel(count, q_ref, valid_ref, *refs):
    blocks, out = refs[:count], refs[count]
    valid = jnp.broadcast_to(valid_ref[...] > 0, (q_ref.shape[0], valid_ref.shape[1]))
    for pair in range(q_ref.shape[1] // (2 * HD)):
        both = []
        for half in range(2):
            probs, _, _, values = head_pair(q_ref, blocks, valid, pair, half)
            both.append(plain_dot(probs.astype(jnp.bfloat16), values))
        out[:, pl.ds(pair * 2 * HD, 2 * HD)] = side_by_side(*both).astype(out.dtype)


def attention_back_kernel(count, q_ref, valid_ref, seed_ref, *refs):
    blocks, q_out, outs = refs[:count], refs[count], refs[count + 1 :]
    rows, features = q_ref.shape
    scale = 1.0 / math.sqrt(HD)
    valid = jnp.broadcast_to(valid_ref[...] > 0, (rows, valid_ref.shape[1]))
    for pair in range(features // (2 * HD)):
        cols = pl.ds(pair * 2 * HD, 2 * HD)
        seed = seed_ref[:, cols]
        q_both, k_both, v_both = [], [], []
        for half in range(2):
            probs, queries, keys, values = head_pair(q_ref, blocks, valid, pair, half)
            probs_grad = back_dot(one_head(seed, half), values)
            inner = jnp.sum(probs * probs_grad, axis=-1, keepdims=True)
            score_grad = (probs * (probs_grad - inner)).astype(jnp.bfloat16)
            q_both.append(plain_dot(score_grad, keys))
            k_both.append(grad_dot(score_grad, queries))
            v_both.append(grad_dot(probs.astype(jnp.bfloat16), seed))
        q_out[:, cols] = (side_by_side(*q_both) * scale).astype(q_out.dtype)
        k_grad = (side_by_side(*k_both) * scale).astype(jnp.bfloat16)
        v_grad = side_by_side(*v_both).astype(jnp.bfloat16)
        for j, out in enumerate(outs):
            out[:, cols] = k_grad[j * rows : (j + 1) * rows]
            out[:, pl.ds(features + pair * 2 * HD, 2 * HD)] = v_grad[j * rows : (j + 1) * rows]


def attention_cost(rows, blocks, features, products):
    span = rows * len(blocks)
    return pl.CostEstimate(
        flops=2 * products * rows * span * features,
        bytes_accessed=8 * span * features,
        transcendentals=rows * span * (features // HD),
    )


def attention(queries, valid, blocks):
    rows, features = queries.shape
    vmem = pl.BlockSpec(memory_space=pltpu.VMEM)
    return pl.pallas_call(
        functools.partial(attention_kernel, len(blocks)),
        out_shape=jax.ShapeDtypeStruct((rows, features), jnp.bfloat16),
        in_specs=[vmem] * (2 + len(blocks)),
        out_specs=vmem,
        cost_estimate=attention_cost(rows, blocks, features, 2),
    )(queries, valid, *blocks)


def attention_back(queries, valid, seed, blocks):
    rows, features = queries.shape
    vmem = pl.BlockSpec(memory_space=pltpu.VMEM)
    return pl.pallas_call(
        functools.partial(attention_back_kernel, len(blocks)),
        out_shape=[jax.ShapeDtypeStruct((rows, features), jnp.bfloat16)]
        + [jax.ShapeDtypeStruct((rows, 2 * features), jnp.bfloat16)] * len(blocks),
        in_specs=[vmem] * (3 + len(blocks)),
        out_specs=[vmem] * (1 + len(blocks)),
        cost_estimate=attention_cost(rows, blocks, features, 5),
    )(queries, valid, seed, *blocks)


def from_next(x, axis, step):
    size = lax.axis_size(axis)
    return lax.ppermute(x, axis, [((i + step) % size, i) for i in range(size)])


def to_next(x, axis, step):
    size = lax.axis_size(axis)
    return lax.ppermute(x, axis, [(i, (i + step) % size) for i in range(size)])


def norm_back(residual, row_gain, seed):
    centered = residual - jnp.mean(residual, axis=-1, keepdims=True)
    spread = jnp.mean(centered * centered, axis=-1, keepdims=True)
    scale = lax.rsqrt(spread + eps)
    unit = centered * scale
    inner = seed * row_gain
    drop = jnp.mean(inner, axis=-1, keepdims=True) + unit * jnp.mean(inner * unit, axis=-1, keepdims=True)
    gain_grad = jnp.sum(seed * unit, axis=0, keepdims=True)
    return scale * (inner - drop), gain_grad, jnp.sum(seed, axis=0, keepdims=True)


def place_norms(gain, bias, index, devices):
    both = jnp.concatenate([gain, bias], 0)
    width = both.shape[1]
    shape = (width, devices * width)
    spot = lax.broadcasted_iota(jnp.int32, shape, 0) + index * width == lax.broadcasted_iota(jnp.int32, shape, 1)
    placed = plain_dot(both, spot.astype(both.dtype)).astype(both.dtype)
    return jnp.pad(placed, ((0, 8 - both.shape[0]), (0, 0)))


def local(
    hidden,
    char_ids,
    groups,
    lengths,
    cotangent,
    qkv_weight,
    out_weight,
    up_weight,
    down_weight,
    norm_gain,
    norm_bias,
    char_table,
    gru_input,
    gru_recur,
    merge_weight,
    conv_weight,
):
    dp_size, devices = lax.axis_size("dp"), lax.axis_size("dp") * lax.axis_size("seq")
    me = lax.axis_index("dp") * lax.axis_size("seq") + lax.axis_index("seq")
    norms = place_norms(norm_gain, norm_bias, me, devices)
    order = (char_table, gru_input, gru_recur, norms, qkv_weight, out_weight, up_weight, down_weight, merge_weight, conv_weight)
    gathered = gather_all(dp_size, devices, order, (2, 9))
    all_norms = jnp.sum(gathered[3].astype(jnp.float32), axis=0)
    (full_table, full_input, full_recur, _, full_qkv, full_out, full_up, full_down, full_merge, full_conv) = [
        x.reshape(-1, x.shape[2]) for x in gathered
    ]
    seq_count, local_len, features = hidden.shape
    nchar = char_ids.shape[2]
    tokens = seq_count * local_len
    key_span = local_len * lax.axis_size("seq")
    gains = [all_norms[k : k + 1] for k in range(3)]
    biases = [all_norms[k : k + 1] for k in range(3, 6)]
    flat_in = hidden.reshape(tokens, features)
    qkv = plain_dot(flat_in, full_qkv).astype(jnp.bfloat16)
    queries, own_kv = qkv[:, :features], qkv[:, features:]
    peers = lax.axis_size("seq")
    kv_blocks = [own_kv] + [from_next(own_kv, "seq", j) for j in range(1, peers)]
    place = lax.rem(lax.axis_index("seq") + jnp.arange(peers), peers) * local_len
    positions = place[:, None] + jnp.arange(local_len)[None, :]
    key_valid = (positions < lengths[0]).astype(jnp.int32).reshape(1, key_span)
    assert seq_count == 1
    flat_ids = char_ids.reshape(tokens, nchar)
    table_start = groups[0] * SUBV
    own_table = lax.dynamic_slice_in_dim(full_table, table_start, SUBV, 0)
    inward = full_input.reshape(2, -1, full_input.shape[1])
    recurrent = full_recur.reshape(2, -1, full_recur.shape[1])
    char_vec, char_emb, *kept = gru_forward(flat_ids, own_table, inward, recurrent)
    factors, keeps, priors = kept[:2], kept[2:4], kept[4:]
    attended = attention(queries, key_valid, kv_blocks)
    resid_one = flat_in.astype(jnp.float32) + plain_dot(attended, full_out)
    norm_one = norm_rows(resid_one, gains[0], biases[0]).astype(jnp.bfloat16)
    up_proj = plain_dot(norm_one, full_up)
    active = gelu_exact(up_proj).astype(jnp.bfloat16)
    resid_two = norm_one.astype(jnp.float32) + plain_dot(active, full_down)
    norm_two = norm_rows(resid_two, gains[1], biases[1]).astype(jnp.bfloat16)
    merge_mats = full_merge.reshape(2, features, features)
    streams = jnp.stack([norm_two, char_vec], 0)
    merged_pair = jnp.einsum("btd,bdf->btf", streams, merge_mats, preferred_element_type=jnp.float32)
    merged_rows = jnp.concatenate([merged_pair[0], merged_pair[1]], -1).astype(jnp.bfloat16)
    padded = with_halo(merged_rows.reshape(seq_count, local_len, 2 * features), (("seq", 1),), 1)
    kernel = full_conv.reshape(3, 2 * features, features)
    windows = [
        padded[:, offset : offset + local_len].reshape(tokens, 2 * features) for offset in range(3)
    ]
    conv_out = (
        plain_dot(windows[0], kernel[0])
        + plain_dot(windows[1], kernel[1])
        + plain_dot(windows[2], kernel[2])
    )
    resid_three = norm_two.astype(jnp.float32) + conv_out
    result = norm_rows(resid_three, gains[2], biases[2]).astype(jnp.bfloat16).reshape(seq_count, local_len, features)
    back_qkv, back_out, back_up, back_down = full_qkv, full_out, full_up, full_down
    back_merge, back_conv = full_merge, full_conv
    merge_back = back_merge.reshape(2, features, features)
    kernel_back = back_conv.reshape(3, 2 * features, features)
    seed_rows = cotangent.reshape(tokens, features).astype(jnp.float32)
    grad_three, gain_three, bias_three = norm_back(resid_three, gains[2], seed_rows)
    conv_seed = grad_three.astype(jnp.bfloat16)
    conv_grad = grad_dot(jnp.concatenate(windows, 1), conv_seed)
    seed_padded = with_halo(conv_seed.reshape(seq_count, local_len, features), (("seq", 1),), 1)
    merged_grad = back_dot(
        seed_padded[:, 2 : 2 + local_len].reshape(tokens, features), kernel_back[0]
    )
    merged_grad = merged_grad + back_dot(
        seed_padded[:, 1 : 1 + local_len].reshape(tokens, features), kernel_back[1]
    )
    merged_grad = merged_grad + back_dot(
        seed_padded[:, 0:local_len].reshape(tokens, features), kernel_back[2]
    )
    merged_grad = merged_grad.astype(jnp.bfloat16)
    pair_grad = jnp.stack([merged_grad[:, :features], merged_grad[:, features:]], 0)
    merge_grad = jnp.einsum("btd,btf->bdf", streams, pair_grad, preferred_element_type=jnp.float32)
    stream_grad = jnp.einsum("btf,bdf->btd", pair_grad, merge_back, preferred_element_type=jnp.float32)
    two_grad = grad_three + stream_grad[0]
    charvec_grad = stream_grad[1]
    grad_two, gain_two, bias_two = norm_back(resid_two, gains[1], two_grad)
    down_seed = grad_two.astype(jnp.bfloat16)
    down_grad = grad_dot(active, down_seed)
    active_grad = back_dot(down_seed, back_down)
    _, pull_gelu = jax.vjp(gelu_exact, up_proj)
    up_seed = pull_gelu(active_grad)[0].astype(jnp.bfloat16)
    up_grad = grad_dot(norm_one, up_seed)
    one_grad = grad_two + back_dot(up_seed, back_up)
    grad_one, gain_one, bias_one = norm_back(resid_one, gains[0], one_grad)
    out_seed = grad_one.astype(jnp.bfloat16)
    out_grad = grad_dot(attended, out_seed)
    attn_seed = back_dot(out_seed, back_out).astype(jnp.bfloat16)
    query_grad, *kv_grads = attention_back(queries, key_valid, attn_seed, kv_blocks)
    kv_own = kv_grads[0].astype(jnp.float32)
    for j in range(1, peers):
        kv_own = kv_own + to_next(kv_grads[j], "seq", j).astype(jnp.float32)
    qkv_seed = jnp.concatenate([query_grad, kv_own.astype(jnp.bfloat16)], -1)
    qkv_grad = grad_dot(flat_in, qkv_seed)
    hidden_grad = (
        (grad_one + back_dot(qkv_seed, back_qkv))
        .astype(jnp.bfloat16)
        .reshape(seq_count, local_len, features)
    )
    input_mats, recur_sum, own_grad = gru_backward(
        flat_ids, charvec_grad, inward, recurrent, char_emb, *priors, *factors, *keeps, SUBV
    )
    table_grad = jnp.zeros(full_table.shape, jnp.bfloat16)
    table_grad = lax.dynamic_update_slice_in_dim(table_grad, own_grad.astype(jnp.bfloat16), table_start, 0)
    norm_grads = jnp.concatenate(
        [gain_one, gain_two, gain_three, bias_one, bias_two, bias_three, jnp.zeros((2, features), jnp.float32)], 0
    )
    terms = [input_mats, recur_sum, merge_grad, conv_grad, down_grad, up_grad, qkv_grad, out_grad, table_grad]
    parts = [x.astype(jnp.bfloat16).reshape(devices, -1, x.shape[-1]) for x in terms]
    width = norm_gain.shape[1]
    *sums, norm_sum = scatter_all(dp_size, parts, norm_grads, width, (1, 3))
    input_total, recur_total, merge_sum, conv_sum, down_sum, up_sum, qkv_sum, out_sum, table_sum = settle(sums)
    skip = me * width - window_start(me, width, features)
    gain_sum = lax.dynamic_slice(norm_sum, (0, skip), (3, width))
    bias_sum = lax.dynamic_slice(norm_sum, (3, skip), (3, width))
    return (result, hidden_grad, qkv_sum, out_sum, up_sum, down_sum, gain_sum, bias_sum, table_sum, input_total, recur_total, merge_sum, conv_sum)


def solution(mesh):
    placed = (
        P("dp", "seq", None),
        P("dp", "seq", None),
        P("dp"),
        P("dp"),
        P("dp", "seq", None),
        P(("dp", "seq"), None),
        P(("dp", "seq"), None),
        P(("dp", "seq"), None),
        P(("dp", "seq"), None),
        P(None, ("dp", "seq")),
        P(None, ("dp", "seq")),
        P(("dp", "seq"), None),
        P(("dp", "seq"), None),
        P(("dp", "seq"), None),
        P(("dp", "seq"), None),
        P(("dp", "seq"), None),
    )
    return jax.shard_map(
        local,
        mesh=mesh,
        in_specs=placed,
        out_specs=(
            P("dp", "seq", None),
            P("dp", "seq", None),
            P(("dp", "seq"), None),
            P(("dp", "seq"), None),
            P(("dp", "seq"), None),
            P(("dp", "seq"), None),
            P(None, ("dp", "seq")),
            P(None, ("dp", "seq")),
            P(("dp", "seq"), None),
            P(("dp", "seq"), None),
            P(("dp", "seq"), None),
            P(("dp", "seq"), None),
            P(("dp", "seq"), None),
        ),
        check_vma=False,
    )
```

```python
import functools
import math

import jax
import jax.numpy as jnp
from jax import lax
from jax.experimental import pallas as pl
from jax.experimental.pallas import tpu as pltpu
from jax.sharding import PartitionSpec as P

MESH = pl.DeviceIdType.MESH

HD = 64
SUBV = 128

eps = 1e-05

class Place:
    def __init__(self, dp_size):
        dp, seq = lax.axis_index("dp"), lax.axis_index("seq")
        self.lines = dp_size // 2
        self.a, self.b = dp // 2, lax.rem(dp, 2)
        self.y, self.c = seq // 2, lax.rem(seq, 2)
        flip_b = (self.a * 2 + 1 - self.b, seq)
        flip_y = (dp, (1 - self.y) * 2 + self.c)
        pick = lambda u, v: tuple(i + self.c * (j - i) for i, j in zip(u, v))
        self.first, self.second = pick(flip_b, flip_y), pick(flip_y, flip_b)
        self.sibling = (dp, self.y * 2 + 1 - self.c)
        self.up, self.down = (dp + 2, seq), (dp - 2, seq)
        self.f = self.b + self.c * (self.y - self.b)
        self.s = self.y + self.c * (self.b - self.y)
        self.has_up, self.has_down = self.a < self.lines - 1, self.a > 0

    def unit(self, a, f, s, c=None):
        c = self.c if c is None else c
        return a * 8 + f * (4 - 2 * c) + s * (2 + 2 * c) + c

    def barrier(self):
        sem = pltpu.get_barrier_semaphore()
        for who in (self.first, self.second, self.sibling):
            pl.semaphore_signal(sem, inc=1, device_id=who, device_id_type=MESH)

        @pl.when(self.has_up)
        def _():
            pl.semaphore_signal(sem, inc=1, device_id=self.up, device_id_type=MESH)

        @pl.when(self.has_down)
        def _():
            pl.semaphore_signal(sem, inc=1, device_id=self.down, device_id_type=MESH)

        pl.semaphore_wait(sem, 3 + self.has_up.astype(jnp.int32) + self.has_down.astype(jnp.int32))


def push(src, dst, send, recv, who):
    return pltpu.make_async_remote_copy(
        src_ref=src, dst_ref=dst, send_sem=send, recv_sem=recv, device_id=who, device_id_type=MESH
    )


class Gather:
    def __init__(self, at, shard, full, sems):
        self.at, self.shard, self.full = at, shard, full
        self.up_s, self.down_s, self.sum_s, self.line_r, self.second_r, self.one = sems

    def to_lines(self, src, slot, index, up, down):
        at = self.at
        if up is not False:
            @pl.when(at.has_up if up is True else jnp.logical_and(up, at.has_up))
            def _():
                push(src, self.full.at[index], self.up_s.at[slot], self.line_r.at[slot], at.up).start()
        if down is not False:
            @pl.when(at.has_down if down is True else jnp.logical_and(down, at.has_down))
            def _():
                push(src, self.full.at[index], self.down_s.at[slot], self.line_r.at[slot], at.down).start()

    def across(self, src, slot, index):
        push(src, self.full.at[index], self.sum_s.at[0], self.second_r.at[slot], self.at.second).start()
        self.aside(src, index)

    def aside(self, src, index):
        push(src, self.full.at[index], self.sum_s.at[1], self.one.at[1], self.at.sibling).start()

    def begin(self):
        at = self.at
        me = at.unit(at.a, at.f, at.s)
        pltpu.make_async_copy(self.shard, self.full.at[me], self.one.at[3]).start()
        push(self.shard, self.full.at[me], self.one.at[2], self.one.at[0], at.first).start()
        slot = at.a * 2 + at.f
        self.to_lines(self.shard, slot, me, True, True)
        self.across(self.shard, slot, me)

    def after_first(self):
        at = self.at
        index = at.unit(at.a, 1 - at.f, at.s)
        ref = self.full.at[index]
        push(ref, ref, self.one.at[2], self.one.at[0], at.first).wait_recv()
        slot = at.a * 2 + 1 - at.f
        self.to_lines(ref, slot, index, True, True)
        self.across(ref, slot, index)

    def after_line(self, k, g):
        at = self.at
        for sign in (-1, 1):
            a = at.a + sign * k
            f = at.f if g == 0 else 1 - at.f

            @pl.when(a >= 0 if sign < 0 else a < at.lines)
            def _():
                index, slot = at.unit(a, f, at.s), a * 2 + f
                ref = self.full.at[index]
                push(ref, ref, self.up_s.at[slot], self.line_r.at[slot], at.up).wait_recv()
                self.to_lines(ref, slot, index, sign < 0, sign > 0)
                self.across(ref, slot, index)

    def after_second(self, k, g):
        at = self.at
        for sign in (-1, 1) if k else (1,):
            a = at.a + sign * k
            f = at.f if g == 0 else 1 - at.f

            @pl.when(a >= 0 if sign < 0 else a < at.lines)
            def _():
                index, slot = at.unit(a, f, 1 - at.s), a * 2 + f
                ref = self.full.at[index]
                push(ref, ref, self.sum_s.at[0], self.second_r.at[slot], at.second).wait_recv()
                self.aside(ref, index)

    def finish(self):
        at, n = self.at, self.at.lines
        me = at.unit(at.a, at.f, at.s)
        half = self.full.at[pl.ds(0, 4 * n)]
        push(half, half, self.sum_s.at[1], self.one.at[1], at.sibling).wait_recv()
        pltpu.make_async_copy(self.shard, self.full.at[me], self.one.at[3]).wait()
        push(self.shard, self.full.at[me], self.one.at[2], self.one.at[0], at.first).wait_send()
        push(half, half, self.sum_s.at[1], self.one.at[1], at.sibling).wait_send()
        part = self.full.at[pl.ds(0, 2 * n)]
        push(part, part, self.sum_s.at[0], self.one.at[0], at.second).wait_send()
        for a in range(n):
            for f in range(2):
                slot = a * 2 + f
                ref = self.full.at[0]

                @pl.when(jnp.logical_and(at.has_up, a <= at.a))
                def _():
                    push(ref, ref, self.up_s.at[slot], self.line_r.at[slot], at.up).wait_send()

                @pl.when(jnp.logical_and(at.has_down, a >= at.a))
                def _():
                    push(ref, ref, self.down_s.at[slot], self.line_r.at[slot], at.down).wait_send()


class LineGather(Gather):
    def begin(self):
        at = self.at
        me = at.unit(at.a, at.f, at.s)
        pltpu.make_async_copy(self.shard, self.full.at[me], self.one.at[3]).start()
        self.to_lines(self.shard, at.a, me, True, True)
        self.to_pairs(self.shard, at.a, me)

    def to_pairs(self, src, a, index):
        at = self.at
        push(src, self.full.at[index], self.one.at[2], self.line_r.at[at.lines + a], at.first).start()
        self.across(src, a * 2 + at.f, index)

    def after_first(self):
        self.from_first(0)

    def from_first(self, k):
        at = self.at
        for sign in (-1, 1) if k else (1,):
            a = at.a + sign * k

            @pl.when(a >= 0 if sign < 0 else a < at.lines)
            def _():
                index = at.unit(a, 1 - at.f, at.s)
                ref = self.full.at[index]
                push(ref, ref, self.one.at[2], self.line_r.at[at.lines + a], at.first).wait_recv()
                self.across(ref, a * 2 + 1 - at.f, index)

    def after_line(self, k, g):
        at = self.at
        if g:
            self.from_first(k)
            return
        for sign in (-1, 1):
            a = at.a + sign * k

            @pl.when(a >= 0 if sign < 0 else a < at.lines)
            def _():
                index = at.unit(a, at.f, at.s)
                ref = self.full.at[index]
                push(ref, ref, self.up_s.at[a], self.line_r.at[a], at.up).wait_recv()
                self.to_lines(ref, a, index, sign < 0, sign > 0)
                self.to_pairs(ref, a, index)

    def finish(self):
        at, n = self.at, self.at.lines
        me = at.unit(at.a, at.f, at.s)
        half = self.full.at[pl.ds(0, 4 * n)]
        push(half, half, self.sum_s.at[1], self.one.at[1], at.sibling).wait_recv()
        pltpu.make_async_copy(self.shard, self.full.at[me], self.one.at[3]).wait()
        push(half, half, self.sum_s.at[1], self.one.at[1], at.sibling).wait_send()
        line = self.full.at[pl.ds(0, n)]
        push(line, line, self.one.at[2], self.one.at[0], at.first).wait_send()
        part = self.full.at[pl.ds(0, 2 * n)]
        push(part, part, self.sum_s.at[0], self.one.at[0], at.second).wait_send()
        ref = self.full.at[0]
        for a in range(n):
            @pl.when(jnp.logical_and(at.has_up, a <= at.a))
            def _():
                push(ref, ref, self.up_s.at[a], self.line_r.at[a], at.up).wait_send()

            @pl.when(jnp.logical_and(at.has_down, a >= at.a))
            def _():
                push(ref, ref, self.down_s.at[a], self.line_r.at[a], at.down).wait_send()


def gather_sems(n):
    dma = pltpu.SemaphoreType.DMA
    return [dma((2 * n,)), dma((2 * n,)), dma((2,)), dma((2 * n,)), dma((2 * n,)), dma((4,))]


def gather_kernel(dp_size, count, early, *refs):
    shards, fulls, sems = refs[:count], refs[count : 2 * count], refs[2 * count :]
    at = Place(dp_size)
    at.barrier()
    kinds = [LineGather if i in early else Gather for i in range(count)]
    jobs = [kinds[i](at, shards[i], fulls[i], sems[6 * i : 6 * i + 6]) for i in range(count)]
    for job in jobs:
        job.begin()
    for job in jobs:
        job.after_first()
    for k in range(1, at.lines):
        for g in range(2):
            for job in jobs:
                job.after_line(k, g)
            for job in jobs:
                job.after_second(k - 1, g)
    for g in range(2):
        for job in jobs:
            job.after_second(at.lines - 1, g)
    for job in jobs:
        job.finish()


def gather_all(dp_size, devices, shards, early, cid=1):
    count = len(shards)
    return pl.pallas_call(
        functools.partial(gather_kernel, dp_size, count, early),
        out_shape=[jax.ShapeDtypeStruct((devices,) + x.shape, x.dtype) for x in shards],
        in_specs=[pl.BlockSpec(memory_space=pl.ANY)] * count,
        out_specs=[pl.BlockSpec(memory_space=pl.ANY)] * count,
        scratch_shapes=gather_sems(dp_size // 2) * count,
        compiler_params=pltpu.CompilerParams(collective_id=cid, has_side_effects=True),
    )(*shards)


def wide(x):
    return x.astype(jnp.float32)


def add_into(dst, src):
    dst[...] = dst[...] + src[...]


class Scatter:
    def __init__(self, at, part, out, bufs, sems):
        self.at, self.part, self.out = at, part, out
        self.own, self.sib, self.sec, self.line, self.fst = bufs
        self.per = 2
        self.one, self.line_s, self.line_r = sems

    def begin(self):
        at = self.at

        def body(j, carry):
            a, f, s = j // 4, lax.rem(j // 2, 2), lax.rem(j, 2)
            push(self.part(at.unit(a, f, s, 1 - at.c)), self.sib.at[j], self.one.at[0], self.one.at[1], at.sibling).start()
            return carry

        lax.fori_loop(0, 4 * at.lines, body, 0)

        def load(j, carry):
            a, f, s = j // 4, lax.rem(j // 2, 2), lax.rem(j, 2)
            pltpu.make_async_copy(self.part(at.unit(a, f, s)), self.own.at[j], self.one.at[2]).start()
            return carry

        lax.fori_loop(0, 4 * at.lines, load, 0)

    def after_sibling(self):
        at = self.at
        n = 2 * at.lines
        pltpu.make_async_copy(self.own, self.own, self.one.at[2]).wait()
        push(self.sib, self.sib, self.one.at[0], self.one.at[1], at.sibling).wait_recv()

        def far(q, carry):
            j = q * 2 + 1 - at.s
            add_into(self.own.at[j], self.sib.at[j])
            return carry

        def send(q, carry):
            push(self.own.at[q * 2 + 1 - at.s], self.sec.at[q], self.one.at[3], self.one.at[4], at.second).start()
            return carry

        def near(q, carry):
            j = q * 2 + at.s
            add_into(self.own.at[j], self.sib.at[j])
            return carry

        lax.fori_loop(0, n, far, 0)
        lax.fori_loop(0, n, send, 0)
        lax.fori_loop(0, n, near, 0)

    def after_second(self):
        at = self.at
        push(self.sec, self.sec, self.one.at[3], self.one.at[4], at.second).wait_recv()

        def body(q, carry):
            add_into(self.own.at[q * 2 + at.s], self.sec.at[q])
            return carry

        lax.fori_loop(0, 2 * at.lines, body, 0)

    def spot(self, q):
        return q * 2 + self.at.s

    def hop(self, low, high, inward, dst, extra):
        at = self.at
        has, who = (at.has_up, at.down) if dst < 0 else (at.has_down, at.up)

        def take(q, carry):
            push(self.line.at[q], self.line.at[q], self.line_s.at[q], self.line_r.at[q], who).wait_recv()
            add_into(self.own.at[self.spot(q)], self.line.at[q])
            return carry

        @pl.when(has)
        def _():
            lax.fori_loop(low, high, take, 0)

        def send(q, carry):
            per = self.per
            slot = q if dst < 0 else jnp.where(q // per == at.a + 1, per * at.lines + lax.rem(q, per), q)
            push(self.own.at[self.spot(q)], self.line.at[slot], self.line_s.at[q], self.line_r.at[slot], who).start()
            return carry

        lax.fori_loop(low, high, send, 0)

    def along(self, h):
        at = self.at
        n = at.lines
        hops = n - 1 if n <= 4 else 1

        @pl.when(jnp.logical_and(at.has_down, at.lines - 1 - at.a == h) if hops > 1 else at.has_down)
        def _():
            self.hop(0, self.per * at.a, at.up, -1, None)

        @pl.when(jnp.logical_and(at.has_up, at.a == h) if hops > 1 else at.has_up)
        def _():
            self.hop(self.per * (at.a + 1), self.per * n, at.down, 1, None)

    def ends(self, f, into):
        at = self.at
        for has, slot in ((at.has_up, 2 * at.a + f), (at.has_down, 2 * at.lines + f)):
            @pl.when(has)
            def _():
                ref = self.line.at[slot]
                push(ref, ref, self.line_s.at[0], self.line_r.at[slot], at.first).wait_recv()
                into[...] = (wide(into[...]) + wide(ref[...])).astype(into.dtype)

    def last_send(self):
        at = self.at
        mine = self.own.at[(2 * at.a + 1 - at.f) * 2 + at.s]
        self.ends(1 - at.f, mine)
        push(mine, self.fst, self.one.at[5], self.one.at[6], at.first).start()
        self.out[...] = wide(self.own[(2 * at.a + at.f) * 2 + at.s])
        self.ends(at.f, self.out)

    def finish(self):
        at = self.at
        push(self.fst, self.fst, self.one.at[5], self.one.at[6], at.first).wait_recv()
        self.out[...] = self.out[...] + wide(self.fst[...])

    def drain(self):
        at = self.at
        n = at.lines
        push(self.sib, self.sib, self.one.at[0], self.one.at[1], at.sibling).wait_send()
        push(self.sec, self.sec, self.one.at[3], self.one.at[4], at.second).wait_send()
        push(self.fst, self.fst, self.one.at[5], self.one.at[6], at.first).wait_send()

        def body(q, carry):
            @pl.when(q // self.per != at.a)
            def _():
                push(self.own.at[q], self.own.at[q], self.line_s.at[q], self.line_r.at[q], at.first).wait_send()
            return carry

        lax.fori_loop(0, self.per * n, body, 0)

    def stages(self):
        return [type(self).after_sibling, type(self).after_second] + self.hops() + [type(self).last_send, type(self).finish]

    def hops(self):
        lines = self.at.lines
        return [functools.partial(type(self).along, h=h) for h in range(lines - 1 if lines <= 4 else 1)]


class LineScatter(Scatter):
    def __init__(self, *args):
        super().__init__(*args)
        self.per = 1

    def spot(self, q):
        return (2 * q + self.at.f) * 2 + self.at.s

    def after_second(self):
        super().after_second()
        at = self.at

        def send(a, carry):
            push(self.own.at[(2 * a + 1 - at.f) * 2 + at.s], self.fst.at[a], self.one.at[5], self.one.at[6], at.first).start()
            return carry

        lax.fori_loop(0, at.lines, send, 0)

    def after_first(self):
        at = self.at
        push(self.fst, self.fst, self.one.at[5], self.one.at[6], at.first).wait_recv()

        def body(a, carry):
            add_into(self.own.at[self.spot(a)], self.fst.at[a])
            return carry

        lax.fori_loop(0, at.lines, body, 0)

    def finish(self):
        at = self.at
        self.out[...] = wide(self.own[self.spot(at.a)])
        for has, slot in ((at.has_up, at.a), (at.has_down, at.lines)):
            @pl.when(has)
            def _():
                ref = self.line.at[slot]
                push(ref, ref, self.line_s.at[0], self.line_r.at[slot], at.first).wait_recv()
                self.out[...] = self.out[...] + wide(ref[...])

    def stages(self):
        kind = type(self)
        return [kind.after_sibling, kind.after_second, kind.after_first] + self.hops() + [kind.finish]


def scatter_buffers(n, shape, dtype, late):
    v = lambda k: pltpu.VMEM((k,) + shape, dtype)
    return [v(4 * n), v(4 * n), v(2 * n)] + ([v(n + 1), v(n)] if late else [v(2 * n + 2), pltpu.VMEM(shape, dtype)])


def scatter_sems(n):
    dma = pltpu.SemaphoreType.DMA
    return [dma((7,)), dma((2 * n,)), dma((2 * n + 2,))]


LANES = 128
AHEAD = 3
ROUNDS = (0, 2, 4, 6, 8, 10, 12)


def window_start(unit, width, features):
    tile = unit * width // LANES
    return (tile - tile // (features // LANES - 1)) * LANES


def whole_part(ref, rows, cols):
    return lambda unit: ref.at[unit, pl.ds(*rows), pl.ds(*cols)]


def window_part(ref, width):
    features = ref.shape[1]
    return lambda unit: ref.at[:, pl.ds(pl.multiple_of(window_start(unit, width, features), LANES), 2 * LANES)]


def cut(shape, cap):
    rows, cols = shape
    pieces = max(1, round(rows * cols / cap))
    while pieces > 1 and not (rows % (16 * pieces) == 0 or cols % (LANES * pieces) == 0):
        pieces -= 1
    if rows % (16 * pieces) == 0:
        step = rows // pieces
        return [((k * step, step), (0, cols)) for k in range(pieces)]
    step = cols // pieces
    return [((0, rows), (k * step, step)) for k in range(pieces)]


def weave(many, few):
    order, i, j = [], 0, 0
    while i < len(many) or j < len(few):
        if j < len(few) and (2 * j + 1) * len(many) <= (2 * i + 1) * len(few):
            order.append(few[j])
            j += 1
        else:
            order.append(many[i])
            i += 1
    return order


def scatter_kernel(dp_size, chunks, count, width, late, *refs):
    parts, outs, rest = refs[:count], refs[count : 2 * count], refs[2 * count :]
    at = Place(dp_size)
    at.barrier()
    jobs = []
    for k, (i, rows, cols) in enumerate(chunks):
        last = i == count - 1
        part = window_part(parts[i], width) if last else whole_part(parts[i], rows, cols)
        out = outs[i] if last else outs[i].at[pl.ds(*rows), pl.ds(*cols)]
        kind = LineScatter if i in late else Scatter
        jobs.append(kind(at, part, out, rest[8 * k : 8 * k + 5], rest[8 * k + 5 : 8 * k + 8]))
    total = len(jobs)
    for job in jobs[:AHEAD]:
        job.begin()
    stages = [job.stages() for job in jobs]
    depth = len(stages[0])
    for t in range(total + ROUNDS[depth - 1]):
        if t + AHEAD < total:
            jobs[t + AHEAD].begin()
        for k in range(depth):
            j = t - ROUNDS[k]
            if 0 <= j < total:
                stages[j][k](jobs[j])
    for job in jobs:
        job.drain()


def scatter_all(dp_size, parts, norm_rows, width, late, cap=18432, cid=2):
    count = len(parts) + 1
    n = dp_size // 2
    outs = [jax.ShapeDtypeStruct(x.shape[1:], jnp.float32) for x in parts]
    outs.append(jax.ShapeDtypeStruct((norm_rows.shape[0], 2 * LANES), jnp.float32))
    pieces = [(i, *piece) for i, x in enumerate(parts) for piece in cut(x.shape[1:], cap)]
    chunks = weave([p for p in pieces if p[0] not in late], [p for p in pieces if p[0] in late])
    scratch = []
    for i, rows, cols in chunks:
        scratch += scatter_buffers(n, (rows[1], cols[1]), parts[i].dtype, i in late) + scatter_sems(n)
    chunks.append((count - 1, None, None))
    scratch += scatter_buffers(n, outs[-1].shape, jnp.float32, count - 1 in late) + scatter_sems(n)
    return pl.pallas_call(
        functools.partial(scatter_kernel, dp_size, chunks, count, width, late),
        out_shape=outs,
        in_specs=[pl.BlockSpec(memory_space=pl.ANY)] * count,
        out_specs=[pl.BlockSpec(memory_space=pltpu.VMEM)] * count,
        scratch_shapes=scratch,
        compiler_params=pltpu.CompilerParams(collective_id=cid, has_side_effects=True, vmem_limit_bytes=64000000),
    )(*parts, norm_rows)


def settle_kernel(*refs):
    half = len(refs) // 2
    for src, dst in zip(refs[:half], refs[half:]):
        dst[...] = src[...]


def settle(arrays):
    spec = [pl.BlockSpec(memory_space=pltpu.VMEM)] * len(arrays)
    return pl.pallas_call(
        settle_kernel,
        out_shape=[jax.ShapeDtypeStruct(x.shape, x.dtype) for x in arrays],
        in_specs=spec,
        out_specs=spec,
    )(*arrays)


def with_halo(x, sides, width):
    for axis, dim in sides:
        devices, length = (lax.axis_size(axis), x.shape[dim])
        up = [(i, (i + 1) % devices) for i in range(devices - 1)]
        down = [(j, i) for i, j in up]
        last = lax.slice_in_dim(x, length - width, length, axis=dim)
        first = lax.slice_in_dim(x, 0, width, axis=dim)
        before = lax.ppermute(last, axis, up)
        after = lax.ppermute(first, axis, down)
        x = jnp.concatenate([before, x, after], axis=dim)
    return x


def norm_rows(residual, row_gain, row_bias):
    centered = residual - jnp.mean(residual, axis=-1, keepdims=True)
    spread = jnp.mean(centered * centered, axis=-1, keepdims=True)
    return centered * lax.rsqrt(spread + eps) * row_gain + row_bias


def gelu_exact(pre_act):
    return jax.nn.gelu(pre_act, approximate=False)


def plain_dot(left, right):
    return jnp.dot(left, right, preferred_element_type=jnp.float32)


def grad_dot(left, right):
    return lax.dot_general(
        left, right, (((0,), (0,)), ((), ())), preferred_element_type=jnp.float32
    )


def back_dot(left, right):
    return lax.dot_general(
        left, right, (((1,), (1,)), ((), ())), preferred_element_type=jnp.float32
    )


def squash(x):
    return 0.5 * jnp.tanh(0.5 * x) + 0.5


def slot_onehot(ids, slots, subset):
    cols = lax.broadcasted_iota(jnp.int32, (ids.shape[0], subset), 1)
    hots = [(ids[:, s : s + 1] == cols).astype(jnp.bfloat16) for s in slots]
    return jnp.concatenate(hots, 0)


def gru_embed(ids_ref, table, w_in, emb_ref, gates, chunk=4):
    rows, nchar = ids_ref.shape
    ids = ids_ref[...]
    for k in range(0, nchar, chunk):
        hot = slot_onehot(ids, range(k, k + chunk), table.shape[0])
        emb = plain_dot(hot, table[...]).astype(jnp.bfloat16)
        emb_ref[k : k + chunk] = emb.reshape(chunk, rows, -1)
        for d in range(2):
            gates[d, k : k + chunk] = plain_dot(emb, w_in[d]).reshape(chunk, rows, -1)


def gru_step(d, slot, count, gates, w_rec, state, factor, keep, prior):
    units = state.shape[2]
    old = state[d]
    low = old.astype(jnp.bfloat16)
    rec = plain_dot(low, w_rec[d])
    gi = gates[d, slot]
    reset = squash(gi[:, :units] + rec[:, :units])
    update = squash(gi[:, units : 2 * units] + rec[:, units : 2 * units])
    rec_n = rec[:, 2 * units :]
    cand = jnp.tanh(gi[:, 2 * units :] + reset * rec_n)
    live = slot < count
    state[d] = jnp.where(live, (1.0 - update) * cand + update * old, old)
    by_cand = jnp.where(live, (1.0 - update) * (1.0 - cand * cand), 0.0)
    by_update = jnp.where(live, (old - cand) * update * (1.0 - update), 0.0)
    by_reset = by_cand * rec_n * reset * (1.0 - reset)
    prior[...] = low
    keep[...] = jnp.where(live, update, 1.0)
    for k, x in enumerate((by_reset, by_update, by_cand, reset)):
        factor[:, k * units : (k + 1) * units] = x.astype(factor.dtype)


def gru_forward_kernel(ids_ref, table, w_in, w_rec, vec, emb, f0, f1, z0, z1, h0, h1, gates, state):
    i = pl.program_id(0)
    nchar = pl.num_programs(0)

    @pl.when(i == 0)
    def _():
        gru_embed(ids_ref, table, w_in, emb, gates)
        state[...] = jnp.zeros_like(state)

    count = jnp.sum((ids_ref[...] > 0).astype(jnp.int32), axis=1, keepdims=True)
    gru_step(0, i, count, gates, w_rec, state, f0.at[0], z0.at[0], h0.at[0])
    gru_step(1, nchar - 1 - i, count, gates, w_rec, state, f1.at[0], z1.at[0], h1.at[0])

    @pl.when(i == nchar - 1)
    def _():
        units = state.shape[2]
        vec[:, :units] = state[0].astype(vec.dtype)
        vec[:, units:] = state[1].astype(vec.dtype)


def slot_specs(nchar, rows, cols, backward):
    up = pl.BlockSpec((1, rows, cols), lambda i: (i, 0, 0))
    down = pl.BlockSpec((1, rows, cols), lambda i: (nchar - 1 - i, 0, 0))
    return [down, up] if backward else [up, down]


def gru_cost(nchar, rows, width, units, products):
    steps = 2 * nchar * rows
    return pl.CostEstimate(
        flops=12 * products * steps * (width + units) * units,
        bytes_accessed=16 * steps * units,
        transcendentals=3 * steps * units,
    )


def gru_forward(ids, table, w_in, w_rec):
    rows, nchar = ids.shape
    width, units = table.shape[1], w_rec.shape[1]
    whole = lambda shape: pl.BlockSpec(shape, lambda i: (0,) * len(shape))
    slots = functools.partial(slot_specs, nchar, rows, backward=False)
    shape = jax.ShapeDtypeStruct
    factor = shape((nchar, rows, 4 * units), jnp.bfloat16)
    keep = shape((nchar, rows, units), jnp.float32)
    prior = shape((nchar, rows, units), jnp.bfloat16)
    return pl.pallas_call(
        gru_forward_kernel,
        grid=(nchar,),
        out_shape=[
            shape((rows, 2 * units), jnp.bfloat16),
            shape((nchar, rows, width), jnp.bfloat16),
            factor, factor, keep, keep, prior, prior,
        ],
        in_specs=[whole(x.shape) for x in (ids, table, w_in, w_rec)],
        out_specs=[whole((rows, 2 * units)), whole((nchar, rows, width))]
        + slots(4 * units) + slots(units) + slots(units),
        scratch_shapes=[
            pltpu.VMEM((2, nchar, rows, 3 * units), jnp.float32),
            pltpu.VMEM((2, rows, units), jnp.float32),
        ],
        compiler_params=pltpu.CompilerParams(vmem_limit_bytes=60000000),
        cost_estimate=gru_cost(nchar, rows, width, units, 1),
    )(ids, table, w_in, w_rec)


def gru_back_step(d, slot, factor, keep, flipped, grad, seeds):
    units = grad.shape[2]
    g = grad[d]
    part = lambda k: factor[:, k * units : (k + 1) * units].astype(jnp.float32)
    by_cand = g * part(2)
    seeds[d, slot, :, :units] = (g * part(0)).astype(seeds.dtype)
    seeds[d, slot, :, units : 2 * units] = (g * part(1)).astype(seeds.dtype)
    seeds[d, slot, :, 2 * units : 3 * units] = (by_cand * part(3)).astype(seeds.dtype)
    seeds[d, slot, :, 3 * units :] = by_cand.astype(seeds.dtype)
    grad[d] = g * keep[...] + plain_dot(seeds[d, slot, :, : 3 * units], flipped[d])


def gru_weight_grads(d, seeds, emb, prior, d_in, d_rec):
    _, nchar, rows, wide = seeds.shape
    units = wide // 4
    states = prior[...].reshape(nchar * rows, units)
    chars = emb[...].reshape(nchar * rows, -1)
    col = lambda k, n: seeds[d, :, :, k * units : (k + n) * units].reshape(nchar * rows, n * units)
    d_rec[d] = grad_dot(states, col(0, 3)).astype(d_rec.dtype)
    d_in[d, :, : 2 * units] = grad_dot(chars, col(0, 2)).astype(d_in.dtype)
    d_in[d, :, 2 * units :] = grad_dot(chars, col(3, 1)).astype(d_in.dtype)


def gru_char_grads(ids_ref, seeds, w_in, d_table, chunk=4):
    _, nchar, rows, wide = seeds.shape
    units = wide // 4
    ids = ids_ref[...]
    total = jnp.zeros(d_table.shape, jnp.float32)
    for k in range(0, nchar, chunk):
        grad = None
        for d in range(2):
            both = seeds[d, k : k + chunk].reshape(chunk * rows, wide)
            part = back_dot(both[:, : 2 * units], w_in[d][:, : 2 * units])
            part = part + back_dot(both[:, 3 * units :], w_in[d][:, 2 * units :])
            grad = part if grad is None else grad + part
        hot = slot_onehot(ids, range(k, k + chunk), d_table.shape[0])
        total = total + grad_dot(hot, grad.astype(jnp.bfloat16))
    d_table[...] = total


def gru_backward_kernel(ids_ref, seed, w_in, w_rec, emb, h0, h1, f0, f1, z0, z1, d_in, d_rec, d_table, grad, seeds, flipped):
    i = pl.program_id(0)
    nchar = pl.num_programs(0)

    @pl.when(i == 0)
    def _():
        units = grad.shape[2]
        grad[0] = seed[:, :units]
        grad[1] = seed[:, units:]
        for d in range(2):
            flipped[d] = w_rec[d].T

    gru_back_step(0, nchar - 1 - i, f0.at[0], z0.at[0], flipped, grad, seeds)
    gru_back_step(1, i, f1.at[0], z1.at[0], flipped, grad, seeds)

    @pl.when(i == nchar - 1)
    def _():
        gru_weight_grads(0, seeds, emb, h0, d_in, d_rec)
        gru_weight_grads(1, seeds, emb, h1, d_in, d_rec)
        gru_char_grads(ids_ref, seeds, w_in, d_table)


def gru_backward(ids, seed, w_in, w_rec, emb, h0, h1, f0, f1, z0, z1, subset):
    nchar, rows, width = emb.shape
    units = w_rec.shape[1]
    whole = lambda shape: pl.BlockSpec(shape, lambda i: (0,) * len(shape))
    slots = functools.partial(slot_specs, nchar, rows, backward=True)
    shape = jax.ShapeDtypeStruct
    return pl.pallas_call(
        gru_backward_kernel,
        grid=(nchar,),
        out_shape=[
            shape(w_in.shape, jnp.bfloat16),
            shape(w_rec.shape, jnp.bfloat16),
            shape((subset, width), jnp.float32),
        ],
        in_specs=[whole(x.shape) for x in (ids, seed, w_in, w_rec, emb, h0, h1)] + slots(4 * units) + slots(units),
        out_specs=[whole(w_in.shape), whole(w_rec.shape), whole((subset, width))],
        scratch_shapes=[
            pltpu.VMEM((2, rows, units), jnp.float32),
            pltpu.VMEM((2, nchar, rows, 4 * units), jnp.bfloat16),
            pltpu.VMEM((2, 3 * units, units), jnp.bfloat16),
        ],
        compiler_params=pltpu.CompilerParams(vmem_limit_bytes=60000000),
        cost_estimate=gru_cost(nchar, rows, width, units, 2),
    )(ids, seed, w_in, w_rec, emb, h0, h1, f0, f1, z0, z1)


def head_pair(q_ref, blocks, valid, pair, half):
    features = q_ref.shape[1]
    cols = pl.ds(pair * 2 * HD, 2 * HD)
    queries = q_ref[:, cols]
    keys = jnp.concatenate([b[:, cols] for b in blocks], 0)
    values = jnp.concatenate([b[:, pl.ds(features + pair * 2 * HD, 2 * HD)] for b in blocks], 0)
    scores = back_dot(one_head(queries, half), keys) * (1.0 / math.sqrt(HD))
    scores = jnp.where(valid, scores, -1000000000.0)
    weight = jnp.exp(scores - jnp.max(scores, axis=-1, keepdims=True))
    return weight / jnp.sum(weight, axis=-1, keepdims=True), queries, keys, values


def first_lanes(shape):
    return lax.broadcasted_iota(jnp.int32, shape, 1) < HD


def one_head(x, half):
    keep = first_lanes(x.shape) if half == 0 else jnp.logical_not(first_lanes(x.shape))
    return jnp.where(keep, x, jnp.zeros_like(x))


def side_by_side(left, right):
    return jnp.where(first_lanes(left.shape), left, right)


def attention_kernel(count, q_ref, valid_ref, *refs):
    blocks, out = refs[:count], refs[count]
    valid = jnp.broadcast_to(valid_ref[...] > 0, (q_ref.shape[0], valid_ref.shape[1]))
    for pair in range(q_ref.shape[1] // (2 * HD)):
        both = []
        for half in range(2):
            probs, _, _, values = head_pair(q_ref, blocks, valid, pair, half)
            both.append(plain_dot(probs.astype(jnp.bfloat16), values))
        out[:, pl.ds(pair * 2 * HD, 2 * HD)] = side_by_side(*both).astype(out.dtype)


def attention_back_kernel(count, q_ref, valid_ref, seed_ref, *refs):
    blocks, q_out, outs = refs[:count], refs[count], refs[count + 1 :]
    rows, features = q_ref.shape
    scale = 1.0 / math.sqrt(HD)
    valid = jnp.broadcast_to(valid_ref[...] > 0, (rows, valid_ref.shape[1]))
    for pair in range(features // (2 * HD)):
        cols = pl.ds(pair * 2 * HD, 2 * HD)
        seed = seed_ref[:, cols]
        q_both, k_both, v_both = [], [], []
        for half in range(2):
            probs, queries, keys, values = head_pair(q_ref, blocks, valid, pair, half)
            probs_grad = back_dot(one_head(seed, half), values)
            inner = jnp.sum(probs * probs_grad, axis=-1, keepdims=True)
            score_grad = (probs * (probs_grad - inner)).astype(jnp.bfloat16)
            q_both.append(plain_dot(score_grad, keys))
            k_both.append(grad_dot(score_grad, queries))
            v_both.append(grad_dot(probs.astype(jnp.bfloat16), seed))
        q_out[:, cols] = (side_by_side(*q_both) * scale).astype(q_out.dtype)
        k_grad = (side_by_side(*k_both) * scale).astype(jnp.bfloat16)
        v_grad = side_by_side(*v_both).astype(jnp.bfloat16)
        for j, out in enumerate(outs):
            out[:, cols] = k_grad[j * rows : (j + 1) * rows]
            out[:, pl.ds(features + pair * 2 * HD, 2 * HD)] = v_grad[j * rows : (j + 1) * rows]


def attention_cost(rows, blocks, features, products):
    span = rows * len(blocks)
    return pl.CostEstimate(
        flops=2 * products * rows * span * features,
        bytes_accessed=8 * span * features,
        transcendentals=rows * span * (features // HD),
    )


def attention(queries, valid, blocks):
    rows, features = queries.shape
    vmem = pl.BlockSpec(memory_space=pltpu.VMEM)
    return pl.pallas_call(
        functools.partial(attention_kernel, len(blocks)),
        out_shape=jax.ShapeDtypeStruct((rows, features), jnp.bfloat16),
        in_specs=[vmem] * (2 + len(blocks)),
        out_specs=vmem,
        cost_estimate=attention_cost(rows, blocks, features, 2),
    )(queries, valid, *blocks)


def attention_back(queries, valid, seed, blocks):
    rows, features = queries.shape
    vmem = pl.BlockSpec(memory_space=pltpu.VMEM)
    return pl.pallas_call(
        functools.partial(attention_back_kernel, len(blocks)),
        out_shape=[jax.ShapeDtypeStruct((rows, features), jnp.bfloat16)]
        + [jax.ShapeDtypeStruct((rows, 2 * features), jnp.bfloat16)] * len(blocks),
        in_specs=[vmem] * (3 + len(blocks)),
        out_specs=[vmem] * (1 + len(blocks)),
        cost_estimate=attention_cost(rows, blocks, features, 5),
    )(queries, valid, seed, *blocks)


def from_next(x, axis, step):
    size = lax.axis_size(axis)
    return lax.ppermute(x, axis, [((i + step) % size, i) for i in range(size)])


def to_next(x, axis, step):
    size = lax.axis_size(axis)
    return lax.ppermute(x, axis, [(i, (i + step) % size) for i in range(size)])


def norm_back(residual, row_gain, seed):
    centered = residual - jnp.mean(residual, axis=-1, keepdims=True)
    spread = jnp.mean(centered * centered, axis=-1, keepdims=True)
    scale = lax.rsqrt(spread + eps)
    unit = centered * scale
    inner = seed * row_gain
    drop = jnp.mean(inner, axis=-1, keepdims=True) + unit * jnp.mean(inner * unit, axis=-1, keepdims=True)
    gain_grad = jnp.sum(seed * unit, axis=0, keepdims=True)
    return scale * (inner - drop), gain_grad, jnp.sum(seed, axis=0, keepdims=True)


def place_norms(gain, bias, index, devices):
    both = jnp.concatenate([gain, bias], 0)
    width = both.shape[1]
    shape = (width, devices * width)
    spot = lax.broadcasted_iota(jnp.int32, shape, 0) + index * width == lax.broadcasted_iota(jnp.int32, shape, 1)
    placed = plain_dot(both, spot.astype(both.dtype)).astype(both.dtype)
    return jnp.pad(placed, ((0, 8 - both.shape[0]), (0, 0)))


def local(
    hidden,
    char_ids,
    groups,
    lengths,
    cotangent,
    qkv_weight,
    out_weight,
    up_weight,
    down_weight,
    norm_gain,
    norm_bias,
    char_table,
    gru_input,
    gru_recur,
    merge_weight,
    conv_weight,
):
    dp_size, devices = lax.axis_size("dp"), lax.axis_size("dp") * lax.axis_size("seq")
    me = lax.axis_index("dp") * lax.axis_size("seq") + lax.axis_index("seq")
    norms = place_norms(norm_gain, norm_bias, me, devices)
    order = (char_table, gru_input, gru_recur, norms, qkv_weight, out_weight, up_weight, down_weight, merge_weight, conv_weight)
    gathered = gather_all(dp_size, devices, order, (2, 9))
    all_norms = jnp.sum(gathered[3].astype(jnp.float32), axis=0)
    (full_table, full_input, full_recur, _, full_qkv, full_out, full_up, full_down, full_merge, full_conv) = [
        x.reshape(-1, x.shape[2]) for x in gathered
    ]
    seq_count, local_len, features = hidden.shape
    nchar = char_ids.shape[2]
    tokens = seq_count * local_len
    key_span = local_len * lax.axis_size("seq")
    gains = [all_norms[k : k + 1] for k in range(3)]
    biases = [all_norms[k : k + 1] for k in range(3, 6)]
    flat_in = hidden.reshape(tokens, features)
    qkv = plain_dot(flat_in, full_qkv).astype(jnp.bfloat16)
    queries, own_kv = qkv[:, :features], qkv[:, features:]
    peers = lax.axis_size("seq")
    kv_blocks = [own_kv] + [from_next(own_kv, "seq", j) for j in range(1, peers)]
    place = lax.rem(lax.axis_index("seq") + jnp.arange(peers), peers) * local_len
    positions = place[:, None] + jnp.arange(local_len)[None, :]
    key_valid = (positions < lengths[0]).astype(jnp.int32).reshape(1, key_span)
    assert seq_count == 1
    flat_ids = char_ids.reshape(tokens, nchar)
    table_start = groups[0] * SUBV
    own_table = lax.dynamic_slice_in_dim(full_table, table_start, SUBV, 0)
    inward = full_input.reshape(2, -1, full_input.shape[1])
    recurrent = full_recur.reshape(2, -1, full_recur.shape[1])
    char_vec, char_emb, *kept = gru_forward(flat_ids, own_table, inward, recurrent)
    factors, keeps, priors = kept[:2], kept[2:4], kept[4:]
    attended = attention(queries, key_valid, kv_blocks)
    resid_one = flat_in.astype(jnp.float32) + plain_dot(attended, full_out)
    norm_one = norm_rows(resid_one, gains[0], biases[0]).astype(jnp.bfloat16)
    up_proj = plain_dot(norm_one, full_up)
    active = gelu_exact(up_proj).astype(jnp.bfloat16)
    resid_two = norm_one.astype(jnp.float32) + plain_dot(active, full_down)
    norm_two = norm_rows(resid_two, gains[1], biases[1]).astype(jnp.bfloat16)
    merge_mats = full_merge.reshape(2, features, features)
    streams = jnp.stack([norm_two, char_vec], 0)
    merged_pair = jnp.einsum("btd,bdf->btf", streams, merge_mats, preferred_element_type=jnp.float32)
    merged_rows = jnp.concatenate([merged_pair[0], merged_pair[1]], -1).astype(jnp.bfloat16)
    padded = with_halo(merged_rows.reshape(seq_count, local_len, 2 * features), (("seq", 1),), 1)
    kernel = full_conv.reshape(3, 2 * features, features)
    windows = [
        padded[:, offset : offset + local_len].reshape(tokens, 2 * features) for offset in range(3)
    ]
    conv_out = (
        plain_dot(windows[0], kernel[0])
        + plain_dot(windows[1], kernel[1])
        + plain_dot(windows[2], kernel[2])
    )
    resid_three = norm_two.astype(jnp.float32) + conv_out
    result = norm_rows(resid_three, gains[2], biases[2]).astype(jnp.bfloat16).reshape(seq_count, local_len, features)
    back_qkv, back_out, back_up, back_down = full_qkv, full_out, full_up, full_down
    back_merge, back_conv = full_merge, full_conv
    merge_back = back_merge.reshape(2, features, features)
    kernel_back = back_conv.reshape(3, 2 * features, features)
    seed_rows = cotangent.reshape(tokens, features).astype(jnp.float32)
    grad_three, gain_three, bias_three = norm_back(resid_three, gains[2], seed_rows)
    conv_seed = grad_three.astype(jnp.bfloat16)
    conv_grad = grad_dot(jnp.concatenate(windows, 1), conv_seed)
    seed_padded = with_halo(conv_seed.reshape(seq_count, local_len, features), (("seq", 1),), 1)
    merged_grad = back_dot(
        seed_padded[:, 2 : 2 + local_len].reshape(tokens, features), kernel_back[0]
    )
    merged_grad = merged_grad + back_dot(
        seed_padded[:, 1 : 1 + local_len].reshape(tokens, features), kernel_back[1]
    )
    merged_grad = merged_grad + back_dot(
        seed_padded[:, 0:local_len].reshape(tokens, features), kernel_back[2]
    )
    merged_grad = merged_grad.astype(jnp.bfloat16)
    pair_grad = jnp.stack([merged_grad[:, :features], merged_grad[:, features:]], 0)
    merge_grad = jnp.einsum("btd,btf->bdf", streams, pair_grad, preferred_element_type=jnp.float32)
    stream_grad = jnp.einsum("btf,bdf->btd", pair_grad, merge_back, preferred_element_type=jnp.float32)
    two_grad = grad_three + stream_grad[0]
    charvec_grad = stream_grad[1]
    grad_two, gain_two, bias_two = norm_back(resid_two, gains[1], two_grad)
    down_seed = grad_two.astype(jnp.bfloat16)
    down_grad = grad_dot(active, down_seed)
    active_grad = back_dot(down_seed, back_down)
    _, pull_gelu = jax.vjp(gelu_exact, up_proj)
    up_seed = pull_gelu(active_grad)[0].astype(jnp.bfloat16)
    up_grad = grad_dot(norm_one, up_seed)
    one_grad = grad_two + back_dot(up_seed, back_up)
    grad_one, gain_one, bias_one = norm_back(resid_one, gains[0], one_grad)
    out_seed = grad_one.astype(jnp.bfloat16)
    out_grad = grad_dot(attended, out_seed)
    attn_seed = back_dot(out_seed, back_out).astype(jnp.bfloat16)
    query_grad, *kv_grads = attention_back(queries, key_valid, attn_seed, kv_blocks)
    kv_own = kv_grads[0].astype(jnp.float32)
    for j in range(1, peers):
        kv_own = kv_own + to_next(kv_grads[j], "seq", j).astype(jnp.float32)
    qkv_seed = jnp.concatenate([query_grad, kv_own.astype(jnp.bfloat16)], -1)
    qkv_grad = grad_dot(flat_in, qkv_seed)
    hidden_grad = (
        (grad_one + back_dot(qkv_seed, back_qkv))
        .astype(jnp.bfloat16)
        .reshape(seq_count, local_len, features)
    )
    input_mats, recur_sum, own_grad = gru_backward(
        flat_ids, charvec_grad, inward, recurrent, char_emb, *priors, *factors, *keeps, SUBV
    )
    table_grad = jnp.zeros(full_table.shape, jnp.bfloat16)
    table_grad = lax.dynamic_update_slice_in_dim(table_grad, own_grad.astype(jnp.bfloat16), table_start, 0)
    norm_grads = jnp.concatenate(
        [gain_one, gain_two, gain_three, bias_one, bias_two, bias_three, jnp.zeros((2, features), jnp.float32)], 0
    )
    terms = [input_mats, recur_sum, merge_grad, conv_grad, down_grad, up_grad, qkv_grad, out_grad, table_grad]
    parts = [x.astype(jnp.bfloat16).reshape(devices, -1, x.shape[-1]) for x in terms]
    width = norm_gain.shape[1]
    *sums, norm_sum = scatter_all(dp_size, parts, norm_grads, width, (3, 6))
    input_total, recur_total, merge_sum, conv_sum, down_sum, up_sum, qkv_sum, out_sum, table_sum = settle(sums)
    skip = me * width - window_start(me, width, features)
    gain_sum = lax.dynamic_slice(norm_sum, (0, skip), (3, width))
    bias_sum = lax.dynamic_slice(norm_sum, (3, skip), (3, width))
    return (result, hidden_grad, qkv_sum, out_sum, up_sum, down_sum, gain_sum, bias_sum, table_sum, input_total, recur_total, merge_sum, conv_sum)


def solution(mesh):
    placed = (
        P("dp", "seq", None),
        P("dp", "seq", None),
        P("dp"),
        P("dp"),
        P("dp", "seq", None),
        P(("dp", "seq"), None),
        P(("dp", "seq"), None),
        P(("dp", "seq"), None),
        P(("dp", "seq"), None),
        P(None, ("dp", "seq")),
        P(None, ("dp", "seq")),
        P(("dp", "seq"), None),
        P(("dp", "seq"), None),
        P(("dp", "seq"), None),
        P(("dp", "seq"), None),
        P(("dp", "seq"), None),
    )
    return jax.shard_map(
        local,
        mesh=mesh,
        in_specs=placed,
        out_specs=(
            P("dp", "seq", None),
            P("dp", "seq", None),
            P(("dp", "seq"), None),
            P(("dp", "seq"), None),
            P(("dp", "seq"), None),
            P(("dp", "seq"), None),
            P(None, ("dp", "seq")),
            P(None, ("dp", "seq")),
            P(("dp", "seq"), None),
            P(("dp", "seq"), None),
            P(("dp", "seq"), None),
            P(("dp", "seq"), None),
            P(("dp", "seq"), None),
        ),
        check_vma=False,
    )
```

```python
import functools
import math

import jax
import jax.numpy as jnp
from jax import lax
from jax.experimental import pallas as pl
from jax.experimental.pallas import tpu as pltpu
from jax.sharding import PartitionSpec as P

MESH = pl.DeviceIdType.MESH

HD = 64
SUBV = 128

eps = 1e-05

class Place:
    def __init__(self, dp_size):
        dp, seq = lax.axis_index("dp"), lax.axis_index("seq")
        self.lines = dp_size // 2
        self.a, self.b = dp // 2, lax.rem(dp, 2)
        self.y, self.c = seq // 2, lax.rem(seq, 2)
        flip_b = (self.a * 2 + 1 - self.b, seq)
        flip_y = (dp, (1 - self.y) * 2 + self.c)
        pick = lambda u, v: tuple(i + self.c * (j - i) for i, j in zip(u, v))
        self.first, self.second = pick(flip_b, flip_y), pick(flip_y, flip_b)
        self.sibling = (dp, self.y * 2 + 1 - self.c)
        self.up, self.down = (dp + 2, seq), (dp - 2, seq)
        self.f = self.b + self.c * (self.y - self.b)
        self.s = self.y + self.c * (self.b - self.y)
        self.has_up, self.has_down = self.a < self.lines - 1, self.a > 0

    def unit(self, a, f, s, c=None):
        c = self.c if c is None else c
        return a * 8 + f * (4 - 2 * c) + s * (2 + 2 * c) + c

    def barrier(self):
        sem = pltpu.get_barrier_semaphore()
        for who in (self.first, self.second, self.sibling):
            pl.semaphore_signal(sem, inc=1, device_id=who, device_id_type=MESH)

        @pl.when(self.has_up)
        def _():
            pl.semaphore_signal(sem, inc=1, device_id=self.up, device_id_type=MESH)

        @pl.when(self.has_down)
        def _():
            pl.semaphore_signal(sem, inc=1, device_id=self.down, device_id_type=MESH)

        pl.semaphore_wait(sem, 3 + self.has_up.astype(jnp.int32) + self.has_down.astype(jnp.int32))


def push(src, dst, send, recv, who):
    return pltpu.make_async_remote_copy(
        src_ref=src, dst_ref=dst, send_sem=send, recv_sem=recv, device_id=who, device_id_type=MESH
    )


class Gather:
    def __init__(self, at, shard, full, sems):
        self.at, self.shard, self.full = at, shard, full
        self.up_s, self.down_s, self.sum_s, self.line_r, self.second_r, self.one = sems

    def to_lines(self, src, slot, index, up, down):
        at = self.at
        if up is not False:
            @pl.when(at.has_up if up is True else jnp.logical_and(up, at.has_up))
            def _():
                push(src, self.full.at[index], self.up_s.at[slot], self.line_r.at[slot], at.up).start()
        if down is not False:
            @pl.when(at.has_down if down is True else jnp.logical_and(down, at.has_down))
            def _():
                push(src, self.full.at[index], self.down_s.at[slot], self.line_r.at[slot], at.down).start()

    def across(self, src, slot, index):
        push(src, self.full.at[index], self.sum_s.at[0], self.second_r.at[slot], self.at.second).start()
        self.aside(src, index)

    def aside(self, src, index):
        push(src, self.full.at[index], self.sum_s.at[1], self.one.at[1], self.at.sibling).start()

    def begin(self):
        at = self.at
        me = at.unit(at.a, at.f, at.s)
        pltpu.make_async_copy(self.shard, self.full.at[me], self.one.at[3]).start()
        push(self.shard, self.full.at[me], self.one.at[2], self.one.at[0], at.first).start()
        slot = at.a * 2 + at.f
        self.to_lines(self.shard, slot, me, True, True)
        self.across(self.shard, slot, me)

    def after_first(self):
        at = self.at
        index = at.unit(at.a, 1 - at.f, at.s)
        ref = self.full.at[index]
        push(ref, ref, self.one.at[2], self.one.at[0], at.first).wait_recv()
        slot = at.a * 2 + 1 - at.f
        self.to_lines(ref, slot, index, True, True)
        self.across(ref, slot, index)

    def after_line(self, k, g):
        at = self.at
        for sign in (-1, 1):
            a = at.a + sign * k
            f = at.f if g == 0 else 1 - at.f

            @pl.when(a >= 0 if sign < 0 else a < at.lines)
            def _():
                index, slot = at.unit(a, f, at.s), a * 2 + f
                ref = self.full.at[index]
                push(ref, ref, self.up_s.at[slot], self.line_r.at[slot], at.up).wait_recv()
                self.to_lines(ref, slot, index, sign < 0, sign > 0)
                self.across(ref, slot, index)

    def after_second(self, k, g):
        at = self.at
        for sign in (-1, 1) if k else (1,):
            a = at.a + sign * k
            f = at.f if g == 0 else 1 - at.f

            @pl.when(a >= 0 if sign < 0 else a < at.lines)
            def _():
                index, slot = at.unit(a, f, 1 - at.s), a * 2 + f
                ref = self.full.at[index]
                push(ref, ref, self.sum_s.at[0], self.second_r.at[slot], at.second).wait_recv()
                self.aside(ref, index)

    def finish(self):
        at, n = self.at, self.at.lines
        me = at.unit(at.a, at.f, at.s)
        half = self.full.at[pl.ds(0, 4 * n)]
        push(half, half, self.sum_s.at[1], self.one.at[1], at.sibling).wait_recv()
        pltpu.make_async_copy(self.shard, self.full.at[me], self.one.at[3]).wait()
        push(self.shard, self.full.at[me], self.one.at[2], self.one.at[0], at.first).wait_send()
        push(half, half, self.sum_s.at[1], self.one.at[1], at.sibling).wait_send()
        part = self.full.at[pl.ds(0, 2 * n)]
        push(part, part, self.sum_s.at[0], self.one.at[0], at.second).wait_send()
        for a in range(n):
            for f in range(2):
                slot = a * 2 + f
                ref = self.full.at[0]

                @pl.when(jnp.logical_and(at.has_up, a <= at.a))
                def _():
                    push(ref, ref, self.up_s.at[slot], self.line_r.at[slot], at.up).wait_send()

                @pl.when(jnp.logical_and(at.has_down, a >= at.a))
                def _():
                    push(ref, ref, self.down_s.at[slot], self.line_r.at[slot], at.down).wait_send()


class LineGather(Gather):
    def begin(self):
        at = self.at
        me = at.unit(at.a, at.f, at.s)
        pltpu.make_async_copy(self.shard, self.full.at[me], self.one.at[3]).start()
        self.to_lines(self.shard, at.a, me, True, True)
        self.to_pairs(self.shard, at.a, me)

    def to_pairs(self, src, a, index):
        at = self.at
        push(src, self.full.at[index], self.one.at[2], self.line_r.at[at.lines + a], at.first).start()
        self.across(src, a * 2 + at.f, index)

    def after_first(self):
        self.from_first(0)

    def from_first(self, k):
        at = self.at
        for sign in (-1, 1) if k else (1,):
            a = at.a + sign * k

            @pl.when(a >= 0 if sign < 0 else a < at.lines)
            def _():
                index = at.unit(a, 1 - at.f, at.s)
                ref = self.full.at[index]
                push(ref, ref, self.one.at[2], self.line_r.at[at.lines + a], at.first).wait_recv()
                self.across(ref, a * 2 + 1 - at.f, index)

    def after_line(self, k, g):
        at = self.at
        if g:
            self.from_first(k)
            return
        for sign in (-1, 1):
            a = at.a + sign * k

            @pl.when(a >= 0 if sign < 0 else a < at.lines)
            def _():
                index = at.unit(a, at.f, at.s)
                ref = self.full.at[index]
                push(ref, ref, self.up_s.at[a], self.line_r.at[a], at.up).wait_recv()
                self.to_lines(ref, a, index, sign < 0, sign > 0)
                self.to_pairs(ref, a, index)

    def finish(self):
        at, n = self.at, self.at.lines
        me = at.unit(at.a, at.f, at.s)
        half = self.full.at[pl.ds(0, 4 * n)]
        push(half, half, self.sum_s.at[1], self.one.at[1], at.sibling).wait_recv()
        pltpu.make_async_copy(self.shard, self.full.at[me], self.one.at[3]).wait()
        push(half, half, self.sum_s.at[1], self.one.at[1], at.sibling).wait_send()
        line = self.full.at[pl.ds(0, n)]
        push(line, line, self.one.at[2], self.one.at[0], at.first).wait_send()
        part = self.full.at[pl.ds(0, 2 * n)]
        push(part, part, self.sum_s.at[0], self.one.at[0], at.second).wait_send()
        ref = self.full.at[0]
        for a in range(n):
            @pl.when(jnp.logical_and(at.has_up, a <= at.a))
            def _():
                push(ref, ref, self.up_s.at[a], self.line_r.at[a], at.up).wait_send()

            @pl.when(jnp.logical_and(at.has_down, a >= at.a))
            def _():
                push(ref, ref, self.down_s.at[a], self.line_r.at[a], at.down).wait_send()


def gather_sems(n):
    dma = pltpu.SemaphoreType.DMA
    return [dma((2 * n,)), dma((2 * n,)), dma((2,)), dma((2 * n,)), dma((2 * n,)), dma((4,))]


def gather_kernel(dp_size, count, early, *refs):
    shards, fulls, sems = refs[:count], refs[count : 2 * count], refs[2 * count :]
    at = Place(dp_size)
    at.barrier()
    kinds = [LineGather if i in early else Gather for i in range(count)]
    jobs = [kinds[i](at, shards[i], fulls[i], sems[6 * i : 6 * i + 6]) for i in range(count)]
    for job in jobs:
        job.begin()
    for job in jobs:
        job.after_first()
    for k in range(1, at.lines):
        for g in range(2):
            for job in jobs:
                job.after_line(k, g)
            for job in jobs:
                job.after_second(k - 1, g)
    for g in range(2):
        for job in jobs:
            job.after_second(at.lines - 1, g)
    for job in jobs:
        job.finish()


def gather_all(dp_size, devices, shards, early, cid=1):
    count = len(shards)
    return pl.pallas_call(
        functools.partial(gather_kernel, dp_size, count, early),
        out_shape=[jax.ShapeDtypeStruct((devices,) + x.shape, x.dtype) for x in shards],
        in_specs=[pl.BlockSpec(memory_space=pl.ANY)] * count,
        out_specs=[pl.BlockSpec(memory_space=pl.ANY)] * count,
        scratch_shapes=gather_sems(dp_size // 2) * count,
        compiler_params=pltpu.CompilerParams(collective_id=cid, has_side_effects=True),
    )(*shards)


def wide(x):
    return x.astype(jnp.float32)


def add_into(dst, src):
    dst[...] = dst[...] + src[...]


class Scatter:
    def __init__(self, at, part, out, bufs, sems):
        self.at, self.part, self.out = at, part, out
        self.own, self.sib, self.sec, self.line, self.fst = bufs
        self.per = 2
        self.one, self.line_s, self.line_r = sems

    def begin(self):
        at = self.at

        def body(j, carry):
            a, f, s = j // 4, lax.rem(j // 2, 2), lax.rem(j, 2)
            push(self.part(at.unit(a, f, s, 1 - at.c)), self.sib.at[j], self.one.at[0], self.one.at[1], at.sibling).start()
            return carry

        lax.fori_loop(0, 4 * at.lines, body, 0)

        def load(j, carry):
            a, f, s = j // 4, lax.rem(j // 2, 2), lax.rem(j, 2)
            pltpu.make_async_copy(self.part(at.unit(a, f, s)), self.own.at[j], self.one.at[2]).start()
            return carry

        lax.fori_loop(0, 4 * at.lines, load, 0)

    def after_sibling(self):
        at = self.at
        n = 2 * at.lines
        pltpu.make_async_copy(self.own, self.own, self.one.at[2]).wait()
        push(self.sib, self.sib, self.one.at[0], self.one.at[1], at.sibling).wait_recv()

        def far(q, carry):
            j = q * 2 + 1 - at.s
            add_into(self.own.at[j], self.sib.at[j])
            return carry

        def send(q, carry):
            push(self.own.at[q * 2 + 1 - at.s], self.sec.at[q], self.one.at[3], self.one.at[4], at.second).start()
            return carry

        def near(q, carry):
            j = q * 2 + at.s
            add_into(self.own.at[j], self.sib.at[j])
            return carry

        lax.fori_loop(0, n, far, 0)
        lax.fori_loop(0, n, send, 0)
        lax.fori_loop(0, n, near, 0)

    def after_second(self):
        at = self.at
        push(self.sec, self.sec, self.one.at[3], self.one.at[4], at.second).wait_recv()

        def body(q, carry):
            add_into(self.own.at[q * 2 + at.s], self.sec.at[q])
            return carry

        lax.fori_loop(0, 2 * at.lines, body, 0)

    def spot(self, q):
        return q * 2 + self.at.s

    def hop(self, low, high, inward, dst, extra):
        at = self.at
        has, who = (at.has_up, at.down) if dst < 0 else (at.has_down, at.up)

        def take(q, carry):
            push(self.line.at[q], self.line.at[q], self.line_s.at[q], self.line_r.at[q], who).wait_recv()
            add_into(self.own.at[self.spot(q)], self.line.at[q])
            return carry

        @pl.when(has)
        def _():
            lax.fori_loop(low, high, take, 0)

        def send(q, carry):
            per = self.per
            slot = q if dst < 0 else jnp.where(q // per == at.a + 1, per * at.lines + lax.rem(q, per), q)
            push(self.own.at[self.spot(q)], self.line.at[slot], self.line_s.at[q], self.line_r.at[slot], who).start()
            return carry

        lax.fori_loop(low, high, send, 0)

    def along(self, h):
        at = self.at
        n = at.lines
        hops = n - 1 if n <= 4 else 1

        @pl.when(jnp.logical_and(at.has_down, at.lines - 1 - at.a == h) if hops > 1 else at.has_down)
        def _():
            self.hop(0, self.per * at.a, at.up, -1, None)

        @pl.when(jnp.logical_and(at.has_up, at.a == h) if hops > 1 else at.has_up)
        def _():
            self.hop(self.per * (at.a + 1), self.per * n, at.down, 1, None)

    def ends(self, f, into):
        at = self.at
        for has, slot in ((at.has_up, 2 * at.a + f), (at.has_down, 2 * at.lines + f)):
            @pl.when(has)
            def _():
                ref = self.line.at[slot]
                push(ref, ref, self.line_s.at[0], self.line_r.at[slot], at.first).wait_recv()
                into[...] = (wide(into[...]) + wide(ref[...])).astype(into.dtype)

    def last_send(self):
        at = self.at
        mine = self.own.at[(2 * at.a + 1 - at.f) * 2 + at.s]
        self.ends(1 - at.f, mine)
        push(mine, self.fst, self.one.at[5], self.one.at[6], at.first).start()
        self.out[...] = wide(self.own[(2 * at.a + at.f) * 2 + at.s])
        self.ends(at.f, self.out)

    def finish(self):
        at = self.at
        push(self.fst, self.fst, self.one.at[5], self.one.at[6], at.first).wait_recv()
        self.out[...] = self.out[...] + wide(self.fst[...])

    def drain(self):
        at = self.at
        n = at.lines
        push(self.sib, self.sib, self.one.at[0], self.one.at[1], at.sibling).wait_send()
        push(self.sec, self.sec, self.one.at[3], self.one.at[4], at.second).wait_send()
        push(self.fst, self.fst, self.one.at[5], self.one.at[6], at.first).wait_send()

        def body(q, carry):
            @pl.when(q // self.per != at.a)
            def _():
                push(self.own.at[q], self.own.at[q], self.line_s.at[q], self.line_r.at[q], at.first).wait_send()
            return carry

        lax.fori_loop(0, self.per * n, body, 0)

    def stages(self):
        return [type(self).after_sibling, type(self).after_second] + self.hops() + [type(self).last_send, type(self).finish]

    def hops(self):
        lines = self.at.lines
        return [functools.partial(type(self).along, h=h) for h in range(lines - 1 if lines <= 4 else 1)]


class LineScatter(Scatter):
    def __init__(self, *args):
        super().__init__(*args)
        self.per = 1

    def spot(self, q):
        return (2 * q + self.at.f) * 2 + self.at.s

    def after_second(self):
        super().after_second()
        at = self.at

        def send(a, carry):
            push(self.own.at[(2 * a + 1 - at.f) * 2 + at.s], self.fst.at[a], self.one.at[5], self.one.at[6], at.first).start()
            return carry

        lax.fori_loop(0, at.lines, send, 0)

    def after_first(self):
        at = self.at
        push(self.fst, self.fst, self.one.at[5], self.one.at[6], at.first).wait_recv()

        def body(a, carry):
            add_into(self.own.at[self.spot(a)], self.fst.at[a])
            return carry

        lax.fori_loop(0, at.lines, body, 0)

    def finish(self):
        at = self.at
        self.out[...] = wide(self.own[self.spot(at.a)])
        for has, slot in ((at.has_up, at.a), (at.has_down, at.lines)):
            @pl.when(has)
            def _():
                ref = self.line.at[slot]
                push(ref, ref, self.line_s.at[0], self.line_r.at[slot], at.first).wait_recv()
                self.out[...] = self.out[...] + wide(ref[...])

    def stages(self):
        kind = type(self)
        return [kind.after_sibling, kind.after_second, kind.after_first] + self.hops() + [kind.finish]


def scatter_buffers(n, shape, dtype, late):
    v = lambda k: pltpu.VMEM((k,) + shape, dtype)
    return [v(4 * n), v(4 * n), v(2 * n)] + ([v(n + 1), v(n)] if late else [v(2 * n + 2), pltpu.VMEM(shape, dtype)])


def scatter_sems(n):
    dma = pltpu.SemaphoreType.DMA
    return [dma((7,)), dma((2 * n,)), dma((2 * n + 2,))]


LANES = 128
AHEAD = 3
ROUNDS = (0, 2, 4, 6, 8, 10, 12)


def window_start(unit, width, features):
    tile = unit * width // LANES
    return (tile - tile // (features // LANES - 1)) * LANES


def whole_part(ref, rows, cols):
    return lambda unit: ref.at[unit, pl.ds(*rows), pl.ds(*cols)]


def window_part(ref, width):
    features = ref.shape[1]
    return lambda unit: ref.at[:, pl.ds(pl.multiple_of(window_start(unit, width, features), LANES), 2 * LANES)]


def cut(shape, cap):
    rows, cols = shape
    pieces = max(1, round(rows * cols / cap))
    while pieces > 1 and not (rows % (16 * pieces) == 0 or cols % (LANES * pieces) == 0):
        pieces -= 1
    if rows % (16 * pieces) == 0:
        step = rows // pieces
        return [((k * step, step), (0, cols)) for k in range(pieces)]
    step = cols // pieces
    return [((0, rows), (k * step, step)) for k in range(pieces)]


def weave(many, few):
    order, i, j = [], 0, 0
    while i < len(many) or j < len(few):
        if j < len(few) and (2 * j + 1) * len(many) <= (2 * i + 1) * len(few):
            order.append(few[j])
            j += 1
        else:
            order.append(many[i])
            i += 1
    return order


def scatter_kernel(dp_size, chunks, count, width, late, *refs):
    parts, outs, rest = refs[:count], refs[count : 2 * count], refs[2 * count :]
    at = Place(dp_size)
    at.barrier()
    jobs = []
    for k, (i, rows, cols) in enumerate(chunks):
        last = i == count - 1
        part = window_part(parts[i], width) if last else whole_part(parts[i], rows, cols)
        out = outs[i] if last else outs[i].at[pl.ds(*rows), pl.ds(*cols)]
        kind = LineScatter if i in late else Scatter
        jobs.append(kind(at, part, out, rest[8 * k : 8 * k + 5], rest[8 * k + 5 : 8 * k + 8]))
    total = len(jobs)
    for job in jobs[:AHEAD]:
        job.begin()
    stages = [job.stages() for job in jobs]
    depth = len(stages[0])
    for t in range(total + ROUNDS[depth - 1]):
        if t + AHEAD < total:
            jobs[t + AHEAD].begin()
        for k in range(depth):
            j = t - ROUNDS[k]
            if 0 <= j < total:
                stages[j][k](jobs[j])
    for job in jobs:
        job.drain()


def scatter_all(dp_size, parts, norm_rows, width, late, cap=18432, cid=2):
    count = len(parts) + 1
    n = dp_size // 2
    outs = [jax.ShapeDtypeStruct(x.shape[1:], jnp.float32) for x in parts]
    outs.append(jax.ShapeDtypeStruct((norm_rows.shape[0], 2 * LANES), jnp.float32))
    pieces = [(i, *piece) for i, x in enumerate(parts) for piece in cut(x.shape[1:], cap)]
    chunks = weave([p for p in pieces if p[0] not in late], [p for p in pieces if p[0] in late])
    scratch = []
    for i, rows, cols in chunks:
        scratch += scatter_buffers(n, (rows[1], cols[1]), parts[i].dtype, i in late) + scatter_sems(n)
    chunks.append((count - 1, None, None))
    scratch += scatter_buffers(n, outs[-1].shape, jnp.float32, count - 1 in late) + scatter_sems(n)
    return pl.pallas_call(
        functools.partial(scatter_kernel, dp_size, chunks, count, width, late),
        out_shape=outs,
        in_specs=[pl.BlockSpec(memory_space=pl.ANY)] * count,
        out_specs=[pl.BlockSpec(memory_space=pltpu.VMEM)] * count,
        scratch_shapes=scratch,
        compiler_params=pltpu.CompilerParams(collective_id=cid, has_side_effects=True, vmem_limit_bytes=64000000),
    )(*parts, norm_rows)


def settle_kernel(*refs):
    half = len(refs) // 2
    for src, dst in zip(refs[:half], refs[half:]):
        dst[...] = src[...]


def settle(arrays):
    spec = [pl.BlockSpec(memory_space=pltpu.VMEM)] * len(arrays)
    return pl.pallas_call(
        settle_kernel,
        out_shape=[jax.ShapeDtypeStruct(x.shape, x.dtype) for x in arrays],
        in_specs=spec,
        out_specs=spec,
    )(*arrays)


def with_halo(x, sides, width):
    for axis, dim in sides:
        devices, length = (lax.axis_size(axis), x.shape[dim])
        up = [(i, (i + 1) % devices) for i in range(devices - 1)]
        down = [(j, i) for i, j in up]
        last = lax.slice_in_dim(x, length - width, length, axis=dim)
        first = lax.slice_in_dim(x, 0, width, axis=dim)
        before = lax.ppermute(last, axis, up)
        after = lax.ppermute(first, axis, down)
        x = jnp.concatenate([before, x, after], axis=dim)
    return x


def norm_rows(residual, row_gain, row_bias):
    centered = residual - jnp.mean(residual, axis=-1, keepdims=True)
    spread = jnp.mean(centered * centered, axis=-1, keepdims=True)
    return centered * lax.rsqrt(spread + eps) * row_gain + row_bias


def gelu_exact(pre_act):
    return jax.nn.gelu(pre_act, approximate=False)


def plain_dot(left, right):
    return jnp.dot(left, right, preferred_element_type=jnp.float32)


def grad_dot(left, right):
    return lax.dot_general(
        left, right, (((0,), (0,)), ((), ())), preferred_element_type=jnp.float32
    )


def back_dot(left, right):
    return lax.dot_general(
        left, right, (((1,), (1,)), ((), ())), preferred_element_type=jnp.float32
    )


def squash(x):
    return 0.5 * jnp.tanh(0.5 * x) + 0.5


def slot_onehot(ids, slots, subset):
    cols = lax.broadcasted_iota(jnp.int32, (ids.shape[0], subset), 1)
    hots = [(ids[:, s : s + 1] == cols).astype(jnp.bfloat16) for s in slots]
    return jnp.concatenate(hots, 0)


def gru_embed(ids_ref, table, w_in, emb_ref, gates, chunk=4):
    rows, nchar = ids_ref.shape
    ids = ids_ref[...]
    for k in range(0, nchar, chunk):
        hot = slot_onehot(ids, range(k, k + chunk), table.shape[0])
        emb = plain_dot(hot, table[...]).astype(jnp.bfloat16)
        emb_ref[k : k + chunk] = emb.reshape(chunk, rows, -1)
        for d in range(2):
            gates[d, k : k + chunk] = plain_dot(emb, w_in[d]).reshape(chunk, rows, -1)


def gru_step(d, slot, count, gates, w_rec, state, factor, keep, prior):
    units = state.shape[2]
    old = state[d]
    low = old.astype(jnp.bfloat16)
    rec = plain_dot(low, w_rec[d])
    gi = gates[d, slot]
    reset = squash(gi[:, :units] + rec[:, :units])
    update = squash(gi[:, units : 2 * units] + rec[:, units : 2 * units])
    rec_n = rec[:, 2 * units :]
    cand = jnp.tanh(gi[:, 2 * units :] + reset * rec_n)
    live = slot < count
    state[d] = jnp.where(live, (1.0 - update) * cand + update * old, old)
    by_cand = jnp.where(live, (1.0 - update) * (1.0 - cand * cand), 0.0)
    by_update = jnp.where(live, (old - cand) * update * (1.0 - update), 0.0)
    by_reset = by_cand * rec_n * reset * (1.0 - reset)
    prior[...] = low
    keep[...] = jnp.where(live, update, 1.0)
    for k, x in enumerate((by_reset, by_update, by_cand, reset)):
        factor[:, k * units : (k + 1) * units] = x.astype(factor.dtype)


def gru_forward_kernel(ids_ref, table, w_in, w_rec, vec, emb, f0, f1, z0, z1, h0, h1, gates, state):
    i = pl.program_id(0)
    nchar = pl.num_programs(0)

    @pl.when(i == 0)
    def _():
        gru_embed(ids_ref, table, w_in, emb, gates)
        state[...] = jnp.zeros_like(state)

    count = jnp.sum((ids_ref[...] > 0).astype(jnp.int32), axis=1, keepdims=True)
    gru_step(0, i, count, gates, w_rec, state, f0.at[0], z0.at[0], h0.at[0])
    gru_step(1, nchar - 1 - i, count, gates, w_rec, state, f1.at[0], z1.at[0], h1.at[0])

    @pl.when(i == nchar - 1)
    def _():
        units = state.shape[2]
        vec[:, :units] = state[0].astype(vec.dtype)
        vec[:, units:] = state[1].astype(vec.dtype)


def slot_specs(nchar, rows, cols, backward):
    up = pl.BlockSpec((1, rows, cols), lambda i: (i, 0, 0))
    down = pl.BlockSpec((1, rows, cols), lambda i: (nchar - 1 - i, 0, 0))
    return [down, up] if backward else [up, down]


def gru_cost(nchar, rows, width, units, products):
    steps = 2 * nchar * rows
    return pl.CostEstimate(
        flops=12 * products * steps * (width + units) * units,
        bytes_accessed=16 * steps * units,
        transcendentals=3 * steps * units,
    )


def gru_forward(ids, table, w_in, w_rec):
    rows, nchar = ids.shape
    width, units = table.shape[1], w_rec.shape[1]
    whole = lambda shape: pl.BlockSpec(shape, lambda i: (0,) * len(shape))
    slots = functools.partial(slot_specs, nchar, rows, backward=False)
    shape = jax.ShapeDtypeStruct
    factor = shape((nchar, rows, 4 * units), jnp.bfloat16)
    keep = shape((nchar, rows, units), jnp.float32)
    prior = shape((nchar, rows, units), jnp.bfloat16)
    return pl.pallas_call(
        gru_forward_kernel,
        grid=(nchar,),
        out_shape=[
            shape((rows, 2 * units), jnp.bfloat16),
            shape((nchar, rows, width), jnp.bfloat16),
            factor, factor, keep, keep, prior, prior,
        ],
        in_specs=[whole(x.shape) for x in (ids, table, w_in, w_rec)],
        out_specs=[whole((rows, 2 * units)), whole((nchar, rows, width))]
        + slots(4 * units) + slots(units) + slots(units),
        scratch_shapes=[
            pltpu.VMEM((2, nchar, rows, 3 * units), jnp.float32),
            pltpu.VMEM((2, rows, units), jnp.float32),
        ],
        compiler_params=pltpu.CompilerParams(vmem_limit_bytes=60000000),
        cost_estimate=gru_cost(nchar, rows, width, units, 1),
    )(ids, table, w_in, w_rec)


def gru_back_step(d, slot, factor, keep, flipped, grad, seeds):
    units = grad.shape[2]
    g = grad[d]
    part = lambda k: factor[:, k * units : (k + 1) * units].astype(jnp.float32)
    by_cand = g * part(2)
    seeds[d, slot, :, :units] = (g * part(0)).astype(seeds.dtype)
    seeds[d, slot, :, units : 2 * units] = (g * part(1)).astype(seeds.dtype)
    seeds[d, slot, :, 2 * units : 3 * units] = (by_cand * part(3)).astype(seeds.dtype)
    seeds[d, slot, :, 3 * units :] = by_cand.astype(seeds.dtype)
    grad[d] = g * keep[...] + plain_dot(seeds[d, slot, :, : 3 * units], flipped[d])


def gru_weight_grads(d, seeds, emb, prior, d_in, d_rec):
    _, nchar, rows, wide = seeds.shape
    units = wide // 4
    states = prior[...].reshape(nchar * rows, units)
    chars = emb[...].reshape(nchar * rows, -1)
    col = lambda k, n: seeds[d, :, :, k * units : (k + n) * units].reshape(nchar * rows, n * units)
    d_rec[d] = grad_dot(states, col(0, 3)).astype(d_rec.dtype)
    d_in[d, :, : 2 * units] = grad_dot(chars, col(0, 2)).astype(d_in.dtype)
    d_in[d, :, 2 * units :] = grad_dot(chars, col(3, 1)).astype(d_in.dtype)


def gru_char_grads(ids_ref, seeds, w_in, d_table, chunk=4):
    _, nchar, rows, wide = seeds.shape
    units = wide // 4
    ids = ids_ref[...]
    total = jnp.zeros(d_table.shape, jnp.float32)
    for k in range(0, nchar, chunk):
        grad = None
        for d in range(2):
            both = seeds[d, k : k + chunk].reshape(chunk * rows, wide)
            part = back_dot(both[:, : 2 * units], w_in[d][:, : 2 * units])
            part = part + back_dot(both[:, 3 * units :], w_in[d][:, 2 * units :])
            grad = part if grad is None else grad + part
        hot = slot_onehot(ids, range(k, k + chunk), d_table.shape[0])
        total = total + grad_dot(hot, grad.astype(jnp.bfloat16))
    d_table[...] = total


def gru_backward_kernel(ids_ref, seed, w_in, w_rec, emb, h0, h1, f0, f1, z0, z1, d_in, d_rec, d_table, grad, seeds, flipped):
    i = pl.program_id(0)
    nchar = pl.num_programs(0)

    @pl.when(i == 0)
    def _():
        units = grad.shape[2]
        grad[0] = seed[:, :units]
        grad[1] = seed[:, units:]
        for d in range(2):
            flipped[d] = w_rec[d].T

    gru_back_step(0, nchar - 1 - i, f0.at[0], z0.at[0], flipped, grad, seeds)
    gru_back_step(1, i, f1.at[0], z1.at[0], flipped, grad, seeds)

    @pl.when(i == nchar - 1)
    def _():
        gru_weight_grads(0, seeds, emb, h0, d_in, d_rec)
        gru_weight_grads(1, seeds, emb, h1, d_in, d_rec)
        gru_char_grads(ids_ref, seeds, w_in, d_table)


def gru_backward(ids, seed, w_in, w_rec, emb, h0, h1, f0, f1, z0, z1, subset):
    nchar, rows, width = emb.shape
    units = w_rec.shape[1]
    whole = lambda shape: pl.BlockSpec(shape, lambda i: (0,) * len(shape))
    slots = functools.partial(slot_specs, nchar, rows, backward=True)
    shape = jax.ShapeDtypeStruct
    return pl.pallas_call(
        gru_backward_kernel,
        grid=(nchar,),
        out_shape=[
            shape(w_in.shape, jnp.bfloat16),
            shape(w_rec.shape, jnp.bfloat16),
            shape((subset, width), jnp.float32),
        ],
        in_specs=[whole(x.shape) for x in (ids, seed, w_in, w_rec, emb, h0, h1)] + slots(4 * units) + slots(units),
        out_specs=[whole(w_in.shape), whole(w_rec.shape), whole((subset, width))],
        scratch_shapes=[
            pltpu.VMEM((2, rows, units), jnp.float32),
            pltpu.VMEM((2, nchar, rows, 4 * units), jnp.bfloat16),
            pltpu.VMEM((2, 3 * units, units), jnp.bfloat16),
        ],
        compiler_params=pltpu.CompilerParams(vmem_limit_bytes=60000000),
        cost_estimate=gru_cost(nchar, rows, width, units, 2),
    )(ids, seed, w_in, w_rec, emb, h0, h1, f0, f1, z0, z1)


def head_pair(q_ref, blocks, valid, pair, half):
    features = q_ref.shape[1]
    cols = pl.ds(pair * 2 * HD, 2 * HD)
    queries = q_ref[:, cols]
    keys = jnp.concatenate([b[:, cols] for b in blocks], 0)
    values = jnp.concatenate([b[:, pl.ds(features + pair * 2 * HD, 2 * HD)] for b in blocks], 0)
    scores = back_dot(one_head(queries, half), keys) * (1.0 / math.sqrt(HD))
    scores = jnp.where(valid, scores, -1000000000.0)
    weight = jnp.exp(scores - jnp.max(scores, axis=-1, keepdims=True))
    return weight / jnp.sum(weight, axis=-1, keepdims=True), queries, keys, values


def first_lanes(shape):
    return lax.broadcasted_iota(jnp.int32, shape, 1) < HD


def one_head(x, half):
    keep = first_lanes(x.shape) if half == 0 else jnp.logical_not(first_lanes(x.shape))
    return jnp.where(keep, x, jnp.zeros_like(x))


def side_by_side(left, right):
    return jnp.where(first_lanes(left.shape), left, right)


def attention_kernel(count, q_ref, valid_ref, *refs):
    blocks, out = refs[:count], refs[count]
    valid = jnp.broadcast_to(valid_ref[...] > 0, (q_ref.shape[0], valid_ref.shape[1]))
    for pair in range(q_ref.shape[1] // (2 * HD)):
        both = []
        for half in range(2):
            probs, _, _, values = head_pair(q_ref, blocks, valid, pair, half)
            both.append(plain_dot(probs.astype(jnp.bfloat16), values))
        out[:, pl.ds(pair * 2 * HD, 2 * HD)] = side_by_side(*both).astype(out.dtype)


def attention_back_kernel(count, q_ref, valid_ref, seed_ref, *refs):
    blocks, q_out, outs = refs[:count], refs[count], refs[count + 1 :]
    rows, features = q_ref.shape
    scale = 1.0 / math.sqrt(HD)
    valid = jnp.broadcast_to(valid_ref[...] > 0, (rows, valid_ref.shape[1]))
    for pair in range(features // (2 * HD)):
        cols = pl.ds(pair * 2 * HD, 2 * HD)
        seed = seed_ref[:, cols]
        q_both, k_both, v_both = [], [], []
        for half in range(2):
            probs, queries, keys, values = head_pair(q_ref, blocks, valid, pair, half)
            probs_grad = back_dot(one_head(seed, half), values)
            inner = jnp.sum(probs * probs_grad, axis=-1, keepdims=True)
            score_grad = (probs * (probs_grad - inner)).astype(jnp.bfloat16)
            q_both.append(plain_dot(score_grad, keys))
            k_both.append(grad_dot(score_grad, queries))
            v_both.append(grad_dot(probs.astype(jnp.bfloat16), seed))
        q_out[:, cols] = (side_by_side(*q_both) * scale).astype(q_out.dtype)
        k_grad = (side_by_side(*k_both) * scale).astype(jnp.bfloat16)
        v_grad = side_by_side(*v_both).astype(jnp.bfloat16)
        for j, out in enumerate(outs):
            out[:, cols] = k_grad[j * rows : (j + 1) * rows]
            out[:, pl.ds(features + pair * 2 * HD, 2 * HD)] = v_grad[j * rows : (j + 1) * rows]


def attention_cost(rows, blocks, features, products):
    span = rows * len(blocks)
    return pl.CostEstimate(
        flops=2 * products * rows * span * features,
        bytes_accessed=8 * span * features,
        transcendentals=rows * span * (features // HD),
    )


def attention(queries, valid, blocks):
    rows, features = queries.shape
    vmem = pl.BlockSpec(memory_space=pltpu.VMEM)
    return pl.pallas_call(
        functools.partial(attention_kernel, len(blocks)),
        out_shape=jax.ShapeDtypeStruct((rows, features), jnp.bfloat16),
        in_specs=[vmem] * (2 + len(blocks)),
        out_specs=vmem,
        cost_estimate=attention_cost(rows, blocks, features, 2),
    )(queries, valid, *blocks)


def attention_back(queries, valid, seed, blocks):
    rows, features = queries.shape
    vmem = pl.BlockSpec(memory_space=pltpu.VMEM)
    return pl.pallas_call(
        functools.partial(attention_back_kernel, len(blocks)),
        out_shape=[jax.ShapeDtypeStruct((rows, features), jnp.bfloat16)]
        + [jax.ShapeDtypeStruct((rows, 2 * features), jnp.bfloat16)] * len(blocks),
        in_specs=[vmem] * (3 + len(blocks)),
        out_specs=[vmem] * (1 + len(blocks)),
        cost_estimate=attention_cost(rows, blocks, features, 5),
    )(queries, valid, seed, *blocks)


def from_next(x, axis, step):
    size = lax.axis_size(axis)
    return lax.ppermute(x, axis, [((i + step) % size, i) for i in range(size)])


def to_next(x, axis, step):
    size = lax.axis_size(axis)
    return lax.ppermute(x, axis, [(i, (i + step) % size) for i in range(size)])


def norm_back(residual, row_gain, seed):
    centered = residual - jnp.mean(residual, axis=-1, keepdims=True)
    spread = jnp.mean(centered * centered, axis=-1, keepdims=True)
    scale = lax.rsqrt(spread + eps)
    unit = centered * scale
    inner = seed * row_gain
    drop = jnp.mean(inner, axis=-1, keepdims=True) + unit * jnp.mean(inner * unit, axis=-1, keepdims=True)
    gain_grad = jnp.sum(seed * unit, axis=0, keepdims=True)
    return scale * (inner - drop), gain_grad, jnp.sum(seed, axis=0, keepdims=True)


def place_norms(gain, bias, index, devices):
    both = jnp.concatenate([gain, bias], 0)
    width = both.shape[1]
    shape = (width, devices * width)
    spot = lax.broadcasted_iota(jnp.int32, shape, 0) + index * width == lax.broadcasted_iota(jnp.int32, shape, 1)
    placed = plain_dot(both, spot.astype(both.dtype)).astype(both.dtype)
    return jnp.pad(placed, ((0, 8 - both.shape[0]), (0, 0)))


def local(
    hidden,
    char_ids,
    groups,
    lengths,
    cotangent,
    qkv_weight,
    out_weight,
    up_weight,
    down_weight,
    norm_gain,
    norm_bias,
    char_table,
    gru_input,
    gru_recur,
    merge_weight,
    conv_weight,
):
    dp_size, devices = lax.axis_size("dp"), lax.axis_size("dp") * lax.axis_size("seq")
    me = lax.axis_index("dp") * lax.axis_size("seq") + lax.axis_index("seq")
    norms = place_norms(norm_gain, norm_bias, me, devices)
    order = (char_table, gru_input, gru_recur, norms, qkv_weight, out_weight, up_weight, down_weight, merge_weight, conv_weight)
    gathered = gather_all(dp_size, devices, order, (6, 9))
    all_norms = jnp.sum(gathered[3].astype(jnp.float32), axis=0)
    (full_table, full_input, full_recur, _, full_qkv, full_out, full_up, full_down, full_merge, full_conv) = [
        x.reshape(-1, x.shape[2]) for x in gathered
    ]
    seq_count, local_len, features = hidden.shape
    nchar = char_ids.shape[2]
    tokens = seq_count * local_len
    key_span = local_len * lax.axis_size("seq")
    gains = [all_norms[k : k + 1] for k in range(3)]
    biases = [all_norms[k : k + 1] for k in range(3, 6)]
    flat_in = hidden.reshape(tokens, features)
    qkv = plain_dot(flat_in, full_qkv).astype(jnp.bfloat16)
    queries, own_kv = qkv[:, :features], qkv[:, features:]
    peers = lax.axis_size("seq")
    kv_blocks = [own_kv] + [from_next(own_kv, "seq", j) for j in range(1, peers)]
    place = lax.rem(lax.axis_index("seq") + jnp.arange(peers), peers) * local_len
    positions = place[:, None] + jnp.arange(local_len)[None, :]
    key_valid = (positions < lengths[0]).astype(jnp.int32).reshape(1, key_span)
    assert seq_count == 1
    flat_ids = char_ids.reshape(tokens, nchar)
    table_start = groups[0] * SUBV
    own_table = lax.dynamic_slice_in_dim(full_table, table_start, SUBV, 0)
    inward = full_input.reshape(2, -1, full_input.shape[1])
    recurrent = full_recur.reshape(2, -1, full_recur.shape[1])
    char_vec, char_emb, *kept = gru_forward(flat_ids, own_table, inward, recurrent)
    factors, keeps, priors = kept[:2], kept[2:4], kept[4:]
    attended = attention(queries, key_valid, kv_blocks)
    resid_one = flat_in.astype(jnp.float32) + plain_dot(attended, full_out)
    norm_one = norm_rows(resid_one, gains[0], biases[0]).astype(jnp.bfloat16)
    up_proj = plain_dot(norm_one, full_up)
    active = gelu_exact(up_proj).astype(jnp.bfloat16)
    resid_two = norm_one.astype(jnp.float32) + plain_dot(active, full_down)
    norm_two = norm_rows(resid_two, gains[1], biases[1]).astype(jnp.bfloat16)
    merge_mats = full_merge.reshape(2, features, features)
    streams = jnp.stack([norm_two, char_vec], 0)
    merged_pair = jnp.einsum("btd,bdf->btf", streams, merge_mats, preferred_element_type=jnp.float32)
    merged_rows = jnp.concatenate([merged_pair[0], merged_pair[1]], -1).astype(jnp.bfloat16)
    padded = with_halo(merged_rows.reshape(seq_count, local_len, 2 * features), (("seq", 1),), 1)
    kernel = full_conv.reshape(3, 2 * features, features)
    windows = [
        padded[:, offset : offset + local_len].reshape(tokens, 2 * features) for offset in range(3)
    ]
    conv_out = (
        plain_dot(windows[0], kernel[0])
        + plain_dot(windows[1], kernel[1])
        + plain_dot(windows[2], kernel[2])
    )
    resid_three = norm_two.astype(jnp.float32) + conv_out
    result = norm_rows(resid_three, gains[2], biases[2]).astype(jnp.bfloat16).reshape(seq_count, local_len, features)
    back_qkv, back_out, back_up, back_down = full_qkv, full_out, full_up, full_down
    back_merge, back_conv = full_merge, full_conv
    merge_back = back_merge.reshape(2, features, features)
    kernel_back = back_conv.reshape(3, 2 * features, features)
    seed_rows = cotangent.reshape(tokens, features).astype(jnp.float32)
    grad_three, gain_three, bias_three = norm_back(resid_three, gains[2], seed_rows)
    conv_seed = grad_three.astype(jnp.bfloat16)
    conv_grad = grad_dot(jnp.concatenate(windows, 1), conv_seed)
    seed_padded = with_halo(conv_seed.reshape(seq_count, local_len, features), (("seq", 1),), 1)
    merged_grad = back_dot(
        seed_padded[:, 2 : 2 + local_len].reshape(tokens, features), kernel_back[0]
    )
    merged_grad = merged_grad + back_dot(
        seed_padded[:, 1 : 1 + local_len].reshape(tokens, features), kernel_back[1]
    )
    merged_grad = merged_grad + back_dot(
        seed_padded[:, 0:local_len].reshape(tokens, features), kernel_back[2]
    )
    merged_grad = merged_grad.astype(jnp.bfloat16)
    pair_grad = jnp.stack([merged_grad[:, :features], merged_grad[:, features:]], 0)
    merge_grad = jnp.einsum("btd,btf->bdf", streams, pair_grad, preferred_element_type=jnp.float32)
    stream_grad = jnp.einsum("btf,bdf->btd", pair_grad, merge_back, preferred_element_type=jnp.float32)
    two_grad = grad_three + stream_grad[0]
    charvec_grad = stream_grad[1]
    grad_two, gain_two, bias_two = norm_back(resid_two, gains[1], two_grad)
    down_seed = grad_two.astype(jnp.bfloat16)
    down_grad = grad_dot(active, down_seed)
    active_grad = back_dot(down_seed, back_down)
    _, pull_gelu = jax.vjp(gelu_exact, up_proj)
    up_seed = pull_gelu(active_grad)[0].astype(jnp.bfloat16)
    up_grad = grad_dot(norm_one, up_seed)
    one_grad = grad_two + back_dot(up_seed, back_up)
    grad_one, gain_one, bias_one = norm_back(resid_one, gains[0], one_grad)
    out_seed = grad_one.astype(jnp.bfloat16)
    out_grad = grad_dot(attended, out_seed)
    attn_seed = back_dot(out_seed, back_out).astype(jnp.bfloat16)
    query_grad, *kv_grads = attention_back(queries, key_valid, attn_seed, kv_blocks)
    kv_own = kv_grads[0].astype(jnp.float32)
    for j in range(1, peers):
        kv_own = kv_own + to_next(kv_grads[j], "seq", j).astype(jnp.float32)
    qkv_seed = jnp.concatenate([query_grad, kv_own.astype(jnp.bfloat16)], -1)
    qkv_grad = grad_dot(flat_in, qkv_seed)
    hidden_grad = (
        (grad_one + back_dot(qkv_seed, back_qkv))
        .astype(jnp.bfloat16)
        .reshape(seq_count, local_len, features)
    )
    input_mats, recur_sum, own_grad = gru_backward(
        flat_ids, charvec_grad, inward, recurrent, char_emb, *priors, *factors, *keeps, SUBV
    )
    table_grad = jnp.zeros(full_table.shape, jnp.bfloat16)
    table_grad = lax.dynamic_update_slice_in_dim(table_grad, own_grad.astype(jnp.bfloat16), table_start, 0)
    norm_grads = jnp.concatenate(
        [gain_one, gain_two, gain_three, bias_one, bias_two, bias_three, jnp.zeros((2, features), jnp.float32)], 0
    )
    terms = [input_mats, recur_sum, merge_grad, conv_grad, down_grad, up_grad, qkv_grad, out_grad, table_grad]
    parts = [x.astype(jnp.bfloat16).reshape(devices, -1, x.shape[-1]) for x in terms]
    width = norm_gain.shape[1]
    *sums, norm_sum = scatter_all(dp_size, parts, norm_grads, width, (3, 6))
    input_total, recur_total, merge_sum, conv_sum, down_sum, up_sum, qkv_sum, out_sum, table_sum = settle(sums)
    skip = me * width - window_start(me, width, features)
    gain_sum = lax.dynamic_slice(norm_sum, (0, skip), (3, width))
    bias_sum = lax.dynamic_slice(norm_sum, (3, skip), (3, width))
    return (result, hidden_grad, qkv_sum, out_sum, up_sum, down_sum, gain_sum, bias_sum, table_sum, input_total, recur_total, merge_sum, conv_sum)


def solution(mesh):
    placed = (
        P("dp", "seq", None),
        P("dp", "seq", None),
        P("dp"),
        P("dp"),
        P("dp", "seq", None),
        P(("dp", "seq"), None),
        P(("dp", "seq"), None),
        P(("dp", "seq"), None),
        P(("dp", "seq"), None),
        P(None, ("dp", "seq")),
        P(None, ("dp", "seq")),
        P(("dp", "seq"), None),
        P(("dp", "seq"), None),
        P(("dp", "seq"), None),
        P(("dp", "seq"), None),
        P(("dp", "seq"), None),
    )
    return jax.shard_map(
        local,
        mesh=mesh,
        in_specs=placed,
        out_specs=(
            P("dp", "seq", None),
            P("dp", "seq", None),
            P(("dp", "seq"), None),
            P(("dp", "seq"), None),
            P(("dp", "seq"), None),
            P(("dp", "seq"), None),
            P(None, ("dp", "seq")),
            P(None, ("dp", "seq")),
            P(("dp", "seq"), None),
            P(("dp", "seq"), None),
            P(("dp", "seq"), None),
            P(("dp", "seq"), None),
            P(("dp", "seq"), None),
        ),
        check_vma=False,
    )
```

```python
import functools
import math

import jax
import jax.numpy as jnp
from jax import lax
from jax.experimental import pallas as pl
from jax.experimental.pallas import tpu as pltpu
from jax.sharding import PartitionSpec as P

MESH = pl.DeviceIdType.MESH

HD = 64
SUBV = 128

eps = 1e-05

class Place:
    def __init__(self, dp_size):
        dp, seq = lax.axis_index("dp"), lax.axis_index("seq")
        self.lines = dp_size // 2
        self.a, self.b = dp // 2, lax.rem(dp, 2)
        self.y, self.c = seq // 2, lax.rem(seq, 2)
        flip_b = (self.a * 2 + 1 - self.b, seq)
        flip_y = (dp, (1 - self.y) * 2 + self.c)
        pick = lambda u, v: tuple(i + self.c * (j - i) for i, j in zip(u, v))
        self.first, self.second = pick(flip_b, flip_y), pick(flip_y, flip_b)
        self.sibling = (dp, self.y * 2 + 1 - self.c)
        self.up, self.down = (dp + 2, seq), (dp - 2, seq)
        self.f = self.b + self.c * (self.y - self.b)
        self.s = self.y + self.c * (self.b - self.y)
        self.has_up, self.has_down = self.a < self.lines - 1, self.a > 0

    def unit(self, a, f, s, c=None):
        c = self.c if c is None else c
        return a * 8 + f * (4 - 2 * c) + s * (2 + 2 * c) + c

    def barrier(self):
        sem = pltpu.get_barrier_semaphore()
        for who in (self.first, self.second, self.sibling):
            pl.semaphore_signal(sem, inc=1, device_id=who, device_id_type=MESH)

        @pl.when(self.has_up)
        def _():
            pl.semaphore_signal(sem, inc=1, device_id=self.up, device_id_type=MESH)

        @pl.when(self.has_down)
        def _():
            pl.semaphore_signal(sem, inc=1, device_id=self.down, device_id_type=MESH)

        pl.semaphore_wait(sem, 3 + self.has_up.astype(jnp.int32) + self.has_down.astype(jnp.int32))


def push(src, dst, send, recv, who):
    return pltpu.make_async_remote_copy(
        src_ref=src, dst_ref=dst, send_sem=send, recv_sem=recv, device_id=who, device_id_type=MESH
    )


class Gather:
    def __init__(self, at, shard, full, sems):
        self.at, self.shard, self.full = at, shard, full
        self.up_s, self.down_s, self.sum_s, self.line_r, self.second_r, self.one = sems

    def to_lines(self, src, slot, index, up, down):
        at = self.at
        if up is not False:
            @pl.when(at.has_up if up is True else jnp.logical_and(up, at.has_up))
            def _():
                push(src, self.full.at[index], self.up_s.at[slot], self.line_r.at[slot], at.up).start()
        if down is not False:
            @pl.when(at.has_down if down is True else jnp.logical_and(down, at.has_down))
            def _():
                push(src, self.full.at[index], self.down_s.at[slot], self.line_r.at[slot], at.down).start()

    def across(self, src, slot, index):
        push(src, self.full.at[index], self.sum_s.at[0], self.second_r.at[slot], self.at.second).start()
        self.aside(src, index)

    def aside(self, src, index):
        push(src, self.full.at[index], self.sum_s.at[1], self.one.at[1], self.at.sibling).start()

    def begin(self):
        at = self.at
        me = at.unit(at.a, at.f, at.s)
        pltpu.make_async_copy(self.shard, self.full.at[me], self.one.at[3]).start()
        push(self.shard, self.full.at[me], self.one.at[2], self.one.at[0], at.first).start()
        slot = at.a * 2 + at.f
        self.to_lines(self.shard, slot, me, True, True)
        self.across(self.shard, slot, me)

    def after_first(self):
        at = self.at
        index = at.unit(at.a, 1 - at.f, at.s)
        ref = self.full.at[index]
        push(ref, ref, self.one.at[2], self.one.at[0], at.first).wait_recv()
        slot = at.a * 2 + 1 - at.f
        self.to_lines(ref, slot, index, True, True)
        self.across(ref, slot, index)

    def after_line(self, k, g):
        at = self.at
        for sign in (-1, 1):
            a = at.a + sign * k
            f = at.f if g == 0 else 1 - at.f

            @pl.when(a >= 0 if sign < 0 else a < at.lines)
            def _():
                index, slot = at.unit(a, f, at.s), a * 2 + f
                ref = self.full.at[index]
                push(ref, ref, self.up_s.at[slot], self.line_r.at[slot], at.up).wait_recv()
                self.to_lines(ref, slot, index, sign < 0, sign > 0)
                self.across(ref, slot, index)

    def after_second(self, k, g):
        at = self.at
        for sign in (-1, 1) if k else (1,):
            a = at.a + sign * k
            f = at.f if g == 0 else 1 - at.f

            @pl.when(a >= 0 if sign < 0 else a < at.lines)
            def _():
                index, slot = at.unit(a, f, 1 - at.s), a * 2 + f
                ref = self.full.at[index]
                push(ref, ref, self.sum_s.at[0], self.second_r.at[slot], at.second).wait_recv()
                self.aside(ref, index)

    def finish(self):
        at, n = self.at, self.at.lines
        me = at.unit(at.a, at.f, at.s)
        half = self.full.at[pl.ds(0, 4 * n)]
        push(half, half, self.sum_s.at[1], self.one.at[1], at.sibling).wait_recv()
        pltpu.make_async_copy(self.shard, self.full.at[me], self.one.at[3]).wait()
        push(self.shard, self.full.at[me], self.one.at[2], self.one.at[0], at.first).wait_send()
        push(half, half, self.sum_s.at[1], self.one.at[1], at.sibling).wait_send()
        part = self.full.at[pl.ds(0, 2 * n)]
        push(part, part, self.sum_s.at[0], self.one.at[0], at.second).wait_send()
        for a in range(n):
            for f in range(2):
                slot = a * 2 + f
                ref = self.full.at[0]

                @pl.when(jnp.logical_and(at.has_up, a <= at.a))
                def _():
                    push(ref, ref, self.up_s.at[slot], self.line_r.at[slot], at.up).wait_send()

                @pl.when(jnp.logical_and(at.has_down, a >= at.a))
                def _():
                    push(ref, ref, self.down_s.at[slot], self.line_r.at[slot], at.down).wait_send()


class LineGather(Gather):
    def begin(self):
        at = self.at
        me = at.unit(at.a, at.f, at.s)
        pltpu.make_async_copy(self.shard, self.full.at[me], self.one.at[3]).start()
        self.to_lines(self.shard, at.a, me, True, True)
        self.to_pairs(self.shard, at.a, me)

    def to_pairs(self, src, a, index):
        at = self.at
        push(src, self.full.at[index], self.one.at[2], self.line_r.at[at.lines + a], at.first).start()
        self.across(src, a * 2 + at.f, index)

    def after_first(self):
        self.from_first(0)

    def from_first(self, k):
        at = self.at
        for sign in (-1, 1) if k else (1,):
            a = at.a + sign * k

            @pl.when(a >= 0 if sign < 0 else a < at.lines)
            def _():
                index = at.unit(a, 1 - at.f, at.s)
                ref = self.full.at[index]
                push(ref, ref, self.one.at[2], self.line_r.at[at.lines + a], at.first).wait_recv()
                self.across(ref, a * 2 + 1 - at.f, index)

    def after_line(self, k, g):
        at = self.at
        if g:
            self.from_first(k)
            return
        for sign in (-1, 1):
            a = at.a + sign * k

            @pl.when(a >= 0 if sign < 0 else a < at.lines)
            def _():
                index = at.unit(a, at.f, at.s)
                ref = self.full.at[index]
                push(ref, ref, self.up_s.at[a], self.line_r.at[a], at.up).wait_recv()
                self.to_lines(ref, a, index, sign < 0, sign > 0)
                self.to_pairs(ref, a, index)

    def finish(self):
        at, n = self.at, self.at.lines
        me = at.unit(at.a, at.f, at.s)
        half = self.full.at[pl.ds(0, 4 * n)]
        push(half, half, self.sum_s.at[1], self.one.at[1], at.sibling).wait_recv()
        pltpu.make_async_copy(self.shard, self.full.at[me], self.one.at[3]).wait()
        push(half, half, self.sum_s.at[1], self.one.at[1], at.sibling).wait_send()
        line = self.full.at[pl.ds(0, n)]
        push(line, line, self.one.at[2], self.one.at[0], at.first).wait_send()
        part = self.full.at[pl.ds(0, 2 * n)]
        push(part, part, self.sum_s.at[0], self.one.at[0], at.second).wait_send()
        ref = self.full.at[0]
        for a in range(n):
            @pl.when(jnp.logical_and(at.has_up, a <= at.a))
            def _():
                push(ref, ref, self.up_s.at[a], self.line_r.at[a], at.up).wait_send()

            @pl.when(jnp.logical_and(at.has_down, a >= at.a))
            def _():
                push(ref, ref, self.down_s.at[a], self.line_r.at[a], at.down).wait_send()


def gather_sems(n):
    dma = pltpu.SemaphoreType.DMA
    return [dma((2 * n,)), dma((2 * n,)), dma((2,)), dma((2 * n,)), dma((2 * n,)), dma((4,))]


def gather_kernel(dp_size, count, early, *refs):
    shards, fulls, sems = refs[:count], refs[count : 2 * count], refs[2 * count :]
    at = Place(dp_size)
    at.barrier()
    kinds = [LineGather if i in early else Gather for i in range(count)]
    jobs = [kinds[i](at, shards[i], fulls[i], sems[6 * i : 6 * i + 6]) for i in range(count)]
    for job in jobs:
        job.begin()
    for job in jobs:
        job.after_first()
    for k in range(1, at.lines):
        for g in range(2):
            for job in jobs:
                job.after_line(k, g)
            for job in jobs:
                job.after_second(k - 1, g)
    for g in range(2):
        for job in jobs:
            job.after_second(at.lines - 1, g)
    for job in jobs:
        job.finish()


def gather_all(dp_size, devices, shards, early, cid=1):
    count = len(shards)
    return pl.pallas_call(
        functools.partial(gather_kernel, dp_size, count, early),
        out_shape=[jax.ShapeDtypeStruct((devices,) + x.shape, x.dtype) for x in shards],
        in_specs=[pl.BlockSpec(memory_space=pl.ANY)] * count,
        out_specs=[pl.BlockSpec(memory_space=pl.ANY)] * count,
        scratch_shapes=gather_sems(dp_size // 2) * count,
        compiler_params=pltpu.CompilerParams(collective_id=cid, has_side_effects=True),
    )(*shards)


def wide(x):
    return x.astype(jnp.float32)


def add_into(dst, src):
    dst[...] = dst[...] + src[...]


class Scatter:
    def __init__(self, at, part, out, bufs, sems):
        self.at, self.part, self.out = at, part, out
        self.own, self.sib, self.sec, self.line, self.fst = bufs
        self.per = 2
        self.one, self.line_s, self.line_r = sems

    def begin(self):
        at = self.at

        def body(j, carry):
            a, f, s = j // 4, lax.rem(j // 2, 2), lax.rem(j, 2)
            push(self.part(at.unit(a, f, s, 1 - at.c)), self.sib.at[j], self.one.at[0], self.one.at[1], at.sibling).start()
            return carry

        lax.fori_loop(0, 4 * at.lines, body, 0)

        def load(j, carry):
            a, f, s = j // 4, lax.rem(j // 2, 2), lax.rem(j, 2)
            pltpu.make_async_copy(self.part(at.unit(a, f, s)), self.own.at[j], self.one.at[2]).start()
            return carry

        lax.fori_loop(0, 4 * at.lines, load, 0)

    def after_sibling(self):
        at = self.at
        n = 2 * at.lines
        pltpu.make_async_copy(self.own, self.own, self.one.at[2]).wait()
        push(self.sib, self.sib, self.one.at[0], self.one.at[1], at.sibling).wait_recv()

        def far(q, carry):
            j = q * 2 + 1 - at.s
            add_into(self.own.at[j], self.sib.at[j])
            return carry

        def send(q, carry):
            push(self.own.at[q * 2 + 1 - at.s], self.sec.at[q], self.one.at[3], self.one.at[4], at.second).start()
            return carry

        def near(q, carry):
            j = q * 2 + at.s
            add_into(self.own.at[j], self.sib.at[j])
            return carry

        lax.fori_loop(0, n, far, 0)
        lax.fori_loop(0, n, send, 0)
        lax.fori_loop(0, n, near, 0)

    def after_second(self):
        at = self.at
        push(self.sec, self.sec, self.one.at[3], self.one.at[4], at.second).wait_recv()

        def body(q, carry):
            add_into(self.own.at[q * 2 + at.s], self.sec.at[q])
            return carry

        lax.fori_loop(0, 2 * at.lines, body, 0)

    def spot(self, q):
        return q * 2 + self.at.s

    def hop(self, low, high, inward, dst, extra):
        at = self.at
        has, who = (at.has_up, at.down) if dst < 0 else (at.has_down, at.up)

        def take(q, carry):
            push(self.line.at[q], self.line.at[q], self.line_s.at[q], self.line_r.at[q], who).wait_recv()
            add_into(self.own.at[self.spot(q)], self.line.at[q])
            return carry

        @pl.when(has)
        def _():
            lax.fori_loop(low, high, take, 0)

        def send(q, carry):
            per = self.per
            slot = q if dst < 0 else jnp.where(q // per == at.a + 1, per * at.lines + lax.rem(q, per), q)
            push(self.own.at[self.spot(q)], self.line.at[slot], self.line_s.at[q], self.line_r.at[slot], who).start()
            return carry

        lax.fori_loop(low, high, send, 0)

    def along(self, h):
        at = self.at
        n = at.lines
        hops = n - 1 if n <= 4 else 1

        @pl.when(jnp.logical_and(at.has_down, at.lines - 1 - at.a == h) if hops > 1 else at.has_down)
        def _():
            self.hop(0, self.per * at.a, at.up, -1, None)

        @pl.when(jnp.logical_and(at.has_up, at.a == h) if hops > 1 else at.has_up)
        def _():
            self.hop(self.per * (at.a + 1), self.per * n, at.down, 1, None)

    def ends(self, f, into):
        at = self.at
        for has, slot in ((at.has_up, 2 * at.a + f), (at.has_down, 2 * at.lines + f)):
            @pl.when(has)
            def _():
                ref = self.line.at[slot]
                push(ref, ref, self.line_s.at[0], self.line_r.at[slot], at.first).wait_recv()
                into[...] = (wide(into[...]) + wide(ref[...])).astype(into.dtype)

    def last_send(self):
        at = self.at
        mine = self.own.at[(2 * at.a + 1 - at.f) * 2 + at.s]
        self.ends(1 - at.f, mine)
        push(mine, self.fst, self.one.at[5], self.one.at[6], at.first).start()
        self.out[...] = wide(self.own[(2 * at.a + at.f) * 2 + at.s])
        self.ends(at.f, self.out)

    def finish(self):
        at = self.at
        push(self.fst, self.fst, self.one.at[5], self.one.at[6], at.first).wait_recv()
        self.out[...] = self.out[...] + wide(self.fst[...])

    def drain(self):
        at = self.at
        n = at.lines
        push(self.sib, self.sib, self.one.at[0], self.one.at[1], at.sibling).wait_send()
        push(self.sec, self.sec, self.one.at[3], self.one.at[4], at.second).wait_send()
        push(self.fst, self.fst, self.one.at[5], self.one.at[6], at.first).wait_send()

        def body(q, carry):
            @pl.when(q // self.per != at.a)
            def _():
                push(self.own.at[q], self.own.at[q], self.line_s.at[q], self.line_r.at[q], at.first).wait_send()
            return carry

        lax.fori_loop(0, self.per * n, body, 0)

    def stages(self):
        return [type(self).after_sibling, type(self).after_second] + self.hops() + [type(self).last_send, type(self).finish]

    def hops(self):
        lines = self.at.lines
        return [functools.partial(type(self).along, h=h) for h in range(lines - 1 if lines <= 4 else 1)]


class LineScatter(Scatter):
    def __init__(self, *args):
        super().__init__(*args)
        self.per = 1

    def spot(self, q):
        return (2 * q + self.at.f) * 2 + self.at.s

    def after_second(self):
        super().after_second()
        at = self.at

        def send(a, carry):
            push(self.own.at[(2 * a + 1 - at.f) * 2 + at.s], self.fst.at[a], self.one.at[5], self.one.at[6], at.first).start()
            return carry

        lax.fori_loop(0, at.lines, send, 0)

    def after_first(self):
        at = self.at
        push(self.fst, self.fst, self.one.at[5], self.one.at[6], at.first).wait_recv()

        def body(a, carry):
            add_into(self.own.at[self.spot(a)], self.fst.at[a])
            return carry

        lax.fori_loop(0, at.lines, body, 0)

    def finish(self):
        at = self.at
        self.out[...] = wide(self.own[self.spot(at.a)])
        for has, slot in ((at.has_up, at.a), (at.has_down, at.lines)):
            @pl.when(has)
            def _():
                ref = self.line.at[slot]
                push(ref, ref, self.line_s.at[0], self.line_r.at[slot], at.first).wait_recv()
                self.out[...] = self.out[...] + wide(ref[...])

    def stages(self):
        kind = type(self)
        return [kind.after_sibling, kind.after_second, kind.after_first] + self.hops() + [kind.finish]


def scatter_buffers(n, shape, dtype, late):
    v = lambda k: pltpu.VMEM((k,) + shape, dtype)
    return [v(4 * n), v(4 * n), v(2 * n)] + ([v(n + 1), v(n)] if late else [v(2 * n + 2), pltpu.VMEM(shape, dtype)])


def scatter_sems(n):
    dma = pltpu.SemaphoreType.DMA
    return [dma((7,)), dma((2 * n,)), dma((2 * n + 2,))]


LANES = 128
AHEAD = 3
ROUNDS = (0, 2, 4, 6, 8, 10, 12)


def window_start(unit, width, features):
    tile = unit * width // LANES
    return (tile - tile // (features // LANES - 1)) * LANES


def whole_part(ref, rows, cols):
    return lambda unit: ref.at[unit, pl.ds(*rows), pl.ds(*cols)]


def window_part(ref, width):
    features = ref.shape[1]
    return lambda unit: ref.at[:, pl.ds(pl.multiple_of(window_start(unit, width, features), LANES), 2 * LANES)]


def cut(shape, cap):
    rows, cols = shape
    pieces = max(1, round(rows * cols / cap))
    while pieces > 1 and not (rows % (16 * pieces) == 0 or cols % (LANES * pieces) == 0):
        pieces -= 1
    if rows % (16 * pieces) == 0:
        step = rows // pieces
        return [((k * step, step), (0, cols)) for k in range(pieces)]
    step = cols // pieces
    return [((0, rows), (k * step, step)) for k in range(pieces)]


def weave(many, few):
    order, i, j = [], 0, 0
    while i < len(many) or j < len(few):
        if j < len(few) and (2 * j + 1) * len(many) <= (2 * i + 1) * len(few):
            order.append(few[j])
            j += 1
        else:
            order.append(many[i])
            i += 1
    return order


def scatter_kernel(dp_size, chunks, count, width, late, *refs):
    parts, outs, rest = refs[:count], refs[count : 2 * count], refs[2 * count :]
    at = Place(dp_size)
    at.barrier()
    jobs = []
    for k, (i, rows, cols) in enumerate(chunks):
        last = i == count - 1
        part = window_part(parts[i], width) if last else whole_part(parts[i], rows, cols)
        out = outs[i] if last else outs[i].at[pl.ds(*rows), pl.ds(*cols)]
        kind = LineScatter if i in late else Scatter
        jobs.append(kind(at, part, out, rest[8 * k : 8 * k + 5], rest[8 * k + 5 : 8 * k + 8]))
    total = len(jobs)
    for job in jobs[:AHEAD]:
        job.begin()
    stages = [job.stages() for job in jobs]
    depth = len(stages[0])
    for t in range(total + ROUNDS[depth - 1]):
        if t + AHEAD < total:
            jobs[t + AHEAD].begin()
        for k in range(depth):
            j = t - ROUNDS[k]
            if 0 <= j < total:
                stages[j][k](jobs[j])
    for job in jobs:
        job.drain()


def scatter_all(dp_size, parts, norm_rows, width, late, cap=18432, cid=2):
    count = len(parts) + 1
    n = dp_size // 2
    outs = [jax.ShapeDtypeStruct(x.shape[1:], jnp.float32) for x in parts]
    outs.append(jax.ShapeDtypeStruct((norm_rows.shape[0], 2 * LANES), jnp.float32))
    pieces = [(i, *piece) for i, x in enumerate(parts) for piece in cut(x.shape[1:], cap)]
    chunks = weave([p for p in pieces if p[0] not in late], [p for p in pieces if p[0] in late])
    scratch = []
    for i, rows, cols in chunks:
        scratch += scatter_buffers(n, (rows[1], cols[1]), parts[i].dtype, i in late) + scatter_sems(n)
    chunks.append((count - 1, None, None))
    scratch += scatter_buffers(n, outs[-1].shape, jnp.float32, count - 1 in late) + scatter_sems(n)
    return pl.pallas_call(
        functools.partial(scatter_kernel, dp_size, chunks, count, width, late),
        out_shape=outs,
        in_specs=[pl.BlockSpec(memory_space=pl.ANY)] * count,
        out_specs=[pl.BlockSpec(memory_space=pltpu.VMEM)] * count,
        scratch_shapes=scratch,
        compiler_params=pltpu.CompilerParams(collective_id=cid, has_side_effects=True, vmem_limit_bytes=64000000),
    )(*parts, norm_rows)


def settle_kernel(*refs):
    half = len(refs) // 2
    for src, dst in zip(refs[:half], refs[half:]):
        dst[...] = src[...]


def settle(arrays):
    spec = [pl.BlockSpec(memory_space=pltpu.VMEM)] * len(arrays)
    return pl.pallas_call(
        settle_kernel,
        out_shape=[jax.ShapeDtypeStruct(x.shape, x.dtype) for x in arrays],
        in_specs=spec,
        out_specs=spec,
    )(*arrays)


def with_halo(x, sides, width):
    for axis, dim in sides:
        devices, length = (lax.axis_size(axis), x.shape[dim])
        up = [(i, (i + 1) % devices) for i in range(devices - 1)]
        down = [(j, i) for i, j in up]
        last = lax.slice_in_dim(x, length - width, length, axis=dim)
        first = lax.slice_in_dim(x, 0, width, axis=dim)
        before = lax.ppermute(last, axis, up)
        after = lax.ppermute(first, axis, down)
        x = jnp.concatenate([before, x, after], axis=dim)
    return x


def norm_rows(residual, row_gain, row_bias):
    centered = residual - jnp.mean(residual, axis=-1, keepdims=True)
    spread = jnp.mean(centered * centered, axis=-1, keepdims=True)
    return centered * lax.rsqrt(spread + eps) * row_gain + row_bias


def gelu_exact(pre_act):
    return jax.nn.gelu(pre_act, approximate=False)


def plain_dot(left, right):
    return jnp.dot(left, right, preferred_element_type=jnp.float32)


def grad_dot(left, right):
    return lax.dot_general(
        left, right, (((0,), (0,)), ((), ())), preferred_element_type=jnp.float32
    )


def back_dot(left, right):
    return lax.dot_general(
        left, right, (((1,), (1,)), ((), ())), preferred_element_type=jnp.float32
    )


def squash(x):
    return 0.5 * jnp.tanh(0.5 * x) + 0.5


def slot_onehot(ids, slots, subset):
    cols = lax.broadcasted_iota(jnp.int32, (ids.shape[0], subset), 1)
    hots = [(ids[:, s : s + 1] == cols).astype(jnp.bfloat16) for s in slots]
    return jnp.concatenate(hots, 0)


def gru_embed(ids_ref, table, w_in, emb_ref, gates, chunk=4):
    rows, nchar = ids_ref.shape
    ids = ids_ref[...]
    for k in range(0, nchar, chunk):
        hot = slot_onehot(ids, range(k, k + chunk), table.shape[0])
        emb = plain_dot(hot, table[...]).astype(jnp.bfloat16)
        emb_ref[k : k + chunk] = emb.reshape(chunk, rows, -1)
        for d in range(2):
            gates[d, k : k + chunk] = plain_dot(emb, w_in[d]).reshape(chunk, rows, -1)


def gru_step(d, slot, count, gates, w_rec, state, factor, keep, prior):
    units = state.shape[2]
    old = state[d]
    low = old.astype(jnp.bfloat16)
    rec = plain_dot(low, w_rec[d])
    gi = gates[d, slot]
    reset = squash(gi[:, :units] + rec[:, :units])
    update = squash(gi[:, units : 2 * units] + rec[:, units : 2 * units])
    rec_n = rec[:, 2 * units :]
    cand = jnp.tanh(gi[:, 2 * units :] + reset * rec_n)
    live = slot < count
    state[d] = jnp.where(live, (1.0 - update) * cand + update * old, old)
    by_cand = jnp.where(live, (1.0 - update) * (1.0 - cand * cand), 0.0)
    by_update = jnp.where(live, (old - cand) * update * (1.0 - update), 0.0)
    by_reset = by_cand * rec_n * reset * (1.0 - reset)
    prior[...] = low
    keep[...] = jnp.where(live, update, 1.0)
    for k, x in enumerate((by_reset, by_update, by_cand, reset)):
        factor[:, k * units : (k + 1) * units] = x.astype(factor.dtype)


def gru_forward_kernel(group, ids_ref, tables, w_in, w_rec, vec, emb, f0, f1, z0, z1, h0, h1, gates, state):
    i = pl.program_id(0)
    nchar = pl.num_programs(0)

    @pl.when(i == 0)
    def _():
        own = pl.ds(pl.multiple_of(group[0] * SUBV, SUBV), SUBV)
        gru_embed(ids_ref, tables.at[own], w_in, emb, gates)
        state[...] = jnp.zeros_like(state)

    count = jnp.sum((ids_ref[...] > 0).astype(jnp.int32), axis=1, keepdims=True)
    gru_step(0, i, count, gates, w_rec, state, f0.at[0], z0.at[0], h0.at[0])
    gru_step(1, nchar - 1 - i, count, gates, w_rec, state, f1.at[0], z1.at[0], h1.at[0])

    @pl.when(i == nchar - 1)
    def _():
        units = state.shape[2]
        vec[:, :units] = state[0].astype(vec.dtype)
        vec[:, units:] = state[1].astype(vec.dtype)


def slot_specs(nchar, rows, cols, backward):
    up = pl.BlockSpec((1, rows, cols), lambda i: (i, 0, 0))
    down = pl.BlockSpec((1, rows, cols), lambda i: (nchar - 1 - i, 0, 0))
    return [down, up] if backward else [up, down]


def gru_cost(nchar, rows, width, units, products):
    steps = 2 * nchar * rows
    return pl.CostEstimate(
        flops=12 * products * steps * (width + units) * units,
        bytes_accessed=16 * steps * units,
        transcendentals=3 * steps * units,
    )


def gru_forward(group, ids, table, w_in, w_rec):
    rows, nchar = ids.shape
    width, units = table.shape[1], w_rec.shape[1]
    whole = lambda shape: pl.BlockSpec(shape, lambda i: (0,) * len(shape))
    slots = functools.partial(slot_specs, nchar, rows, backward=False)
    shape = jax.ShapeDtypeStruct
    factor = shape((nchar, rows, 4 * units), jnp.bfloat16)
    keep = shape((nchar, rows, units), jnp.float32)
    prior = shape((nchar, rows, units), jnp.bfloat16)
    return pl.pallas_call(
        gru_forward_kernel,
        grid=(nchar,),
        out_shape=[
            shape((rows, 2 * units), jnp.bfloat16),
            shape((nchar, rows, width), jnp.bfloat16),
            factor, factor, keep, keep, prior, prior,
        ],
        in_specs=[pl.BlockSpec(memory_space=pltpu.SMEM)] + [whole(x.shape) for x in (ids, table, w_in, w_rec)],
        out_specs=[whole((rows, 2 * units)), whole((nchar, rows, width))]
        + slots(4 * units) + slots(units) + slots(units),
        scratch_shapes=[
            pltpu.VMEM((2, nchar, rows, 3 * units), jnp.float32),
            pltpu.VMEM((2, rows, units), jnp.float32),
        ],
        compiler_params=pltpu.CompilerParams(vmem_limit_bytes=60000000),
        cost_estimate=gru_cost(nchar, rows, width, units, 1),
    )(group, ids, table, w_in, w_rec)


def gru_back_step(d, slot, factor, keep, flipped, grad, seeds):
    units = grad.shape[2]
    g = grad[d]
    part = lambda k: factor[:, k * units : (k + 1) * units].astype(jnp.float32)
    by_cand = g * part(2)
    seeds[d, slot, :, :units] = (g * part(0)).astype(seeds.dtype)
    seeds[d, slot, :, units : 2 * units] = (g * part(1)).astype(seeds.dtype)
    seeds[d, slot, :, 2 * units : 3 * units] = (by_cand * part(3)).astype(seeds.dtype)
    seeds[d, slot, :, 3 * units :] = by_cand.astype(seeds.dtype)
    grad[d] = g * keep[...] + plain_dot(seeds[d, slot, :, : 3 * units], flipped[d])


def gru_weight_grads(d, seeds, emb, prior, d_in, d_rec):
    _, nchar, rows, wide = seeds.shape
    units = wide // 4
    states = prior[...].reshape(nchar * rows, units)
    chars = emb[...].reshape(nchar * rows, -1)
    col = lambda k, n: seeds[d, :, :, k * units : (k + n) * units].reshape(nchar * rows, n * units)
    d_rec[d] = grad_dot(states, col(0, 3)).astype(d_rec.dtype)
    d_in[d, :, : 2 * units] = grad_dot(chars, col(0, 2)).astype(d_in.dtype)
    d_in[d, :, 2 * units :] = grad_dot(chars, col(3, 1)).astype(d_in.dtype)


def gru_char_grads(ids_ref, seeds, w_in, d_table, chunk=4):
    _, nchar, rows, wide = seeds.shape
    units = wide // 4
    ids = ids_ref[...]
    total = jnp.zeros(d_table.shape, jnp.float32)
    for k in range(0, nchar, chunk):
        grad = None
        for d in range(2):
            both = seeds[d, k : k + chunk].reshape(chunk * rows, wide)
            part = back_dot(both[:, : 2 * units], w_in[d][:, : 2 * units])
            part = part + back_dot(both[:, 3 * units :], w_in[d][:, 2 * units :])
            grad = part if grad is None else grad + part
        hot = slot_onehot(ids, range(k, k + chunk), d_table.shape[0])
        total = total + grad_dot(hot, grad.astype(jnp.bfloat16))
    d_table[...] = total


def gru_backward_kernel(ids_ref, seed, w_in, w_rec, emb, h0, h1, f0, f1, z0, z1, d_in, d_rec, d_table, grad, seeds, flipped):
    i = pl.program_id(0)
    nchar = pl.num_programs(0)

    @pl.when(i == 0)
    def _():
        units = grad.shape[2]
        grad[0] = seed[:, :units]
        grad[1] = seed[:, units:]
        for d in range(2):
            flipped[d] = w_rec[d].T

    gru_back_step(0, nchar - 1 - i, f0.at[0], z0.at[0], flipped, grad, seeds)
    gru_back_step(1, i, f1.at[0], z1.at[0], flipped, grad, seeds)

    @pl.when(i == nchar - 1)
    def _():
        gru_weight_grads(0, seeds, emb, h0, d_in, d_rec)
        gru_weight_grads(1, seeds, emb, h1, d_in, d_rec)
        gru_char_grads(ids_ref, seeds, w_in, d_table)


def gru_backward(ids, seed, w_in, w_rec, emb, h0, h1, f0, f1, z0, z1, subset):
    nchar, rows, width = emb.shape
    units = w_rec.shape[1]
    whole = lambda shape: pl.BlockSpec(shape, lambda i: (0,) * len(shape))
    slots = functools.partial(slot_specs, nchar, rows, backward=True)
    shape = jax.ShapeDtypeStruct
    return pl.pallas_call(
        gru_backward_kernel,
        grid=(nchar,),
        out_shape=[
            shape(w_in.shape, jnp.bfloat16),
            shape(w_rec.shape, jnp.bfloat16),
            shape((subset, width), jnp.float32),
        ],
        in_specs=[whole(x.shape) for x in (ids, seed, w_in, w_rec, emb, h0, h1)] + slots(4 * units) + slots(units),
        out_specs=[whole(w_in.shape), whole(w_rec.shape), whole((subset, width))],
        scratch_shapes=[
            pltpu.VMEM((2, rows, units), jnp.float32),
            pltpu.VMEM((2, nchar, rows, 4 * units), jnp.bfloat16),
            pltpu.VMEM((2, 3 * units, units), jnp.bfloat16),
        ],
        compiler_params=pltpu.CompilerParams(vmem_limit_bytes=60000000),
        cost_estimate=gru_cost(nchar, rows, width, units, 2),
    )(ids, seed, w_in, w_rec, emb, h0, h1, f0, f1, z0, z1)


def head_pair(q_ref, blocks, valid, pair, half):
    features = q_ref.shape[1]
    cols = pl.ds(pair * 2 * HD, 2 * HD)
    queries = q_ref[:, cols]
    keys = jnp.concatenate([b[:, cols] for b in blocks], 0)
    values = jnp.concatenate([b[:, pl.ds(features + pair * 2 * HD, 2 * HD)] for b in blocks], 0)
    scores = back_dot(one_head(queries, half), keys) * (1.0 / math.sqrt(HD))
    scores = jnp.where(valid, scores, -1000000000.0)
    weight = jnp.exp(scores - jnp.max(scores, axis=-1, keepdims=True))
    return weight / jnp.sum(weight, axis=-1, keepdims=True), queries, keys, values


def first_lanes(shape):
    return lax.broadcasted_iota(jnp.int32, shape, 1) < HD


def one_head(x, half):
    keep = first_lanes(x.shape) if half == 0 else jnp.logical_not(first_lanes(x.shape))
    return jnp.where(keep, x, jnp.zeros_like(x))


def side_by_side(left, right):
    return jnp.where(first_lanes(left.shape), left, right)


def attention_kernel(count, q_ref, valid_ref, *refs):
    blocks, out = refs[:count], refs[count]
    valid = jnp.broadcast_to(valid_ref[...] > 0, (q_ref.shape[0], valid_ref.shape[1]))
    for pair in range(q_ref.shape[1] // (2 * HD)):
        both = []
        for half in range(2):
            probs, _, _, values = head_pair(q_ref, blocks, valid, pair, half)
            both.append(plain_dot(probs.astype(jnp.bfloat16), values))
        out[:, pl.ds(pair * 2 * HD, 2 * HD)] = side_by_side(*both).astype(out.dtype)


def attention_back_kernel(count, q_ref, valid_ref, seed_ref, *refs):
    blocks, q_out, outs = refs[:count], refs[count], refs[count + 1 :]
    rows, features = q_ref.shape
    scale = 1.0 / math.sqrt(HD)
    valid = jnp.broadcast_to(valid_ref[...] > 0, (rows, valid_ref.shape[1]))
    for pair in range(features // (2 * HD)):
        cols = pl.ds(pair * 2 * HD, 2 * HD)
        seed = seed_ref[:, cols]
        q_both, k_both, v_both = [], [], []
        for half in range(2):
            probs, queries, keys, values = head_pair(q_ref, blocks, valid, pair, half)
            probs_grad = back_dot(one_head(seed, half), values)
            inner = jnp.sum(probs * probs_grad, axis=-1, keepdims=True)
            score_grad = (probs * (probs_grad - inner)).astype(jnp.bfloat16)
            q_both.append(plain_dot(score_grad, keys))
            k_both.append(grad_dot(score_grad, queries))
            v_both.append(grad_dot(probs.astype(jnp.bfloat16), seed))
        q_out[:, cols] = (side_by_side(*q_both) * scale).astype(q_out.dtype)
        k_grad = (side_by_side(*k_both) * scale).astype(jnp.bfloat16)
        v_grad = side_by_side(*v_both).astype(jnp.bfloat16)
        for j, out in enumerate(outs):
            out[:, cols] = k_grad[j * rows : (j + 1) * rows]
            out[:, pl.ds(features + pair * 2 * HD, 2 * HD)] = v_grad[j * rows : (j + 1) * rows]


def attention_cost(rows, blocks, features, products):
    span = rows * len(blocks)
    return pl.CostEstimate(
        flops=2 * products * rows * span * features,
        bytes_accessed=8 * span * features,
        transcendentals=rows * span * (features // HD),
    )


def attention(queries, valid, blocks):
    rows, features = queries.shape
    vmem = pl.BlockSpec(memory_space=pltpu.VMEM)
    return pl.pallas_call(
        functools.partial(attention_kernel, len(blocks)),
        out_shape=jax.ShapeDtypeStruct((rows, features), jnp.bfloat16),
        in_specs=[vmem] * (2 + len(blocks)),
        out_specs=vmem,
        cost_estimate=attention_cost(rows, blocks, features, 2),
    )(queries, valid, *blocks)


def attention_back(queries, valid, seed, blocks):
    rows, features = queries.shape
    vmem = pl.BlockSpec(memory_space=pltpu.VMEM)
    return pl.pallas_call(
        functools.partial(attention_back_kernel, len(blocks)),
        out_shape=[jax.ShapeDtypeStruct((rows, features), jnp.bfloat16)]
        + [jax.ShapeDtypeStruct((rows, 2 * features), jnp.bfloat16)] * len(blocks),
        in_specs=[vmem] * (3 + len(blocks)),
        out_specs=[vmem] * (1 + len(blocks)),
        cost_estimate=attention_cost(rows, blocks, features, 5),
    )(queries, valid, seed, *blocks)


def from_next(x, axis, step):
    size = lax.axis_size(axis)
    return lax.ppermute(x, axis, [((i + step) % size, i) for i in range(size)])


def to_next(x, axis, step):
    size = lax.axis_size(axis)
    return lax.ppermute(x, axis, [(i, (i + step) % size) for i in range(size)])


def norm_back(residual, row_gain, seed):
    centered = residual - jnp.mean(residual, axis=-1, keepdims=True)
    spread = jnp.mean(centered * centered, axis=-1, keepdims=True)
    scale = lax.rsqrt(spread + eps)
    unit = centered * scale
    inner = seed * row_gain
    drop = jnp.mean(inner, axis=-1, keepdims=True) + unit * jnp.mean(inner * unit, axis=-1, keepdims=True)
    gain_grad = jnp.sum(seed * unit, axis=0, keepdims=True)
    return scale * (inner - drop), gain_grad, jnp.sum(seed, axis=0, keepdims=True)


def place_norms(gain, bias, index, devices):
    both = jnp.concatenate([gain, bias], 0)
    width = both.shape[1]
    shape = (width, devices * width)
    spot = lax.broadcasted_iota(jnp.int32, shape, 0) + index * width == lax.broadcasted_iota(jnp.int32, shape, 1)
    placed = plain_dot(both, spot.astype(both.dtype)).astype(both.dtype)
    return jnp.pad(placed, ((0, 8 - both.shape[0]), (0, 0)))


def local(
    hidden,
    char_ids,
    groups,
    lengths,
    cotangent,
    qkv_weight,
    out_weight,
    up_weight,
    down_weight,
    norm_gain,
    norm_bias,
    char_table,
    gru_input,
    gru_recur,
    merge_weight,
    conv_weight,
):
    dp_size, devices = lax.axis_size("dp"), lax.axis_size("dp") * lax.axis_size("seq")
    me = lax.axis_index("dp") * lax.axis_size("seq") + lax.axis_index("seq")
    norms = place_norms(norm_gain, norm_bias, me, devices)
    order = (char_table, gru_input, gru_recur, norms, qkv_weight, out_weight, up_weight, down_weight, merge_weight, conv_weight)
    gathered = gather_all(dp_size, devices, order, (6, 9))
    all_norms = jnp.sum(gathered[3].astype(jnp.float32), axis=0)
    (full_table, full_input, full_recur, _, full_qkv, full_out, full_up, full_down, full_merge, full_conv) = [
        x.reshape(-1, x.shape[2]) for x in gathered
    ]
    seq_count, local_len, features = hidden.shape
    nchar = char_ids.shape[2]
    tokens = seq_count * local_len
    key_span = local_len * lax.axis_size("seq")
    gains = [all_norms[k : k + 1] for k in range(3)]
    biases = [all_norms[k : k + 1] for k in range(3, 6)]
    flat_in = hidden.reshape(tokens, features)
    qkv = plain_dot(flat_in, full_qkv).astype(jnp.bfloat16)
    queries, own_kv = qkv[:, :features], qkv[:, features:]
    peers = lax.axis_size("seq")
    kv_blocks = [own_kv] + [from_next(own_kv, "seq", j) for j in range(1, peers)]
    place = lax.rem(lax.axis_index("seq") + jnp.arange(peers), peers) * local_len
    positions = place[:, None] + jnp.arange(local_len)[None, :]
    key_valid = (positions < lengths[0]).astype(jnp.int32).reshape(1, key_span)
    assert seq_count == 1
    flat_ids = char_ids.reshape(tokens, nchar)
    table_start = groups[0] * SUBV
    inward = full_input.reshape(2, -1, full_input.shape[1])
    recurrent = full_recur.reshape(2, -1, full_recur.shape[1])
    char_vec, char_emb, *kept = gru_forward(groups, flat_ids, full_table, inward, recurrent)
    factors, keeps, priors = kept[:2], kept[2:4], kept[4:]
    attended = attention(queries, key_valid, kv_blocks)
    resid_one = flat_in.astype(jnp.float32) + plain_dot(attended, full_out)
    norm_one = norm_rows(resid_one, gains[0], biases[0]).astype(jnp.bfloat16)
    up_proj = plain_dot(norm_one, full_up)
    active = gelu_exact(up_proj).astype(jnp.bfloat16)
    resid_two = norm_one.astype(jnp.float32) + plain_dot(active, full_down)
    norm_two = norm_rows(resid_two, gains[1], biases[1]).astype(jnp.bfloat16)
    merge_mats = full_merge.reshape(2, features, features)
    streams = jnp.stack([norm_two, char_vec], 0)
    merged_pair = jnp.einsum("btd,bdf->btf", streams, merge_mats, preferred_element_type=jnp.float32)
    merged_rows = jnp.concatenate([merged_pair[0], merged_pair[1]], -1).astype(jnp.bfloat16)
    padded = with_halo(merged_rows.reshape(seq_count, local_len, 2 * features), (("seq", 1),), 1)
    kernel = full_conv.reshape(3, 2 * features, features)
    windows = [
        padded[:, offset : offset + local_len].reshape(tokens, 2 * features) for offset in range(3)
    ]
    conv_out = (
        plain_dot(windows[0], kernel[0])
        + plain_dot(windows[1], kernel[1])
        + plain_dot(windows[2], kernel[2])
    )
    resid_three = norm_two.astype(jnp.float32) + conv_out
    result = norm_rows(resid_three, gains[2], biases[2]).astype(jnp.bfloat16).reshape(seq_count, local_len, features)
    back_qkv, back_out, back_up, back_down = full_qkv, full_out, full_up, full_down
    back_merge, back_conv = full_merge, full_conv
    merge_back = back_merge.reshape(2, features, features)
    kernel_back = back_conv.reshape(3, 2 * features, features)
    seed_rows = cotangent.reshape(tokens, features).astype(jnp.float32)
    grad_three, gain_three, bias_three = norm_back(resid_three, gains[2], seed_rows)
    conv_seed = grad_three.astype(jnp.bfloat16)
    conv_grad = grad_dot(jnp.concatenate(windows, 1), conv_seed)
    seed_padded = with_halo(conv_seed.reshape(seq_count, local_len, features), (("seq", 1),), 1)
    merged_grad = back_dot(
        seed_padded[:, 2 : 2 + local_len].reshape(tokens, features), kernel_back[0]
    )
    merged_grad = merged_grad + back_dot(
        seed_padded[:, 1 : 1 + local_len].reshape(tokens, features), kernel_back[1]
    )
    merged_grad = merged_grad + back_dot(
        seed_padded[:, 0:local_len].reshape(tokens, features), kernel_back[2]
    )
    merged_grad = merged_grad.astype(jnp.bfloat16)
    pair_grad = jnp.stack([merged_grad[:, :features], merged_grad[:, features:]], 0)
    merge_grad = jnp.einsum("btd,btf->bdf", streams, pair_grad, preferred_element_type=jnp.float32)
    stream_grad = jnp.einsum("btf,bdf->btd", pair_grad, merge_back, preferred_element_type=jnp.float32)
    two_grad = grad_three + stream_grad[0]
    charvec_grad = stream_grad[1]
    grad_two, gain_two, bias_two = norm_back(resid_two, gains[1], two_grad)
    down_seed = grad_two.astype(jnp.bfloat16)
    down_grad = grad_dot(active, down_seed)
    active_grad = back_dot(down_seed, back_down)
    _, pull_gelu = jax.vjp(gelu_exact, up_proj)
    up_seed = pull_gelu(active_grad)[0].astype(jnp.bfloat16)
    up_grad = grad_dot(norm_one, up_seed)
    one_grad = grad_two + back_dot(up_seed, back_up)
    grad_one, gain_one, bias_one = norm_back(resid_one, gains[0], one_grad)
    out_seed = grad_one.astype(jnp.bfloat16)
    out_grad = grad_dot(attended, out_seed)
    attn_seed = back_dot(out_seed, back_out).astype(jnp.bfloat16)
    query_grad, *kv_grads = attention_back(queries, key_valid, attn_seed, kv_blocks)
    kv_own = kv_grads[0].astype(jnp.float32)
    for j in range(1, peers):
        kv_own = kv_own + to_next(kv_grads[j], "seq", j).astype(jnp.float32)
    qkv_seed = jnp.concatenate([query_grad, kv_own.astype(jnp.bfloat16)], -1)
    qkv_grad = grad_dot(flat_in, qkv_seed)
    hidden_grad = (
        (grad_one + back_dot(qkv_seed, back_qkv))
        .astype(jnp.bfloat16)
        .reshape(seq_count, local_len, features)
    )
    input_mats, recur_sum, own_grad = gru_backward(
        flat_ids, charvec_grad, inward, recurrent, char_emb, *priors, *factors, *keeps, SUBV
    )
    table_grad = jnp.zeros(full_table.shape, jnp.bfloat16)
    table_grad = lax.dynamic_update_slice_in_dim(table_grad, own_grad.astype(jnp.bfloat16), table_start, 0)
    norm_grads = jnp.concatenate(
        [gain_one, gain_two, gain_three, bias_one, bias_two, bias_three, jnp.zeros((2, features), jnp.float32)], 0
    )
    terms = [input_mats, recur_sum, merge_grad, conv_grad, down_grad, up_grad, qkv_grad, out_grad, table_grad]
    parts = [x.astype(jnp.bfloat16).reshape(devices, -1, x.shape[-1]) for x in terms]
    width = norm_gain.shape[1]
    *sums, norm_sum = scatter_all(dp_size, parts, norm_grads, width, (3, 6))
    input_total, recur_total, merge_sum, conv_sum, down_sum, up_sum, qkv_sum, out_sum, table_sum = settle(sums)
    skip = me * width - window_start(me, width, features)
    gain_sum = lax.dynamic_slice(norm_sum, (0, skip), (3, width))
    bias_sum = lax.dynamic_slice(norm_sum, (3, skip), (3, width))
    return (result, hidden_grad, qkv_sum, out_sum, up_sum, down_sum, gain_sum, bias_sum, table_sum, input_total, recur_total, merge_sum, conv_sum)


def solution(mesh):
    placed = (
        P("dp", "seq", None),
        P("dp", "seq", None),
        P("dp"),
        P("dp"),
        P("dp", "seq", None),
        P(("dp", "seq"), None),
        P(("dp", "seq"), None),
        P(("dp", "seq"), None),
        P(("dp", "seq"), None),
        P(None, ("dp", "seq")),
        P(None, ("dp", "seq")),
        P(("dp", "seq"), None),
        P(("dp", "seq"), None),
        P(("dp", "seq"), None),
        P(("dp", "seq"), None),
        P(("dp", "seq"), None),
    )
    return jax.shard_map(
        local,
        mesh=mesh,
        in_specs=placed,
        out_specs=(
            P("dp", "seq", None),
            P("dp", "seq", None),
            P(("dp", "seq"), None),
            P(("dp", "seq"), None),
            P(("dp", "seq"), None),
            P(("dp", "seq"), None),
            P(None, ("dp", "seq")),
            P(None, ("dp", "seq")),
            P(("dp", "seq"), None),
            P(("dp", "seq"), None),
            P(("dp", "seq"), None),
            P(("dp", "seq"), None),
            P(("dp", "seq"), None),
        ),
        check_vma=False,
    )
```
